32 devices in a mesh: gx: 8 (over z, y), gy: 4 (over x, core).
Axes of the slice: x: 2, y: 2, z: 4, core: 2. Of those that a mesh axis runs over, the one named last changes fastest.
Arguments:
- mass_per_volume: float32 [16, 256, 512], P(None, 'gx', 'gy'), may hold values from 0.5 to 2
- momentum: float32 [3, 16, 256, 512], P(None, None, 'gx', 'gy'), may hold values from -1 to 1
- energy: float32 [16, 256, 512], P(None, 'gx', 'gy'), may hold values from 4 to 6
Outputs:
- updated_state: float32 [5, 16, 256, 512], P(None, None, 'gx', 'gy')
The draws below stay inside these ranges and needn't reach their ends.
All inputs are finite; a program needn't handle non-finite values.
Results may differ from the reference program's by a relative error of at most 0.00012.
Values sent between devices are 32-bit elements; how exact they have to be, the bound alone decides.
A program may use at most 64 MiB of HBM per device.

```python
import math
import jax
import jax.numpy as jnp
from jax import lax

CX = 32
CY = 128
NZ = 16
NX = 256
NY = 512


def level_of(stream_key, shape, cuts, low, top_value):
    loudness = 1.0
    for dim, blocks in cuts:
        steps = jax.random.uniform(jax.random.fold_in(jax.random.fold_in(stream_key, 6), dim), (blocks,), jnp.float32, low / len(cuts), top_value / len(cuts))
        loudness = loudness * jnp.repeat(jnp.exp(steps), shape[dim] // blocks).reshape((-1,) + (1,) * (len(shape) - 1 - dim))
    return loudness


def gaussian(key, shape, scale, most, shards=(), kind=jnp.bfloat16):
    level = level_of(key, shape, shards, -0.22, 0.18) if shards else 1.0
    result = jax.random.normal(key, shape, jnp.float32) * scale * level
    return jnp.minimum(jnp.maximum(result, -most), most).astype(kind)


def setup_inputs(seed: int = 0) -> dict:
    arg_keys = jax.random.split(jax.random.key(seed), 4)
    mass_per_volume = jnp.clip(jnp.exp(math.log(2.0) - 1.3862944 * jax.random.uniform(arg_keys[0], (NZ, NX, NY), jnp.float32) ** level_of(arg_keys[0], (NZ, NX, NY), ((1, 8), (2, 4)), -0.2, 0.2)), 0.5, 2.0)
    momentum = gaussian(arg_keys[1], (3, NZ, NX, NY), 0.2, 1.0, ((2, 8), (3, 4)), jnp.float32)
    energy = jnp.clip(4.0 + 2.0 * jax.random.uniform(arg_keys[2], (NZ, NX, NY), jnp.float32) ** level_of(arg_keys[2], (NZ, NX, NY), ((1, 8), (2, 4)), -0.2, 0.2), 4.0, 6.0)
    return {"mass_per_volume": mass_per_volume, "momentum": momentum, "energy": energy}


gamma_ratio = 1.4
viscosity = 0.1
conductivity = 0.1 * 1.4 / (0.4 * 0.72)

def central(field, dimension):
    length = field.shape[dimension]
    widths = [(0, 0)] * field.ndim
    widths[dimension] = (3, 3)
    padded = jnp.pad(field, widths)

    def shifted_field(k):
        return lax.slice_in_dim(padded, 3 + k, 3 + k + length, axis=dimension)
    return 0.75 * (shifted_field(1) - shifted_field(-1)) - 0.15 * (shifted_field(2) - shifted_field(-2)) + 1.0 / 60.0 * (shifted_field(3) - shifted_field(-3))

def implicit_line(field, dimension, coefficient):
    extent = field.shape[dimension]
    position = jnp.arange(extent, dtype=jnp.int32)
    lower_band = jnp.where(position == 0, jnp.float32(0.0), jnp.float32(-coefficient))
    upper_band = jnp.where(position == extent - 1, jnp.float32(0.0), jnp.float32(coefficient))
    diagonal = jnp.ones((extent,), jnp.float32)
    results = []
    for member in range(field.shape[0]):
        moved = jnp.moveaxis(field[member], dimension - 1, 0)
        block_shape = moved.shape
        solved = lax.linalg.tridiagonal_solve(lower_band, diagonal, upper_band, moved.reshape(extent, -1))
        results.append(jnp.moveaxis(solved.reshape(block_shape), 0, dimension - 1))
    return jnp.stack(results, 0)

def derive_third(field):

    def rolled(k):
        return jnp.roll(field, -k, axis=1)
    return 0.75 * (rolled(1) - rolled(-1)) - 0.15 * (rolled(2) - rolled(-2)) + 1.0 / 60.0 * (rolled(3) - rolled(-3))

def flux_terms(mass_per_volume, momentum, energy, bulk_speed_vector, normal_thermodynamic_load, grads):
    dilation = grads[0][0] + grads[1][1] + grads[2][2]
    flux_vectors = []
    for j in range(3):
        entries = [momentum[j]]
        viscous_shear_power = jnp.zeros_like(mass_per_volume)
        for i in range(3):
            stress = viscosity * (grads[j][i] + grads[i][j])
            if i == j:
                stress = stress - 2.0 / 3.0 * viscosity * dilation
            momentum_flux = momentum[i] * bulk_speed_vector[j] - stress
            if i == j:
                momentum_flux = momentum_flux + normal_thermodynamic_load
            entries.append(momentum_flux)
            viscous_shear_power = viscous_shear_power + bulk_speed_vector[i] * stress
        entries.append((energy + normal_thermodynamic_load) * bulk_speed_vector[j] - viscous_shear_power - conductivity * grads[j][3])
        flux_vectors.append(jnp.stack(entries, 0))
    return flux_vectors

def reference(mass_per_volume, momentum, energy):
    coefficient = float(max(CX, CY))
    bulk_speed_vector = momentum / mass_per_volume[None]
    normal_thermodynamic_load = (gamma_ratio - 1.0) * (energy - 0.5 * jnp.sum(momentum * bulk_speed_vector, axis=0))
    thermal_level = normal_thermodynamic_load / mass_per_volume
    basic_physical_quantities = jnp.concatenate([bulk_speed_vector, thermal_level[None]], 0)
    grads = (central(basic_physical_quantities, 2), central(basic_physical_quantities, 3), derive_third(basic_physical_quantities))
    flux_vectors = flux_terms(mass_per_volume, momentum, energy, bulk_speed_vector, normal_thermodynamic_load, grads)
    divergence = central(flux_vectors[0], 2) + central(flux_vectors[1], 3) + derive_third(flux_vectors[2])
    source = -2.0 * coefficient * divergence
    partial_derivative_value = implicit_line(source, 2, coefficient)
    increment = implicit_line(partial_derivative_value, 3, coefficient)
    state = jnp.concatenate([mass_per_volume[None], momentum, energy[None]], 0)
    return state + increment
```

```python
import functools
import jax
import jax.numpy as jnp
import numpy as np
from jax import lax
from jax.experimental import pallas as pl
from jax.experimental.pallas import tpu as pltpu
from jax.sharding import PartitionSpec as P

viscosity = 0.1
conductivity = 0.1 * 1.4 / (0.4 * 0.72)
MESH = pl.DeviceIdType.MESH
WEIGHTS = {1: 0.75, -1: -0.75, 2: -0.15, -2: 0.15, 3: 1.0 / 60.0, -3: -1.0 / 60.0}
GROUPS = ((0, 2), (2, 5))


def local_inverse(length, coefficient):
    matrix = np.eye(length)
    matrix += coefficient * (np.eye(length, k=1) - np.eye(length, k=-1))
    return np.linalg.inv(matrix)


def reduced_tables(length, count, coefficient):
    inverse = local_inverse(length, coefficient)
    alpha, beta = coefficient * inverse[:, 0], -coefficient * inverse[:, -1]
    system = np.eye(2 * count)
    for b in range(count):
        for row, at in ((2 * b, 0), (2 * b + 1, length - 1)):
            if b > 0:
                system[row, 2 * b - 1] -= alpha[at]
            if b < count - 1:
                system[row, 2 * b + 2] -= beta[at]
    g = np.linalg.inv(system)
    up = [g[2 * b + 1, 2 * b : 2 * b + 2] for b in range(count)]
    down = [g[2 * b, 2 * b : 2 * b + 2] for b in range(count)]
    rows = []
    for b in range(count):
        prev = g[2 * b - 1] if b > 0 else np.zeros(2 * count)
        nxt = g[2 * b + 2] if b < count - 1 else np.zeros(2 * count)
        t = []
        for line in (prev, nxt):
            for d in range(1, count):
                other = (b - d) % count
                basis = up[other] if other < b else down[other]
                part = line[2 * other : 2 * other + 2]
                t.append(part @ basis / (basis @ basis))
        own = [*prev[2 * b : 2 * b + 2], *nxt[2 * b : 2 * b + 2]]
        rows.append([*up[b], *down[b], *own, *t])
    return np.asarray(rows).astype(np.float32), alpha, beta


def pivots(length, coefficient):
    inverse_pivot = np.ones(length)
    for i in range(1, length):
        inverse_pivot[i] = 1.0 / (1.0 + coefficient * coefficient * inverse_pivot[i - 1])
    return inverse_pivot


def lane_tables(ly, coefficient, alpha, beta):
    inverse = local_inverse(ly, coefficient)
    dy = np.zeros((ly, ly))
    for j in range(ly):
        for k, w in WEIGHTS.items():
            if 0 <= j + k < ly:
                dy[j + k, j] = w
    sel = np.zeros((5, 32, ly))
    ed = np.zeros((5, 32, ly))
    wy = np.zeros((5, 16, ly))
    ey = np.zeros((5, 16, ly))
    for f in range(5):
        for k in range(3):
            sel[f, 3 * f + k, k] = 1.0
            sel[f, 16 + 3 * f + k, ly - 3 + k] = 1.0
            for row, position in ((3 * f + k, k - 3), (16 + 3 * f + k, ly + k)):
                for step, w in WEIGHTS.items():
                    if 0 <= position - step < ly:
                        ed[f, row, position - step] = w
        wy[f, f], wy[f, 8 + f] = inverse[0], inverse[-1]
        ey[f, f], ey[f, 8 + f] = alpha, beta
    parts = [dy, inverse.T, sel.reshape(-1, ly), ed.reshape(-1, ly), wy.reshape(-1, ly), ey.reshape(-1, ly)]
    return np.concatenate(parts, 0).astype(np.float32)


def dot(a, b, dims):
    return lax.dot_general(
        a, b, (dims, ((), ())), precision=lax.Precision.HIGHEST, preferred_element_type=jnp.float32
    )


NN, NT, TN = ((1,), (0,)), ((1,), (1,)), ((0,), (0,))


def difference(at):
    return 0.75 * (at(1) - at(-1)) - 0.15 * (at(2) - at(-2)) + (1.0 / 60.0) * (at(3) - at(-3))


def around(v):
    n = v.shape[0]
    return difference(lambda k: pltpu.roll(v, (-k) % n, 0))


def kernel(
    nx, ny, lx, lz, ly, coefficient, ipiv, alpha, beta,
    mass_in, mom_in, energy_in, tab_in, xt_in, yt_in, out,
    mass, mom, energy, tab, xt, yt,
    xp, pt, ept, mt, gy, fxp, fy, dz, inc, ysend, yhalo, ysend2, yhalo2,
    xs, xr, ws, wr,
    hss, hrs, xss, xrs, wss, wrs, lsem,
):
    ix, iy = lax.axis_index("gx"), lax.axis_index("gy")
    rows = lx * lz

    barrier = pltpu.get_barrier_semaphore()
    for d in range(1, nx):
        pl.semaphore_signal(barrier, inc=1, device_id={"gx": lax.rem(ix + d, nx)}, device_id_type=MESH)
    for d in range(1, ny):
        pl.semaphore_signal(barrier, inc=1, device_id={"gy": lax.rem(iy + d, ny)}, device_id_type=MESH)

    loads = [
        pltpu.make_async_copy(a, b, lsem.at[k])
        for k, (a, b) in enumerate((
            (mass_in, mass), (mom_in, mom), (energy_in, energy), (tab_in, tab), (xt_in, xt), (yt_in, yt)))
    ]
    for load in loads:
        load.start()

    o = 2 * ly
    dy = tab.at[pl.ds(0, ly)]
    inverse = tab.at[pl.ds(ly, ly)]

    def sel(f):
        return tab[o + 32 * f : o + 32 * f + 32]

    def ed(f):
        return tab[o + 160 + 32 * f : o + 160 + 32 * f + 32]

    def wy(f):
        return tab[o + 320 + 16 * f : o + 320 + 16 * f + 16]

    def ey(f):
        return tab[o + 400 + 16 * f : o + 400 + 16 * f + 16]

    def flat(v):
        return v.reshape(rows, ly)

    def primitives(i, _=None):
        at = pl.ds(i, lz, stride=lx)
        rho, e = mass[at, :], energy[at, :]
        m = [mom[k, at, :] for k in range(3)]
        inv = 1.0 / rho
        u = [a * inv for a in m]
        p = 0.4 * (e - 0.5 * (m[0] * u[0] + m[1] * u[1] + m[2] * u[2]))
        for k in range(3):
            xp[k, i + 3] = u[k]
            mt[k, i] = m[k]
        xp[3, i + 3] = p * inv
        pt[i] = p
        ept[i] = e + p
        return 0

    for load in loads[:3]:
        load.wait()
    edges = sorted({*range(3), *range(lx - 3, lx)})
    for i in edges:
        primitives(i)

    zeros3 = jnp.zeros((3, lz, ly), jnp.float32)

    def x_halo(ref, fields, base):
        to_next = pltpu.make_async_remote_copy(
            ref.at[:, pl.ds(lx, 3)], ref.at[:, pl.ds(0, 3)], hss.at[base], hrs.at[base],
            device_id={"gx": ix + 1}, device_id_type=MESH)
        to_prev = pltpu.make_async_remote_copy(
            ref.at[:, pl.ds(3, 3)], ref.at[:, pl.ds(lx + 3, 3)], hss.at[base + 1], hrs.at[base + 1],
            device_id={"gx": ix - 1}, device_id_type=MESH)

        @pl.when(ix == 0)
        def _():
            for f in range(fields):
                ref[f, 0:3] = zeros3

        @pl.when(ix == nx - 1)
        def _():
            for f in range(fields):
                ref[f, lx + 3 : lx + 6] = zeros3

        return to_next, to_prev, ix, nx

    def y_halo(source, ref, base):
        to_next = pltpu.make_async_remote_copy(
            source.at[pl.ds(16, 16)], ref.at[pl.ds(0, 16)], hss.at[base], hrs.at[base],
            device_id={"gy": iy + 1}, device_id_type=MESH)
        to_prev = pltpu.make_async_remote_copy(
            source.at[pl.ds(0, 16)], ref.at[pl.ds(16, 16)], hss.at[base + 1], hrs.at[base + 1],
            device_id={"gy": iy - 1}, device_id_type=MESH)

        @pl.when(iy == 0)
        def _():
            ref[0:16] = jnp.zeros((16, rows), jnp.float32)

        @pl.when(iy == ny - 1)
        def _():
            ref[16:32] = jnp.zeros((16, rows), jnp.float32)

        return to_next, to_prev, iy, ny

    def start(halo):
        to_next, to_prev, here, count = halo
        pl.when(here < count - 1)(to_next.start)
        pl.when(here > 0)(to_prev.start)

    def arrive(halo):
        to_next, to_prev, here, count = halo
        pl.when(here > 0)(to_next.wait_recv)
        pl.when(here < count - 1)(to_prev.wait_recv)

    def sent(halo):
        to_next, to_prev, here, count = halo
        pl.when(here < count - 1)(to_next.wait_send)
        pl.when(here > 0)(to_prev.wait_send)

    h1x = x_halo(xp, 4, 0)
    lax.fori_loop(3, lx - 3, primitives, 0, unroll=2)
    for load in loads[3:]:
        load.wait()

    packed = dot(sel(0), flat(xp[0, 3 : lx + 3]), NT)
    for f in range(1, 4):
        packed += dot(sel(f), flat(xp[f, 3 : lx + 3]), NT)
    ysend[...] = packed
    h1y = y_halo(ysend, yhalo, 2)
    pl.semaphore_wait(barrier, nx + ny - 2)
    start(h1x)
    start(h1y)
    for f in range(4):
        gy[f] = dot(flat(xp[f, 3 : lx + 3]), dy[...], NN).reshape(lx, lz, ly)
    arrive(h1y)
    for f in range(4):
        gy[f] += dot(yhalo[...], ed(f), TN).reshape(lx, lz, ly)
    arrive(h1x)

    def fluxes(i, _=None):
        u = [xp[k, i + 3] for k in range(3)]
        m = [mt[k, i] for k in range(3)]
        p, ep = pt[i], ept[i]
        g = [
            [difference(lambda k: xp[f, i + 3 + k]) for f in range(4)],
            [gy[f, i] for f in range(4)],
            [around(xp[f, i + 3]) for f in range(4)],
        ]
        dilation = (2.0 / 3.0 * viscosity) * (g[0][0] + g[1][1] + g[2][2])
        stress = {}
        for a in range(3):
            for b in range(a, 3):
                s = viscosity * (g[a][b] + g[b][a])
                if a == b:
                    s = s - dilation
                stress[a, b] = stress[b, a] = s
        for j in range(3):
            entries = [m[j]]
            for k in range(3):
                e = m[k] * u[j] - stress[k, j]
                entries.append(e + p if k == j else e)
            power = u[0] * stress[0, j] + u[1] * stress[1, j] + u[2] * stress[2, j]
            entries.append(ep * u[j] - power - conductivity * g[j][3])
            for c in range(5):
                if j == 0:
                    fxp[c, i + 3] = entries[c]
                elif j == 1:
                    fy[c, i] = entries[c]
                else:
                    dz[c, i] = around(entries[c])
        return 0

    for i in edges:
        fluxes(i)
    h2x = x_halo(fxp, 5, 4)
    start(h2x)
    lax.fori_loop(3, lx - 3, fluxes, 0)

    packed = dot(sel(0), flat(fy[0]), NT)
    for f in range(1, 5):
        packed += dot(sel(f), flat(fy[f]), NT)
    ysend2[...] = packed
    h2y = y_halo(ysend2, yhalo2, 6)
    start(h2y)
    for c in range(5):
        dz[c] += dot(flat(fy[c]), dy[...], NN).reshape(lx, lz, ly)
    arrive(h2y)
    for c in range(5):
        dz[c] += dot(yhalo2[...], ed(c), TN).reshape(lx, lz, ly)
    arrive(h2x)

    width = 8 + 2 * (nx - 1)

    def xtab(k):
        return xt[ix * width + k]

    copies = []
    ends = {}
    for g, (f0, f1) in enumerate(GROUPS):
        v = [None] * 5
        for i in range(lx):
            for f in range(f0, f1):
                s = difference(lambda k: fxp[f, i + 3 + k]) + dz[f, i]
                s = s * (-2.0 * coefficient)
                v[f] = s if i == 0 else (s + coefficient * v[f]) * float(ipiv[i])
                inc[f, i] = v[f]
        last = list(v)
        for i in range(lx - 2, -1, -1):
            for f in range(f0, f1):
                v[f] = inc[f, i] - float(coefficient * ipiv[i]) * v[f]
                inc[f, i] = v[f]
        for f in range(f0, f1):
            ends[f] = (v[f], last[f])
            xs[0, f] = xtab(0) * v[f] + xtab(1) * last[f]
            xs[1, f] = xtab(2) * v[f] + xtab(3) * last[f]
        for d in range(1, nx):
            which = jnp.where(ix + d >= nx, 1, 0).astype(jnp.int32)
            copy = pltpu.make_async_remote_copy(
                xs.at[which, pl.ds(f0, f1 - f0)], xr.at[d - 1, pl.ds(f0, f1 - f0)],
                xss.at[g, d - 1], xrs.at[g, d - 1],
                device_id={"gx": lax.rem(ix + d, nx)}, device_id_type=MESH)
            copy.start()
            copies.append((g, d, copy))

    edges_y = None
    for g, (f0, f1) in enumerate(GROUPS):
        for group, d, copy in copies:
            if group == g:
                copy.wait_recv()
        for f in range(f0, f1):
            y0, yl = inc[f, 0], inc[f, lx - 1]
            before = xtab(4) * y0 + xtab(5) * yl
            after = xtab(6) * y0 + xtab(7) * yl
            for d in range(1, nx):
                r = xr[d - 1, f]
                before += xtab(7 + d) * r
                after += xtab(7 + nx - 1 + d) * r
            for i in range(lx):
                inc[f, i] += float(alpha[i]) * before + float(beta[i]) * after
            part = dot(wy(f), flat(inc[f]), NT)
            edges_y = part if edges_y is None else edges_y + part

    ywidth = 8 + 2 * (ny - 1)

    def ytab(k):
        return yt[iy * ywidth + k]

    y0, yl = edges_y[0:8], edges_y[8:16]
    ws[0] = ytab(0) * y0 + ytab(1) * yl
    ws[1] = ytab(2) * y0 + ytab(3) * yl
    ycopies = []
    for d in range(1, ny):
        which = jnp.where(iy + d >= ny, 1, 0).astype(jnp.int32)
        copy = pltpu.make_async_remote_copy(
            ws.at[which], wr.at[d - 1], wss.at[d - 1], wrs.at[d - 1],
            device_id={"gy": lax.rem(iy + d, ny)}, device_id_type=MESH)
        copy.start()
        ycopies.append(copy)
    for f in range(5):
        gy5 = dot(flat(inc[f]), inverse[...], NN)
        inc[f] = gy5.reshape(lx, lz, ly)
    before = ytab(4) * y0 + ytab(5) * yl
    after = ytab(6) * y0 + ytab(7) * yl
    for d in range(1, ny):
        ycopies[d - 1].wait_recv()
        r = wr[d - 1]
        before += ytab(7 + d) * r
        after += ytab(7 + ny - 1 + d) * r
    outside = jnp.concatenate([before, after], 0)
    for f in range(5):
        total = (flat(inc[f]) + dot(outside, ey(f), TN)).reshape(lx, lz, ly)
        for i in range(lx):
            at = pl.ds(i, lz, stride=lx)
            state = mass[at, :] if f == 0 else (energy[at, :] if f == 4 else mt[f - 1, i])
            out[f, at, :] = state + total[i]

    for halo in (h1x, h1y, h2x, h2y):
        sent(halo)
    for _, _, copy in copies:
        copy.wait_send()
    for copy in ycopies:
        copy.wait_send()


def body(nx, ny, mass, mom, energy):
    lz, lx, ly = mass.shape
    rows = lx * lz
    coefficient = float(max(lx, ly))
    xtab, xa, xb = reduced_tables(lx, nx, coefficient)
    ytab, ya, yb = reduced_tables(ly, ny, coefficient)
    tab = lane_tables(ly, coefficient, ya, yb)
    vm = pl.BlockSpec(memory_space=pltpu.VMEM)
    hbm = pl.BlockSpec(memory_space=pltpu.HBM)
    f32 = jnp.float32
    groups = len(GROUPS)
    block = (lx, lz, ly)
    dma = pltpu.SemaphoreType.DMA
    result = pl.pallas_call(
        functools.partial(kernel, nx, ny, lx, lz, ly, coefficient, pivots(lx, coefficient), xa, xb),
        out_shape=jax.ShapeDtypeStruct((5, rows, ly), f32),
        in_specs=[hbm] * 6,
        out_specs=vm,
        scratch_shapes=[
            pltpu.VMEM((rows, ly), f32),
            pltpu.VMEM((3, rows, ly), f32),
            pltpu.VMEM((rows, ly), f32),
            pltpu.VMEM(tab.shape, f32),
            pltpu.SMEM((xtab.size,), f32),
            pltpu.SMEM((ytab.size,), f32),
            pltpu.VMEM((4, lx + 6, lz, ly), f32),
            pltpu.VMEM(block, f32),
            pltpu.VMEM(block, f32),
            pltpu.VMEM((3, *block), f32),
            pltpu.VMEM((4, *block), f32),
            pltpu.VMEM((5, lx + 6, lz, ly), f32),
            pltpu.VMEM((5, *block), f32),
            pltpu.VMEM((5, *block), f32),
            pltpu.VMEM((5, *block), f32),
            pltpu.VMEM((32, rows), f32),
            pltpu.VMEM((32, rows), f32),
            pltpu.VMEM((32, rows), f32),
            pltpu.VMEM((32, rows), f32),
            pltpu.VMEM((2, 5, lz, ly), f32),
            pltpu.VMEM((nx - 1, 5, lz, ly), f32),
            pltpu.VMEM((2, 8, rows), f32),
            pltpu.VMEM((ny - 1, 8, rows), f32),
            dma((8,)),
            dma((8,)),
            dma((groups, nx - 1)),
            dma((groups, nx - 1)),
            dma((ny - 1,)),
            dma((ny - 1,)),
            dma((6,)),
        ],
        compiler_params=pltpu.CompilerParams(
            collective_id=0, has_side_effects=True, vmem_limit_bytes=40 * 2**20
        ),
    )(*[pltpu.with_memory_space_constraint(a, pltpu.HBM) for a in (
        mass.reshape(rows, ly), mom.reshape(3, rows, ly), energy.reshape(rows, ly),
        jnp.asarray(tab), jnp.asarray(xtab.reshape(-1)), jnp.asarray(ytab.reshape(-1)),
    )])
    return result.reshape(5, lz, lx, ly)


def solution(mesh):
    return jax.shard_map(
        functools.partial(body, mesh.shape["gx"], mesh.shape["gy"]),
        mesh=mesh,
        in_specs=(P(None, "gx", "gy"), P(None, None, "gx", "gy"), P(None, "gx", "gy")),
        out_specs=P(None, None, "gx", "gy"),
        check_vma=False,
    )
```

```python
import functools
import jax
import jax.numpy as jnp
import ml_dtypes
import numpy as np
from jax import lax
from jax.experimental import pallas as pl
from jax.experimental.pallas import tpu as pltpu
from jax.sharding import PartitionSpec as P

viscosity = 0.1
conductivity = 0.1 * 1.4 / (0.4 * 0.72)
MESH = pl.DeviceIdType.MESH
WEIGHTS = {1: 45.0, -1: -45.0, 2: -9.0, -2: 9.0, 3: 1.0, -3: -1.0}
STEP = 1.0 / 60.0


def local_inverse(length, coefficient):
    matrix = np.eye(length)
    matrix += coefficient * (np.eye(length, k=1) - np.eye(length, k=-1))
    return np.linalg.inv(matrix)


def reduced_system(length, count, coefficient):
    inverse = local_inverse(length, coefficient)
    alpha, beta = coefficient * inverse[:, 0], -coefficient * inverse[:, -1]
    system = np.eye(2 * count)
    for b in range(count):
        for row, at in ((2 * b, 0), (2 * b + 1, length - 1)):
            if b > 0:
                system[row, 2 * b - 1] -= alpha[at]
            if b < count - 1:
                system[row, 2 * b + 2] -= beta[at]
    g = np.linalg.inv(system)
    up = [g[2 * b + 1, 2 * b : 2 * b + 2] for b in range(count)]
    down = [g[2 * b, 2 * b : 2 * b + 2] for b in range(count)]
    return inverse, alpha, beta, g, up, down


def outside_lines(g, b, count):
    prev = g[2 * b - 1] if b > 0 else np.zeros(2 * count)
    nxt = g[2 * b + 2] if b < count - 1 else np.zeros(2 * count)
    return prev, nxt


def received(line, b, count, up, down):
    weights = []
    for d in range(1, count):
        other = (b - d) % count
        basis = up[other] if other < b else down[other]
        weights.append(line[2 * other : 2 * other + 2] @ basis / (basis @ basis))
    return weights


def reduced_tables(length, count, coefficient):
    inverse, alpha, beta, g, up, down = reduced_system(length, count, coefficient)
    rows = []
    for b in range(count):
        prev, nxt = outside_lines(g, b, count)
        own = [*prev[2 * b : 2 * b + 2], *nxt[2 * b : 2 * b + 2]]
        rows.append([*up[b], *down[b], *own, *received(prev, b, count, up, down), *received(nxt, b, count, up, down)])
    return np.asarray(rows).astype(np.float32), alpha, beta


def coupled_tables(length, count, coefficient, scale):
    inverse, alpha, beta, g, up, down = reduced_system(length, count, coefficient)
    ends = [0, length - 1]
    to_next, to_prev = [], []
    for m in range(3):
        n, p = np.zeros(2), np.zeros(2)
        for r in range(3 - m):
            n += scale * inverse[ends, r] * WEIGHTS[-(r + 1 + m)]
            p += scale * inverse[ends, length - 1 - r] * WEIGHTS[r + 1 + m]
        to_next.append(n)
        to_prev.append(p)
    rows = []
    for b in range(count):
        prev, nxt = outside_lines(g, b, count)

        def via(line, j, spread):
            if not 0 <= j < count:
                return [0.0] * 3
            return [line[2 * j : 2 * j + 2] @ s for s in spread]

        def ratio(line, j, basis):
            return line[2 * j : 2 * j + 2] @ basis[j] / (basis[j] @ basis[j])

        def sent(basis, t, line_at):
            if not 0 <= t < count:
                low, high = 0.0, 0.0
                ref = None
            else:
                ref = g[line_at(t)]
            out = []
            for j, spread in ((b - 1, to_prev), (b + 1, to_next)):
                if not 0 <= j < count:
                    out += [0.0] * 3
                    continue
                line = ref
                if line is None:
                    line = g[line_at(b + 1 if basis is up else b - 1)] if 0 <= (b + 1 if basis is up else b - 1) < count else None
                beyond = (j > b) if basis is up else (j < b)
                if line is None or (ref is None and beyond):
                    out += [0.0] * 3
                    continue
                scale_j = ratio(line, j, basis) / ratio(line, b, basis)
                out += [scale_j * (basis[j] @ s) for s in spread]
            return out

        u = sent(up, b + 2, lambda t: 2 * t - 1)
        d = sent(down, b - 2, lambda t: 2 * t + 2)
        own = []
        for line in (prev, nxt):
            own += [*line[2 * b : 2 * b + 2], *via(line, b - 1, to_prev), *via(line, b + 1, to_next)]
        rows.append([*up[b], *u, *down[b], *d, *own, *received(prev, b, count, up, down), *received(nxt, b, count, up, down)])
    return np.asarray(rows).astype(np.float32), inverse, alpha, beta


def pivots(length, coefficient):
    inverse_pivot = np.ones(length)
    for i in range(1, length):
        inverse_pivot[i] = 1.0 / (1.0 + coefficient * coefficient * inverse_pivot[i - 1])
    return inverse_pivot


def halves(matrix):
    high = matrix.astype(ml_dtypes.bfloat16)
    low = (matrix - high.astype(np.float64)).astype(ml_dtypes.bfloat16)
    return high.astype(np.float64), low.astype(np.float64)


def lane_tables(lx, lz, ly, coefficient, xa, xb, ya, yb):
    inverse = local_inverse(ly, coefficient)
    dy = np.zeros((ly, ly))
    for j in range(ly):
        for k, w in WEIGHTS.items():
            if 0 <= j + k < ly:
                dy[j + k, j] = w
    sel = np.zeros((5, 32, ly))
    ed = np.zeros((5, 32, ly))
    wy = np.zeros((5, 16, ly))
    ey = np.zeros((5, 16, ly))
    for f in range(5):
        for k in range(3):
            sel[f, 3 * f + k, k] = 1.0
            sel[f, 16 + 3 * f + k, ly - 3 + k] = 1.0
            for row, position in ((3 * f + k, k - 3), (16 + 3 * f + k, ly + k)):
                for step, w in WEIGHTS.items():
                    if 0 <= position - step < ly:
                        ed[f, row, position - step] = w
        wy[f, f], wy[f, 8 + f] = inverse[0], inverse[-1]
        ey[f, f], ey[f, 8 + f] = ya, yb
    spread = np.zeros((2, lz, lx, lz))
    for z in range(lz):
        spread[0, z, :, z], spread[1, z, :, z] = xa, xb
    spread = spread.reshape(2 * lz, lx * lz)
    parts = {"dy": np.concatenate([dy, dy])}
    high, low = halves(inverse.T)
    parts["inverse"] = np.concatenate([high, high, low])
    for f in range(5):
        parts["sel", f] = sel[f]
        parts["ed", f] = np.concatenate([ed[f], ed[f]])
        high, low = halves(wy[f])
        parts["wy", f] = np.concatenate([high, low])
        high, low = halves(ey[f])
        parts["ey", f] = np.concatenate([high, high, low])
    high, low = halves(spread)
    spread = np.concatenate([high, high, low])
    for c in range(lx * lz // ly):
        parts["spread", c] = spread[:, c * ly : c * ly + ly]
    places, at = {}, 0
    for name, part in parts.items():
        places[name] = (at, at + part.shape[0])
        at += part.shape[0]
    return np.concatenate(list(parts.values()), 0).astype(ml_dtypes.bfloat16), places


NN, NT, TN = ((1,), (0,)), ((1,), (1,)), ((0,), (0,))


def dot(a, b, dims):
    return lax.dot_general(a, b, (dims, ((), ())), preferred_element_type=jnp.float32)


def split(v):
    high = v.astype(jnp.bfloat16)
    low = (v - high.astype(jnp.float32)).astype(jnp.bfloat16)
    return high, low


def two(v, axis):
    return jnp.concatenate(split(v), axis)


def three(v, axis):
    high, low = split(v)
    return jnp.concatenate([high, low, high], axis)


def difference(at):
    total = None
    for k, w in ((1, 45.0), (2, -9.0), (3, 1.0)):
        a, b = at(k), at(-k)
        if a is None and b is None:
            continue
        pair = -b if a is None else (a if b is None else a - b)
        pair = pair if w == 1.0 else w * pair
        total = pair if total is None else total + pair
    return total


def around(v):
    n = v.shape[0]
    return difference(lambda k: pltpu.roll(v, (-k) % n, 0))


def kernel(
    nx, ny, lx, lz, ly, coefficient, ipiv, xinv, alpha, beta, places,
    mass_in, mom_in, energy_in, tab_in, xt_in, yt_in, out,
    mass, mom, energy, tab, xt, yt,
    xp, pt, ept, mt, gy, fxp, fy, dz, inc, ysend, yhalo, ysend2, yhalo2,
    xs, xr, ws, wr,
    hss, hrs, xss, xrs, wss, wrs, lsem,
):
    ix, iy = lax.axis_index("gx"), lax.axis_index("gy")
    rows = lx * lz
    scale = -2.0 * coefficient * STEP

    barrier = pltpu.get_barrier_semaphore()
    for d in range(1, nx):
        pl.semaphore_signal(barrier, inc=1, device_id={"gx": lax.rem(ix + d, nx)}, device_id_type=MESH)
    for d in range(1, ny):
        pl.semaphore_signal(barrier, inc=1, device_id={"gy": lax.rem(iy + d, ny)}, device_id_type=MESH)

    loads = [
        pltpu.make_async_copy(a, b, lsem.at[k])
        for k, (a, b) in enumerate((
            (mass_in, mass), (mom_in, mom), (energy_in, energy), (tab_in, tab), (xt_in, xt), (yt_in, yt)))
    ]
    for load in loads:
        load.start()

    def part(*name):
        low, high = places[name if len(name) > 1 else name[0]]
        return tab[low:high]

    def flat(v):
        return v.reshape(rows, ly)

    def block(v):
        return v.reshape(lx, lz, ly)

    def primitives(i, _=None):
        at = pl.ds(i, lz, stride=lx)
        rho, e = mass[at, :], energy[at, :]
        m = [mom[k, at, :] for k in range(3)]
        inv = 1.0 / rho
        u = [a * inv for a in m]
        p = 0.4 * (e - 0.5 * (m[0] * u[0] + m[1] * u[1] + m[2] * u[2]))
        for k in range(3):
            xp[k, i + 3] = u[k]
            mt[k, i] = m[k]
        xp[3, i + 3] = p * inv
        pt[i] = p
        ept[i] = e + p
        return 0

    for load in loads[:3]:
        load.wait()
    edges = sorted({*range(3), *range(lx - 3, lx)})
    for i in edges:
        primitives(i)

    zeros3 = jnp.zeros((3, lz, ly), jnp.float32)

    def x_halo(ref, fields, base):
        to_next = pltpu.make_async_remote_copy(
            ref.at[:, pl.ds(lx, 3)], ref.at[:, pl.ds(0, 3)], hss.at[base], hrs.at[base],
            device_id={"gx": ix + 1}, device_id_type=MESH)
        to_prev = pltpu.make_async_remote_copy(
            ref.at[:, pl.ds(3, 3)], ref.at[:, pl.ds(lx + 3, 3)], hss.at[base + 1], hrs.at[base + 1],
            device_id={"gx": ix - 1}, device_id_type=MESH)

        @pl.when(ix == 0)
        def _():
            for f in range(fields):
                ref[f, 0:3] = zeros3

        @pl.when(ix == nx - 1)
        def _():
            for f in range(fields):
                ref[f, lx + 3 : lx + 6] = zeros3

        return to_next, to_prev, ix, nx

    def y_halo(source, ref, base):
        to_next = pltpu.make_async_remote_copy(
            source.at[pl.ds(16, 16)], ref.at[pl.ds(0, 16)], hss.at[base], hrs.at[base],
            device_id={"gy": iy + 1}, device_id_type=MESH)
        to_prev = pltpu.make_async_remote_copy(
            source.at[pl.ds(0, 16)], ref.at[pl.ds(16, 16)], hss.at[base + 1], hrs.at[base + 1],
            device_id={"gy": iy - 1}, device_id_type=MESH)

        @pl.when(iy == 0)
        def _():
            ref[0:16] = jnp.zeros((16, rows), jnp.float32)

        @pl.when(iy == ny - 1)
        def _():
            ref[16:32] = jnp.zeros((16, rows), jnp.float32)

        return to_next, to_prev, iy, ny

    def start(halo):
        to_next, to_prev, here, count = halo
        pl.when(here < count - 1)(to_next.start)
        pl.when(here > 0)(to_prev.start)

    def arrive(halo):
        to_next, to_prev, here, count = halo
        pl.when(here > 0)(to_next.wait_recv)
        pl.when(here < count - 1)(to_prev.wait_recv)

    def sent(halo):
        to_next, to_prev, here, count = halo
        pl.when(here < count - 1)(to_next.wait_send)
        pl.when(here > 0)(to_prev.wait_send)

    def packed(field, fields):
        total = None
        for f in range(fields):
            s = part("sel", f)
            p = dot(jnp.concatenate([s, s], 1), two(flat(field(f)), 1), NT)
            total = p if total is None else total + p
        return total

    def pairs(count):
        return [tuple(range(f, min(f + 2, count))) for f in range(0, count, 2)]

    h1x = x_halo(xp, 4, 0)
    lax.fori_loop(3, lx - 3, primitives, 0, unroll=2)
    for load in loads[3:]:
        load.wait()
    ysend[...] = packed(lambda f: xp[f, 3 : lx + 3], 4)
    h1y = y_halo(ysend, yhalo, 2)
    pl.semaphore_wait(barrier, nx + ny - 2)
    start(h1x)
    start(h1y)
    for f in range(4):
        gy[f] = block(dot(two(flat(xp[f, 3 : lx + 3]), 1), part("dy"), NN))
    arrive(h1y)
    outer = two(yhalo[...], 0)
    for fs in pairs(4):
        near = dot(outer, jnp.concatenate([part("ed", f) for f in fs], 1), TN)
        for n, f in enumerate(fs):
            gy[f] += block(near[:, n * ly : n * ly + ly])

    def fluxes(i, _=None):
        u = [xp[k, i + 3] for k in range(3)]
        m = [mt[k, i] for k in range(3)]
        p, ep = pt[i], ept[i]
        g = [
            [difference(lambda k: xp[f, i + 3 + k]) for f in range(4)],
            [gy[f, i] for f in range(4)],
            [around(xp[f, i + 3]) for f in range(4)],
        ]
        dilation = (2.0 / 3.0 * viscosity * STEP) * (g[0][0] + g[1][1] + g[2][2])
        stress = {}
        for a in range(3):
            for b in range(a, 3):
                if a == b:
                    s = (2.0 * viscosity * STEP) * g[a][a] - dilation
                else:
                    s = (viscosity * STEP) * (g[a][b] + g[b][a])
                stress[a, b] = stress[b, a] = s
        for j in range(3):
            entries = [m[j]]
            for k in range(3):
                e = m[k] * u[j] - stress[k, j]
                entries.append(e + p if k == j else e)
            power = u[0] * stress[0, j] + u[1] * stress[1, j] + u[2] * stress[2, j]
            entries.append(ep * u[j] - power - (conductivity * STEP) * g[j][3])
            for c in range(5):
                if j == 0:
                    fxp[c, i + 3] = entries[c]
                elif j == 1:
                    fy[c, i] = entries[c]
                else:
                    dz[c, i] = around(entries[c])
        return 0

    lax.fori_loop(3, lx - 3, fluxes, 0)
    arrive(h1x)
    for i in edges:
        fluxes(i)
    h2x = x_halo(fxp, 5, 4)
    start(h2x)
    ysend2[...] = packed(lambda f: fy[f], 5)
    h2y = y_halo(ysend2, yhalo2, 6)
    start(h2y)

    for f in range(5):
        inner = block(dot(two(flat(fy[f]), 1), part("dy"), NN))
        for i in range(lx):
            s = difference(lambda k: fxp[f, i + 3 + k] if 0 <= i + k < lx else None)
            inc[f, i] = s + dz[f, i] + inner[i]

    width = 32 + 2 * (nx - 1)

    def xtab(k):
        return xt[ix * width + k]

    arrive(h2y)
    outer = two(yhalo2[...], 0)
    for fs in pairs(5):
        near = dot(outer, jnp.concatenate([part("ed", f) for f in fs], 1), TN)
        for n, f in enumerate(fs):
            add = block(near[:, n * ly : n * ly + ly])
            y0 = yl = None
            for i in range(lx):
                s = inc[f, i] + add[i]
                inc[f, i] = s
                a, b = float(scale * xinv[0, i]) * s, float(scale * xinv[-1, i]) * s
                y0, yl = (a, b) if i == 0 else (y0 + a, yl + b)
            first = [fxp[f, 3 + m] for m in range(3)]
            last = [fxp[f, lx + 2 - m] for m in range(3)]
            for w, base in ((0, 0), (1, 8)):
                near_side, far_side = (first, last) if w == 0 else (last, first)
                near_at, far_at = (2, 5) if w == 0 else (5, 2)
                total = xtab(base) * y0 + xtab(base + 1) * yl
                for m in range(3):
                    total += xtab(base + near_at + m) * near_side[m]
                xs[2 + w, f] = total
                for m in range(3):
                    total += xtab(base + far_at + m) * far_side[m]
                xs[w, f] = total
    copies = []
    for d in range(1, nx):
        above, below = (2 if d == 1 else 0), (3 if d == nx - 1 else 1)
        which = jnp.where(ix + d >= nx, below, above).astype(jnp.int32)
        copy = pltpu.make_async_remote_copy(
            xs.at[which], xr.at[d - 1], xss.at[d - 1], xrs.at[d - 1],
            device_id={"gx": lax.rem(ix + d, nx)}, device_id_type=MESH)
        copy.start()
        copies.append(copy)

    arrive(h2x)
    for fs in pairs(5):
        v = {}
        for i in range(lx):
            for f in fs:
                s = inc[f, i]
                if i < 3 or i >= lx - 3:
                    s = s + difference(lambda k: None if 0 <= i + k < lx else fxp[f, i + 3 + k])
                s = float(scale * ipiv[i]) * s
                v[f] = s if i == 0 else s + float(coefficient * ipiv[i]) * v[f]
                inc[f, i] = v[f]
        for i in range(lx - 2, -1, -1):
            for f in fs:
                v[f] = inc[f, i] - float(coefficient * ipiv[i]) * v[f]
                inc[f, i] = v[f]

    edges_y = None
    for f in range(5):
        data = three(flat(inc[f]), 1)
        w = part("wy", f)
        p = dot(jnp.concatenate([w[0:16], w[0:16], w[16:32]], 1), data, NT)
        edges_y = p if edges_y is None else edges_y + p
        fy[f] = block(dot(data, part("inverse"), NN))

    for copy in copies:
        copy.wait_recv()
    outside_x = []
    for f in range(5):
        y0, yl = inc[f, 0], inc[f, lx - 1]
        terms = [y0, yl] + [fxp[f, 3 + m] for m in range(3)] + [fxp[f, lx + 2 - m] for m in range(3)]
        sides = []
        for base in (16, 24):
            total = xtab(base) * terms[0]
            for k in range(1, 8):
                total += xtab(base + k) * terms[k]
            sides.append(total)
        for d in range(1, nx):
            r = xr[d - 1, f]
            sides[0] += xtab(31 + d) * r
            sides[1] += xtab(31 + nx - 1 + d) * r
        outside_x.append(jnp.concatenate(sides, 0))
    small = None
    for f in range(5):
        w = part("wy", f)
        p = dot(jnp.concatenate([w[0:16], w[0:16], w[16:32]], 1), three(outside_x[f], 1), NT)
        small = p if small is None else small + p
    spread = jnp.concatenate([part("spread", c) for c in range(rows // ly)], 1)
    edges_y += dot(three(small, 1), spread, NN)

    ywidth = 8 + 2 * (ny - 1)

    def ytab(k):
        return yt[iy * ywidth + k]

    y0, yl = edges_y[0:8], edges_y[8:16]
    ws[0] = ytab(0) * y0 + ytab(1) * yl
    ws[1] = ytab(2) * y0 + ytab(3) * yl
    ycopies = []
    for d in range(1, ny):
        which = jnp.where(iy + d >= ny, 1, 0).astype(jnp.int32)
        copy = pltpu.make_async_remote_copy(
            ws.at[which], wr.at[d - 1], wss.at[d - 1], wrs.at[d - 1],
            device_id={"gy": lax.rem(iy + d, ny)}, device_id_type=MESH)
        copy.start()
        ycopies.append(copy)
    solved = dot(three(jnp.concatenate(outside_x, 0), 1), part("inverse"), NN)
    for f in range(5):
        low, high = solved[2 * lz * f : 2 * lz * f + lz], solved[2 * lz * f + lz : 2 * lz * (f + 1)]
        for i in range(lx):
            at = pl.ds(i, lz, stride=lx)
            state = mass[at, :] if f == 0 else (energy[at, :] if f == 4 else mt[f - 1, i])
            inc[f, i] = state + fy[f, i] + float(alpha[i]) * low + float(beta[i]) * high
    before = ytab(4) * y0 + ytab(5) * yl
    after = ytab(6) * y0 + ytab(7) * yl
    for d in range(1, ny):
        ycopies[d - 1].wait_recv()
        r = wr[d - 1]
        before += ytab(7 + d) * r
        after += ytab(7 + ny - 1 + d) * r
    outside = three(jnp.concatenate([before, after], 0), 0)
    for fs in pairs(5):
        far = dot(outside, jnp.concatenate([part("ey", f) for f in fs], 1), TN)
        for n, f in enumerate(fs):
            total = block(far[:, n * ly : n * ly + ly])
            for i in range(lx):
                out[f, pl.ds(i, lz, stride=lx), :] = inc[f, i] + total[i]

    for halo in (h1x, h1y, h2x, h2y):
        sent(halo)
    for copy in copies + ycopies:
        copy.wait_send()


def body(nx, ny, mass, mom, energy):
    lz, lx, ly = mass.shape
    rows = lx * lz
    coefficient = float(max(lx, ly))
    xtab, xinv, xa, xb = coupled_tables(lx, nx, coefficient, -2.0 * coefficient * STEP)
    ytab, ya, yb = reduced_tables(ly, ny, coefficient)
    tab, places = lane_tables(lx, lz, ly, coefficient, xa, xb, ya, yb)
    vm = pl.BlockSpec(memory_space=pltpu.VMEM)
    hbm = pl.BlockSpec(memory_space=pltpu.HBM)
    f32 = jnp.float32
    block = (lx, lz, ly)
    dma = pltpu.SemaphoreType.DMA
    operands = (
        mass.reshape(rows, ly), mom.reshape(3, rows, ly), energy.reshape(rows, ly),
        jnp.asarray(tab), jnp.asarray(xtab.reshape(-1)), jnp.asarray(ytab.reshape(-1)),
    )
    result = pl.pallas_call(
        functools.partial(
            kernel, nx, ny, lx, lz, ly, coefficient, pivots(lx, coefficient), xinv, xa, xb, places),
        out_shape=jax.ShapeDtypeStruct((5, rows, ly), f32),
        in_specs=[hbm] * 6,
        out_specs=vm,
        scratch_shapes=[
            pltpu.VMEM((rows, ly), f32),
            pltpu.VMEM((3, rows, ly), f32),
            pltpu.VMEM((rows, ly), f32),
            pltpu.VMEM(tab.shape, jnp.bfloat16),
            pltpu.SMEM((xtab.size,), f32),
            pltpu.SMEM((ytab.size,), f32),
            pltpu.VMEM((4, lx + 6, lz, ly), f32),
            pltpu.VMEM(block, f32),
            pltpu.VMEM(block, f32),
            pltpu.VMEM((3, *block), f32),
            pltpu.VMEM((4, *block), f32),
            pltpu.VMEM((5, lx + 6, lz, ly), f32),
            pltpu.VMEM((5, *block), f32),
            pltpu.VMEM((5, *block), f32),
            pltpu.VMEM((5, *block), f32),
            pltpu.VMEM((32, rows), f32),
            pltpu.VMEM((32, rows), f32),
            pltpu.VMEM((32, rows), f32),
            pltpu.VMEM((32, rows), f32),
            pltpu.VMEM((4, 5, lz, ly), f32),
            pltpu.VMEM((nx - 1, 5, lz, ly), f32),
            pltpu.VMEM((2, 8, rows), f32),
            pltpu.VMEM((ny - 1, 8, rows), f32),
            dma((8,)),
            dma((8,)),
            dma((nx - 1,)),
            dma((nx - 1,)),
            dma((ny - 1,)),
            dma((ny - 1,)),
            dma((6,)),
        ],
        compiler_params=pltpu.CompilerParams(
            collective_id=0, has_side_effects=True, vmem_limit_bytes=40 * 2**20
        ),
    )(*[pltpu.with_memory_space_constraint(a, pltpu.HBM) for a in operands])
    return result.reshape(5, lz, lx, ly)


def solution(mesh):
    return jax.shard_map(
        functools.partial(body, mesh.shape["gx"], mesh.shape["gy"]),
        mesh=mesh,
        in_specs=(P(None, "gx", "gy"), P(None, None, "gx", "gy"), P(None, "gx", "gy")),
        out_specs=P(None, None, "gx", "gy"),
        check_vma=False,
    )
```

```python
import functools
import jax
import jax.numpy as jnp
import ml_dtypes
import numpy as np
from jax import lax
from jax.experimental import pallas as pl
from jax.experimental.pallas import tpu as pltpu
from jax.sharding import PartitionSpec as P

viscosity = 0.1
conductivity = 0.1 * 1.4 / (0.4 * 0.72)
MESH = pl.DeviceIdType.MESH
WEIGHTS = {1: 45.0, -1: -45.0, 2: -9.0, -2: 9.0, 3: 1.0, -3: -1.0}
STEP = 1.0 / 60.0


def local_inverse(length, coefficient):
    matrix = np.eye(length)
    matrix += coefficient * (np.eye(length, k=1) - np.eye(length, k=-1))
    return np.linalg.inv(matrix)


def reduced_system(length, count, coefficient):
    inverse = local_inverse(length, coefficient)
    alpha, beta = coefficient * inverse[:, 0], -coefficient * inverse[:, -1]
    system = np.eye(2 * count)
    for b in range(count):
        for row, at in ((2 * b, 0), (2 * b + 1, length - 1)):
            if b > 0:
                system[row, 2 * b - 1] -= alpha[at]
            if b < count - 1:
                system[row, 2 * b + 2] -= beta[at]
    g = np.linalg.inv(system)
    up = [g[2 * b + 1, 2 * b : 2 * b + 2] for b in range(count)]
    down = [g[2 * b, 2 * b : 2 * b + 2] for b in range(count)]
    return inverse, alpha, beta, g, up, down


def outside_lines(g, b, count):
    prev = g[2 * b - 1] if b > 0 else np.zeros(2 * count)
    nxt = g[2 * b + 2] if b < count - 1 else np.zeros(2 * count)
    return prev, nxt


def received(line, b, count, up, down):
    weights = []
    for d in range(1, count):
        other = (b - d) % count
        basis = up[other] if other < b else down[other]
        weights.append(line[2 * other : 2 * other + 2] @ basis / (basis @ basis))
    return weights


def reduced_tables(length, count, coefficient):
    inverse, alpha, beta, g, up, down = reduced_system(length, count, coefficient)
    rows = []
    for b in range(count):
        prev, nxt = outside_lines(g, b, count)
        own = [*prev[2 * b : 2 * b + 2], *nxt[2 * b : 2 * b + 2]]
        rows.append([*up[b], *down[b], *own, *received(prev, b, count, up, down), *received(nxt, b, count, up, down)])
    return np.asarray(rows).astype(np.float32), alpha, beta


def coupled_tables(length, count, coefficient, scale):
    inverse, alpha, beta, g, up, down = reduced_system(length, count, coefficient)
    ends = [0, length - 1]
    to_next, to_prev = [], []
    for m in range(3):
        n, p = np.zeros(2), np.zeros(2)
        for r in range(3 - m):
            n += scale * inverse[ends, r] * WEIGHTS[-(r + 1 + m)]
            p += scale * inverse[ends, length - 1 - r] * WEIGHTS[r + 1 + m]
        to_next.append(n)
        to_prev.append(p)
    rows = []
    for b in range(count):
        prev, nxt = outside_lines(g, b, count)

        def via(line, j, spread):
            if not 0 <= j < count:
                return [0.0] * 3
            return [line[2 * j : 2 * j + 2] @ s for s in spread]

        def ratio(line, j, basis):
            return line[2 * j : 2 * j + 2] @ basis[j] / (basis[j] @ basis[j])

        def sent(basis, t, line_at):
            if not 0 <= t < count:
                low, high = 0.0, 0.0
                ref = None
            else:
                ref = g[line_at(t)]
            out = []
            for j, spread in ((b - 1, to_prev), (b + 1, to_next)):
                if not 0 <= j < count:
                    out += [0.0] * 3
                    continue
                line = ref
                if line is None:
                    line = g[line_at(b + 1 if basis is up else b - 1)] if 0 <= (b + 1 if basis is up else b - 1) < count else None
                beyond = (j > b) if basis is up else (j < b)
                if line is None or (ref is None and beyond):
                    out += [0.0] * 3
                    continue
                scale_j = ratio(line, j, basis) / ratio(line, b, basis)
                out += [scale_j * (basis[j] @ s) for s in spread]
            return out

        u = sent(up, b + 2, lambda t: 2 * t - 1)
        d = sent(down, b - 2, lambda t: 2 * t + 2)
        own = []
        for line in (prev, nxt):
            own += [*line[2 * b : 2 * b + 2], *via(line, b - 1, to_prev), *via(line, b + 1, to_next)]
        rows.append([*up[b], *u, *down[b], *d, *own, *received(prev, b, count, up, down), *received(nxt, b, count, up, down)])
    return np.asarray(rows).astype(np.float32), inverse, alpha, beta


def pivots(length, coefficient):
    inverse_pivot = np.ones(length)
    for i in range(1, length):
        inverse_pivot[i] = 1.0 / (1.0 + coefficient * coefficient * inverse_pivot[i - 1])
    return inverse_pivot


def halves(matrix):
    high = matrix.astype(ml_dtypes.bfloat16)
    low = (matrix - high.astype(np.float64)).astype(ml_dtypes.bfloat16)
    return high.astype(np.float64), low.astype(np.float64)


def lane_tables(lx, lz, ly, coefficient, xa, xb, ya, yb):
    inverse = local_inverse(ly, coefficient)
    dy = np.zeros((ly, ly))
    for j in range(ly):
        for k, w in WEIGHTS.items():
            if 0 <= j + k < ly:
                dy[j + k, j] = w
    sel = np.zeros((5, 32, ly))
    ed = np.zeros((5, 32, ly))
    wy = np.zeros((5, 16, ly))
    ey = np.zeros((5, 16, ly))
    for f in range(5):
        for k in range(3):
            sel[f, 3 * f + k, k] = 1.0
            sel[f, 16 + 3 * f + k, ly - 3 + k] = 1.0
            for row, position in ((3 * f + k, k - 3), (16 + 3 * f + k, ly + k)):
                for step, w in WEIGHTS.items():
                    if 0 <= position - step < ly:
                        ed[f, row, position - step] = w
        wy[f, f], wy[f, 8 + f] = inverse[0], inverse[-1]
        ey[f, f], ey[f, 8 + f] = ya, yb
    spread = np.zeros((2, lz, lx, lz))
    for z in range(lz):
        spread[0, z, :, z], spread[1, z, :, z] = xa, xb
    spread = spread.reshape(2 * lz, lx * lz)
    parts = {"dy": np.concatenate([dy, dy])}
    high, low = halves(inverse.T)
    parts["inverse"] = np.concatenate([high, high, low])
    for f in range(5):
        parts["sel", f] = sel[f]
        parts["ed", f] = np.concatenate([ed[f], ed[f]])
        high, low = halves(wy[f])
        parts["wy", f] = np.concatenate([high, low])
        high, low = halves(ey[f])
        parts["ey", f] = np.concatenate([high, high, low])
    high, low = halves(spread)
    spread = np.concatenate([high, high, low])
    for c in range(lx * lz // ly):
        parts["spread", c] = spread[:, c * ly : c * ly + ly]
    places, at = {}, 0
    for name, part in parts.items():
        places[name] = (at, at + part.shape[0])
        at += part.shape[0]
    return np.concatenate(list(parts.values()), 0).astype(ml_dtypes.bfloat16), places


NN, NT, TN = ((1,), (0,)), ((1,), (1,)), ((0,), (0,))


def dot(a, b, dims):
    return lax.dot_general(a, b, (dims, ((), ())), preferred_element_type=jnp.float32)


def split(v):
    high = v.astype(jnp.bfloat16)
    low = (v - high.astype(jnp.float32)).astype(jnp.bfloat16)
    return high, low


def two(v, axis):
    return jnp.concatenate(split(v), axis)


def three(v, axis):
    high, low = split(v)
    return jnp.concatenate([high, low, high], axis)


def difference(at):
    total = None
    for k, w in ((1, 45.0), (2, -9.0), (3, 1.0)):
        a, b = at(k), at(-k)
        if a is None and b is None:
            continue
        pair = -b if a is None else (a if b is None else a - b)
        pair = pair if w == 1.0 else w * pair
        total = pair if total is None else total + pair
    return total


def around(v):
    n = v.shape[0]
    return difference(lambda k: pltpu.roll(v, (-k) % n, 0))


def kernel(
    nx, ny, lx, lz, ly, coefficient, ipiv, xinv, alpha, beta, places,
    mass_in, mom_in, energy_in, tab_in, xt_in, yt_in, out,
    mass, mom, energy, tab, xt, yt,
    xp, pt, ept, mt, gy, fxp, fy, dz, inc, ysend, yhalo, ysend2, yhalo2,
    xs, xl, xr, ws, wr, vs, vr, cs, cr,
    hss, hrs, xss, xrs, wss, wrs, vss, vrs, css, crs, lsem, near_sem,
):
    ix, iy = lax.axis_index("gx"), lax.axis_index("gy")
    rows = lx * lz
    scale = -2.0 * coefficient * STEP

    barrier = pltpu.get_barrier_semaphore()


    def both_sides(semaphore, distance):
        above, below = ix + distance < nx, ix - distance >= 0

        @pl.when(above)
        def _():
            pl.semaphore_signal(semaphore, inc=1, device_id={"gx": ix + distance}, device_id_type=MESH)

        @pl.when(below)
        def _():
            pl.semaphore_signal(semaphore, inc=1, device_id={"gx": ix - distance}, device_id_type=MESH)

        return above.astype(jnp.int32) + below.astype(jnp.int32)

    expected = both_sides(barrier, 1)
    stages = []

    def tell():
        distance = 1 << len(stages)
        if distance < nx - 1:
            stages.append(both_sides(near_sem.at[len(stages)], distance))

    def hear():
        if stages and stages[-1] is not None:
            pl.semaphore_wait(near_sem.at[len(stages) - 1], stages[-1])

    for d in range(1, ny):
        pl.semaphore_signal(barrier, inc=1, device_id={"gy": lax.rem(iy + d, ny)}, device_id_type=MESH)

    loads = [
        pltpu.make_async_copy(a, b, lsem.at[k])
        for k, (a, b) in enumerate((
            (mass_in, mass), (mom_in, mom), (energy_in, energy), (tab_in, tab), (xt_in, xt), (yt_in, yt)))
    ]
    for load in loads:
        load.start()

    def part(*name):
        low, high = places[name if len(name) > 1 else name[0]]
        return tab[low:high]

    def flat(v):
        return v.reshape(rows, ly)

    def block(v):
        return v.reshape(lx, lz, ly)

    def primitives(i, _=None):
        at = pl.ds(i, lz, stride=lx)
        rho, e = mass[at, :], energy[at, :]
        m = [mom[k, at, :] for k in range(3)]
        inv = 1.0 / rho
        u = [a * inv for a in m]
        p = 0.4 * (e - 0.5 * (m[0] * u[0] + m[1] * u[1] + m[2] * u[2]))
        for k in range(3):
            xp[k, i + 3] = u[k]
            mt[k, i] = m[k]
        xp[3, i + 3] = p * inv
        pt[i] = p
        ept[i] = e + p
        return 0

    for load in loads[:3]:
        load.wait()
    edges = sorted({*range(3), *range(lx - 3, lx)})
    for i in edges:
        primitives(i)

    zeros3 = jnp.zeros((3, lz, ly), jnp.float32)

    def x_halo(ref, fields, base):
        to_next = pltpu.make_async_remote_copy(
            ref.at[:, pl.ds(lx, 3)], ref.at[:, pl.ds(0, 3)], hss.at[base], hrs.at[base],
            device_id={"gx": ix + 1}, device_id_type=MESH)
        to_prev = pltpu.make_async_remote_copy(
            ref.at[:, pl.ds(3, 3)], ref.at[:, pl.ds(lx + 3, 3)], hss.at[base + 1], hrs.at[base + 1],
            device_id={"gx": ix - 1}, device_id_type=MESH)

        @pl.when(ix == 0)
        def _():
            for f in range(fields):
                ref[f, 0:3] = zeros3

        @pl.when(ix == nx - 1)
        def _():
            for f in range(fields):
                ref[f, lx + 3 : lx + 6] = zeros3

        return to_next, to_prev, ix, nx

    def y_halo(source, ref, base):
        to_next = pltpu.make_async_remote_copy(
            source.at[pl.ds(16, 16)], ref.at[pl.ds(0, 16)], hss.at[base], hrs.at[base],
            device_id={"gy": iy + 1}, device_id_type=MESH)
        to_prev = pltpu.make_async_remote_copy(
            source.at[pl.ds(0, 16)], ref.at[pl.ds(16, 16)], hss.at[base + 1], hrs.at[base + 1],
            device_id={"gy": iy - 1}, device_id_type=MESH)

        @pl.when(iy == 0)
        def _():
            ref[0:16] = jnp.zeros((16, rows), jnp.float32)

        @pl.when(iy == ny - 1)
        def _():
            ref[16:32] = jnp.zeros((16, rows), jnp.float32)

        return to_next, to_prev, iy, ny

    def start(halo):
        to_next, to_prev, here, count = halo
        pl.when(here < count - 1)(to_next.start)
        pl.when(here > 0)(to_prev.start)

    def arrive(halo):
        to_next, to_prev, here, count = halo
        pl.when(here > 0)(to_next.wait_recv)
        pl.when(here < count - 1)(to_prev.wait_recv)

    def sent(halo):
        to_next, to_prev, here, count = halo
        pl.when(here < count - 1)(to_next.wait_send)
        pl.when(here > 0)(to_prev.wait_send)

    def packed(field, fields):
        total = None
        for f in range(fields):
            s = part("sel", f)
            p = dot(jnp.concatenate([s, s], 1), two(flat(field(f)), 1), NT)
            total = p if total is None else total + p
        return total

    def pairs(count):
        return [tuple(range(f, min(f + 2, count))) for f in range(0, count, 2)]

    h1x = x_halo(xp, 4, 0)
    lax.fori_loop(3, lx - 3, primitives, 0, unroll=2)
    for load in loads[3:]:
        load.wait()
    ysend[...] = packed(lambda f: xp[f, 3 : lx + 3], 4)
    h1y = y_halo(ysend, yhalo, 2)
    pl.semaphore_wait(barrier, expected + (ny - 1))
    start(h1x)
    start(h1y)
    tell()
    for f in range(4):
        gy[f] = block(dot(two(flat(xp[f, 3 : lx + 3]), 1), part("dy"), NN))
    arrive(h1y)
    hear()
    tell()
    outer = two(yhalo[...], 0)
    for fs in pairs(4):
        near = dot(outer, jnp.concatenate([part("ed", f) for f in fs], 1), TN)
        for n, f in enumerate(fs):
            gy[f] += block(near[:, n * ly : n * ly + ly])

    def fluxes(i, _=None):
        u = [xp[k, i + 3] for k in range(3)]
        m = [mt[k, i] for k in range(3)]
        p, ep = pt[i], ept[i]
        g = [
            [difference(lambda k: xp[f, i + 3 + k]) for f in range(4)],
            [gy[f, i] for f in range(4)],
            [around(xp[f, i + 3]) for f in range(4)],
        ]
        dilation = (2.0 / 3.0 * viscosity * STEP) * (g[0][0] + g[1][1] + g[2][2])
        stress = {}
        for a in range(3):
            for b in range(a, 3):
                if a == b:
                    s = (2.0 * viscosity * STEP) * g[a][a] - dilation
                else:
                    s = (viscosity * STEP) * (g[a][b] + g[b][a])
                stress[a, b] = stress[b, a] = s
        for j in range(3):
            entries = [m[j]]
            for k in range(3):
                e = m[k] * u[j] - stress[k, j]
                entries.append(e + p if k == j else e)
            power = u[0] * stress[0, j] + u[1] * stress[1, j] + u[2] * stress[2, j]
            entries.append(ep * u[j] - power - (conductivity * STEP) * g[j][3])
            for c in range(5):
                if j == 0:
                    fxp[c, i + 3] = entries[c]
                elif j == 1:
                    fy[c, i] = entries[c]
                else:
                    dz[c, i] = around(entries[c])
        return 0

    lax.fori_loop(3, lx - 3, fluxes, 0)
    arrive(h1x)
    hear()
    tell()
    for i in edges:
        fluxes(i)
    h2x = x_halo(fxp, 5, 4)
    start(h2x)
    ysend2[...] = packed(lambda f: fy[f], 5)
    h2y = y_halo(ysend2, yhalo2, 6)
    start(h2y)

    for f in range(5):
        inner = block(dot(two(flat(fy[f]), 1), part("dy"), NN))
        for i in range(lx):
            s = difference(lambda k: fxp[f, i + 3 + k] if 0 <= i + k < lx else None)
            inc[f, i] = s + dz[f, i] + inner[i]

    width = 32 + 2 * (nx - 1)

    def xtab(k):
        return xt[ix * width + k]

    arrive(h2y)
    outer = two(yhalo2[...], 0)
    for fs in pairs(5):
        near = dot(outer, jnp.concatenate([part("ed", f) for f in fs], 1), TN)
        for n, f in enumerate(fs):
            add = block(near[:, n * ly : n * ly + ly])
            y0 = yl = None
            for i in range(lx):
                s = inc[f, i] + add[i]
                inc[f, i] = s
                a, b = float(scale * xinv[0, i]) * s, float(scale * xinv[-1, i]) * s
                y0, yl = (a, b) if i == 0 else (y0 + a, yl + b)
            first = [fxp[f, 3 + m] for m in range(3)]
            last = [fxp[f, lx + 2 - m] for m in range(3)]
            for w, base in ((0, 0), (1, 8)):
                near_side, far_side = (first, last) if w == 0 else (last, first)
                near_at, far_at = (2, 5) if w == 0 else (5, 2)
                total = xtab(base) * y0 + xtab(base + 1) * yl
                for m in range(3):
                    total += xtab(base + near_at + m) * near_side[m]
                xs[2 + w, f] = total
                for m in range(3):
                    total += xtab(base + far_at + m) * far_side[m]
                xs[w, f] = total
    solved = dot(three(xs[...].reshape(20 * lz, ly), 1), part("inverse"), NN)
    xl[...] = solved.reshape(4, 5, lz, ly)
    hear()
    while (1 << len(stages)) < nx - 1:
        tell()
        hear()
    copies = []
    for d in range(1, nx):
        above, below = (2 if d == 1 else 0), (3 if d == nx - 1 else 1)
        which = jnp.where(ix + d >= nx, below, above).astype(jnp.int32)
        copy = pltpu.make_async_remote_copy(
            xl.at[which], xr.at[d - 1], xss.at[d - 1], xrs.at[d - 1],
            device_id={"gx": lax.rem(ix + d, nx)}, device_id_type=MESH)
        copy.start()
        copies.append(copy)

    ywidth = 8 + 2 * (ny - 1)

    def ytab(k):
        return yt[iy * ywidth + k]

    def ends(data, f):
        w = part("wy", f)
        return dot(jnp.concatenate([w[0:16], w[0:16], w[16:32]], 1), data, NT)

    def y_exchange(values, source, target, send, receive):
        y0, yl = values[0:8], values[8:16]
        source[0] = ytab(0) * y0 + ytab(1) * yl
        source[1] = ytab(2) * y0 + ytab(3) * yl
        started = []
        for d in range(1, ny):
            which = jnp.where(iy + d >= ny, 1, 0).astype(jnp.int32)
            copy = pltpu.make_async_remote_copy(
                source.at[which], target.at[d - 1], send.at[d - 1], receive.at[d - 1],
                device_id={"gy": lax.rem(iy + d, ny)}, device_id_type=MESH)
            copy.start()
            started.append(copy)

        def finish():
            before = ytab(4) * y0 + ytab(5) * yl
            after = ytab(6) * y0 + ytab(7) * yl
            for d in range(1, ny):
                started[d - 1].wait_recv()
                r = target[d - 1]
                before += ytab(7 + d) * r
                after += ytab(7 + ny - 1 + d) * r
            return before, after

        return started, finish

    values = None
    spare = jnp.zeros((ly - 4 * lz, ly), jnp.float32)
    for f in range(5):
        p = ends(three(jnp.concatenate([xs[:, f].reshape(4 * lz, ly), spare], 0), 1), f)
        values = p if values is None else values + p
    vcopies, finish = y_exchange(values, vs, vr, vss, vrs)
    before, after = finish()
    lane = lax.broadcasted_iota(jnp.int32, (8, ly), 1)

    def shifted(v, by):
        return pltpu.roll(v, by % ly, 1) if by % ly else v

    for w in range(4):
        low, high = shifted(before, -lz * w), shifted(after, lz - lz * w)
        cs[w] = jnp.where(lane < lz, low, jnp.where(lane < 2 * lz, high, 0.0))
    ccopies = []
    for d in range(1, nx):
        above, below = (2 if d == 1 else 0), (3 if d == nx - 1 else 1)
        which = jnp.where(ix + d >= nx, below, above).astype(jnp.int32)
        copy = pltpu.make_async_remote_copy(
            cs.at[which], cr.at[d - 1], css.at[d - 1], crs.at[d - 1],
            device_id={"gx": lax.rem(ix + d, nx)}, device_id_type=MESH)
        copy.start()
        ccopies.append(copy)

    arrive(h2x)
    for fs in pairs(5):
        v = {}
        for i in range(lx):
            for f in fs:
                s = inc[f, i]
                if i < 3 or i >= lx - 3:
                    s = s + difference(lambda k: None if 0 <= i + k < lx else fxp[f, i + 3 + k])
                s = float(scale * ipiv[i]) * s
                v[f] = s if i == 0 else s + float(coefficient * ipiv[i]) * v[f]
                inc[f, i] = v[f]
        for i in range(lx - 2, -1, -1):
            for f in fs:
                v[f] = inc[f, i] - float(coefficient * ipiv[i]) * v[f]
                inc[f, i] = v[f]

    own_x = []
    for f in range(5):
        y0, yl = inc[f, 0], inc[f, lx - 1]
        terms = [y0, yl] + [fxp[f, 3 + m] for m in range(3)] + [fxp[f, lx + 2 - m] for m in range(3)]
        sides = []
        for base in (16, 24):
            total = xtab(base) * terms[0]
            for k in range(1, 8):
                total += xtab(base + k) * terms[k]
            sides.append(total)
        own_x.append(jnp.concatenate(sides, 0))

    values = small = None
    for f in range(5):
        data = three(flat(inc[f]), 1)
        p = ends(data, f)
        values = p if values is None else values + p
        fy[f] = block(dot(data, part("inverse"), NN))
        p = ends(three(own_x[f], 1), f)
        small = p if small is None else small + p
    spread = jnp.concatenate([part("spread", c) for c in range(rows // ly)], 1)
    values += dot(three(small, 1), spread, NN)
    ycopies, finish = y_exchange(values, ws, wr, wss, wrs)
    solved = dot(three(jnp.concatenate(own_x, 0), 1), part("inverse"), NN)
    for f in range(5):
        low, high = solved[2 * lz * f : 2 * lz * f + lz], solved[2 * lz * f + lz : 2 * lz * (f + 1)]
        for i in range(lx):
            at = pl.ds(i, lz, stride=lx)
            state = mass[at, :] if f == 0 else (energy[at, :] if f == 4 else mt[f - 1, i])
            inc[f, i] = state + fy[f, i] + float(alpha[i]) * low + float(beta[i]) * high
    outside = three(jnp.concatenate(finish(), 0), 0)
    for fs in pairs(5):
        far = dot(outside, jnp.concatenate([part("ey", f) for f in fs], 1), TN)
        for n, f in enumerate(fs):
            inc[f] += block(far[:, n * ly : n * ly + ly])

    for copy in ccopies:
        copy.wait_recv()
    sides = []
    for at in (31, 31 + nx - 1):
        total = xtab(at + 1) * cr[0]
        for d in range(2, nx):
            total += xtab(at + d) * cr[d - 1]
        sides.append(jnp.concatenate([total, shifted(total, -lz)], 0))
    lane = lax.broadcasted_iota(jnp.int32, (16, ly), 1)
    outside = three(jnp.where(lane < lz, sides[0], jnp.where(lane < 2 * lz, shifted(sides[1], lz), 0.0)), 0)
    for copy in copies:
        copy.wait_recv()
    for fs in pairs(5):
        far = dot(outside, jnp.concatenate([part("ey", f) for f in fs], 1), TN)
        for n, f in enumerate(fs):
            low = far[0:lz, n * ly : n * ly + ly]
            high = far[lz : 2 * lz, n * ly : n * ly + ly]
            for d in range(1, nx):
                r = xr[d - 1, f]
                low += xtab(31 + d) * r
                high += xtab(31 + nx - 1 + d) * r
            for i in range(lx):
                out[f, pl.ds(i, lz, stride=lx), :] = inc[f, i] + float(alpha[i]) * low + float(beta[i]) * high

    for halo in (h1x, h1y, h2x, h2y):
        sent(halo)
    for copy in copies + ccopies + vcopies + ycopies:
        copy.wait_send()


def body(nx, ny, mass, mom, energy):
    lz, lx, ly = mass.shape
    rows = lx * lz
    coefficient = float(max(lx, ly))
    xtab, xinv, xa, xb = coupled_tables(lx, nx, coefficient, -2.0 * coefficient * STEP)
    ytab, ya, yb = reduced_tables(ly, ny, coefficient)
    tab, places = lane_tables(lx, lz, ly, coefficient, xa, xb, ya, yb)
    vm = pl.BlockSpec(memory_space=pltpu.VMEM)
    hbm = pl.BlockSpec(memory_space=pltpu.HBM)
    f32 = jnp.float32
    block = (lx, lz, ly)
    dma = pltpu.SemaphoreType.DMA
    operands = (
        mass.reshape(rows, ly), mom.reshape(3, rows, ly), energy.reshape(rows, ly),
        jnp.asarray(tab), jnp.asarray(xtab.reshape(-1)), jnp.asarray(ytab.reshape(-1)),
    )
    result = pl.pallas_call(
        functools.partial(
            kernel, nx, ny, lx, lz, ly, coefficient, pivots(lx, coefficient), xinv, xa, xb, places),
        out_shape=jax.ShapeDtypeStruct((5, rows, ly), f32),
        in_specs=[hbm] * 6,
        out_specs=vm,
        scratch_shapes=[
            pltpu.VMEM((rows, ly), f32),
            pltpu.VMEM((3, rows, ly), f32),
            pltpu.VMEM((rows, ly), f32),
            pltpu.VMEM(tab.shape, jnp.bfloat16),
            pltpu.SMEM((xtab.size,), f32),
            pltpu.SMEM((ytab.size,), f32),
            pltpu.VMEM((4, lx + 6, lz, ly), f32),
            pltpu.VMEM(block, f32),
            pltpu.VMEM(block, f32),
            pltpu.VMEM((3, *block), f32),
            pltpu.VMEM((4, *block), f32),
            pltpu.VMEM((5, lx + 6, lz, ly), f32),
            pltpu.VMEM((5, *block), f32),
            pltpu.VMEM((5, *block), f32),
            pltpu.VMEM((5, *block), f32),
            pltpu.VMEM((32, rows), f32),
            pltpu.VMEM((32, rows), f32),
            pltpu.VMEM((32, rows), f32),
            pltpu.VMEM((32, rows), f32),
            pltpu.VMEM((4, 5, lz, ly), f32),
            pltpu.VMEM((4, 5, lz, ly), f32),
            pltpu.VMEM((nx - 1, 5, lz, ly), f32),
            pltpu.VMEM((2, 8, rows), f32),
            pltpu.VMEM((ny - 1, 8, rows), f32),
            pltpu.VMEM((2, 8, ly), f32),
            pltpu.VMEM((ny - 1, 8, ly), f32),
            pltpu.VMEM((4, 8, ly), f32),
            pltpu.VMEM((nx - 1, 8, ly), f32),
            dma((8,)),
            dma((8,)),
            dma((nx - 1,)),
            dma((nx - 1,)),
            dma((ny - 1,)),
            dma((ny - 1,)),
            dma((ny - 1,)),
            dma((ny - 1,)),
            dma((nx - 1,)),
            dma((nx - 1,)),
            dma((6,)),
            pltpu.SemaphoreType.REGULAR((max(1, (nx - 1).bit_length()),)),
        ],
        compiler_params=pltpu.CompilerParams(
            collective_id=0, has_side_effects=True, vmem_limit_bytes=40 * 2**20
        ),
    )(*[pltpu.with_memory_space_constraint(a, pltpu.HBM) for a in operands])
    return result.reshape(5, lz, lx, ly)


def solution(mesh):
    return jax.shard_map(
        functools.partial(body, mesh.shape["gx"], mesh.shape["gy"]),
        mesh=mesh,
        in_specs=(P(None, "gx", "gy"), P(None, None, "gx", "gy"), P(None, "gx", "gy")),
        out_specs=P(None, None, "gx", "gy"),
        check_vma=False,
    )
```

```python
import functools
import jax
import jax.numpy as jnp
import ml_dtypes
import numpy as np
from jax import lax
from jax.experimental import pallas as pl
from jax.experimental.pallas import tpu as pltpu
from jax.sharding import PartitionSpec as P

viscosity = 0.1
conductivity = 0.1 * 1.4 / (0.4 * 0.72)
MESH = pl.DeviceIdType.MESH
WEIGHTS = {1: 45.0, -1: -45.0, 2: -9.0, -2: 9.0, 3: 1.0, -3: -1.0}
STEP = 1.0 / 60.0


def local_inverse(length, coefficient):
    matrix = np.eye(length)
    matrix += coefficient * (np.eye(length, k=1) - np.eye(length, k=-1))
    return np.linalg.inv(matrix)


def reduced_system(length, count, coefficient):
    inverse = local_inverse(length, coefficient)
    alpha, beta = coefficient * inverse[:, 0], -coefficient * inverse[:, -1]
    system = np.eye(2 * count)
    for b in range(count):
        for row, at in ((2 * b, 0), (2 * b + 1, length - 1)):
            if b > 0:
                system[row, 2 * b - 1] -= alpha[at]
            if b < count - 1:
                system[row, 2 * b + 2] -= beta[at]
    g = np.linalg.inv(system)
    up = [g[2 * b + 1, 2 * b : 2 * b + 2] for b in range(count)]
    down = [g[2 * b, 2 * b : 2 * b + 2] for b in range(count)]
    return inverse, alpha, beta, g, up, down


def outside_lines(g, b, count):
    prev = g[2 * b - 1] if b > 0 else np.zeros(2 * count)
    nxt = g[2 * b + 2] if b < count - 1 else np.zeros(2 * count)
    return prev, nxt


def received(line, b, count, up, down):
    weights = []
    for d in range(1, count):
        other = (b - d) % count
        basis = up[other] if other < b else down[other]
        weights.append(line[2 * other : 2 * other + 2] @ basis / (basis @ basis))
    return weights


def reduced_tables(length, count, coefficient):
    inverse, alpha, beta, g, up, down = reduced_system(length, count, coefficient)
    rows = []
    for b in range(count):
        prev, nxt = outside_lines(g, b, count)
        own = [*prev[2 * b : 2 * b + 2], *nxt[2 * b : 2 * b + 2]]
        rows.append([*up[b], *down[b], *own, *received(prev, b, count, up, down), *received(nxt, b, count, up, down)])
    return np.asarray(rows).astype(np.float32), alpha, beta


def coupled_tables(length, count, coefficient, scale):
    inverse, alpha, beta, g, up, down = reduced_system(length, count, coefficient)
    ends = [0, length - 1]
    to_next, to_prev = [], []
    for m in range(3):
        n, p = np.zeros(2), np.zeros(2)
        for r in range(3 - m):
            n += scale * inverse[ends, r] * WEIGHTS[-(r + 1 + m)]
            p += scale * inverse[ends, length - 1 - r] * WEIGHTS[r + 1 + m]
        to_next.append(n)
        to_prev.append(p)
    rows = []
    for b in range(count):
        prev, nxt = outside_lines(g, b, count)

        def via(line, j, spread):
            if not 0 <= j < count:
                return [0.0] * 3
            return [line[2 * j : 2 * j + 2] @ s for s in spread]

        def ratio(line, j, basis):
            return line[2 * j : 2 * j + 2] @ basis[j] / (basis[j] @ basis[j])

        def sent(basis, t, line_at):
            if not 0 <= t < count:
                low, high = 0.0, 0.0
                ref = None
            else:
                ref = g[line_at(t)]
            out = []
            for j, spread in ((b - 1, to_prev), (b + 1, to_next)):
                if not 0 <= j < count:
                    out += [0.0] * 3
                    continue
                line = ref
                if line is None:
                    line = g[line_at(b + 1 if basis is up else b - 1)] if 0 <= (b + 1 if basis is up else b - 1) < count else None
                beyond = (j > b) if basis is up else (j < b)
                if line is None or (ref is None and beyond):
                    out += [0.0] * 3
                    continue
                scale_j = ratio(line, j, basis) / ratio(line, b, basis)
                out += [scale_j * (basis[j] @ s) for s in spread]
            return out

        u = sent(up, b + 2, lambda t: 2 * t - 1)
        d = sent(down, b - 2, lambda t: 2 * t + 2)
        own = []
        for line in (prev, nxt):
            own += [*line[2 * b : 2 * b + 2], *via(line, b - 1, to_prev), *via(line, b + 1, to_next)]
        rows.append([*up[b], *u, *down[b], *d, *own, *received(prev, b, count, up, down), *received(nxt, b, count, up, down)])
    return np.asarray(rows).astype(np.float32), inverse, alpha, beta


def pivots(length, coefficient):
    inverse_pivot = np.ones(length)
    for i in range(1, length):
        inverse_pivot[i] = 1.0 / (1.0 + coefficient * coefficient * inverse_pivot[i - 1])
    return inverse_pivot


def halves(matrix):
    high = matrix.astype(ml_dtypes.bfloat16)
    low = (matrix - high.astype(np.float64)).astype(ml_dtypes.bfloat16)
    return high.astype(np.float64), low.astype(np.float64)


def lane_tables(lx, lz, ly, coefficient, xinv, xa, xb, ya, yb):
    inverse = local_inverse(ly, coefficient)
    dy = np.zeros((ly, ly))
    for j in range(ly):
        for k, w in WEIGHTS.items():
            if 0 <= j + k < ly:
                dy[j + k, j] = w
    sel = np.zeros((5, 32, ly))
    ed = np.zeros((5, 32, ly))
    wy = np.zeros((5, 16, ly))
    ey = np.zeros((5, 16, ly))
    for f in range(5):
        for k in range(3):
            sel[f, 3 * f + k, k] = 1.0
            sel[f, 16 + 3 * f + k, ly - 3 + k] = 1.0
            for row, position in ((3 * f + k, k - 3), (16 + 3 * f + k, ly + k)):
                for step, w in WEIGHTS.items():
                    if 0 <= position - step < ly:
                        ed[f, row, position - step] = w
        wy[f, f], wy[f, 8 + f] = inverse[0], inverse[-1]
        ey[f, f], ey[f, 8 + f] = ya, yb
    profiles = [xa, xb, *(xinv[:, r] for r in (*range(3), *range(lx - 3, lx)))]
    spread = np.zeros((8, lz, lx, lz))
    for n, profile in enumerate(profiles):
        for z in range(lz):
            spread[n, z, :, z] = profile
    spread = spread.reshape(8 * lz, lx * lz)
    parts = {"dy": np.concatenate([dy, dy])}
    high, low = halves(inverse.T)
    parts["inverse"] = np.concatenate([high, high, low])
    for f in range(5):
        parts["sel", f] = sel[f]
        parts["ed", f] = np.concatenate([ed[f], ed[f]])
        high, low = halves(wy[f])
        parts["wy", f] = np.concatenate([high, low])
        high, low = halves(ey[f])
        parts["ey", f] = np.concatenate([high, high, low])
    high, low = halves(spread)
    spread = np.concatenate([high, high, low])
    for c in range(lx * lz // ly):
        parts["spread", c] = spread[:, c * ly : c * ly + ly]
    places, at = {}, 0
    for name, part in parts.items():
        places[name] = (at, at + part.shape[0])
        at += part.shape[0]
    return np.concatenate(list(parts.values()), 0).astype(ml_dtypes.bfloat16), places


NN, NT, TN = ((1,), (0,)), ((1,), (1,)), ((0,), (0,))


def dot(a, b, dims):
    return lax.dot_general(a, b, (dims, ((), ())), preferred_element_type=jnp.float32)


def split(v):
    high = v.astype(jnp.bfloat16)
    low = (v - high.astype(jnp.float32)).astype(jnp.bfloat16)
    return high, low


def two(v, axis):
    return jnp.concatenate(split(v), axis)


def three(v, axis):
    high, low = split(v)
    return jnp.concatenate([high, low, high], axis)


def difference(at):
    total = None
    for k, w in ((1, 45.0), (2, -9.0), (3, 1.0)):
        a, b = at(k), at(-k)
        if a is None and b is None:
            continue
        pair = -b if a is None else (a if b is None else a - b)
        pair = pair if w == 1.0 else w * pair
        total = pair if total is None else total + pair
    return total


def around(v):
    n = v.shape[0]
    return difference(lambda k: pltpu.roll(v, (-k) % n, 0))


def kernel(
    nx, ny, lx, lz, ly, coefficient, ipiv, xinv, alpha, beta, places,
    mass_in, mom_in, energy_in, tab_in, xt_in, yt_in, out, low_out, high_out,
    mass, mom, energy, tab, xt, yt,
    xp, pt, ept, mt, gy, pre, fxp, fy, dz, inc, ysend, yhalo, ysend2, yhalo2,
    xs, xl, xr, ws, wr, vs, vr, cs, cr,
    hss, hrs, xss, xrs, wss, wrs, vss, vrs, css, crs, lsem, near_sem,
):
    ix, iy = lax.axis_index("gx"), lax.axis_index("gy")
    rows = lx * lz
    scale = -2.0 * coefficient * STEP

    barrier = pltpu.get_barrier_semaphore()


    def both_sides(semaphore, distance):
        above, below = ix + distance < nx, ix - distance >= 0

        @pl.when(above)
        def _():
            pl.semaphore_signal(semaphore, inc=1, device_id={"gx": ix + distance}, device_id_type=MESH)

        @pl.when(below)
        def _():
            pl.semaphore_signal(semaphore, inc=1, device_id={"gx": ix - distance}, device_id_type=MESH)

        return above.astype(jnp.int32) + below.astype(jnp.int32)

    expected = both_sides(barrier, 1)
    stages = []

    def tell():
        distance = 1 << len(stages)
        if distance < nx - 1:
            stages.append(both_sides(near_sem.at[len(stages)], distance))

    def hear():
        if stages and stages[-1] is not None:
            pl.semaphore_wait(near_sem.at[len(stages) - 1], stages[-1])

    for d in range(1, ny):
        pl.semaphore_signal(barrier, inc=1, device_id={"gy": lax.rem(iy + d, ny)}, device_id_type=MESH)

    loads = [
        pltpu.make_async_copy(a, b, lsem.at[k])
        for k, (a, b) in enumerate((
            (mass_in, mass), (mom_in, mom), (energy_in, energy), (tab_in, tab), (xt_in, xt), (yt_in, yt)))
    ]
    for load in loads:
        load.start()

    def part(*name):
        low, high = places[name if len(name) > 1 else name[0]]
        return tab[low:high]

    def flat(v):
        return v.reshape(rows, ly)

    def block(v):
        return v.reshape(lx, lz, ly)

    def primitives(i, _=None):
        at = pl.ds(i, lz, stride=lx)
        rho, e = mass[at, :], energy[at, :]
        m = [mom[k, at, :] for k in range(3)]
        inv = 1.0 / rho
        u = [a * inv for a in m]
        p = 0.4 * (e - 0.5 * (m[0] * u[0] + m[1] * u[1] + m[2] * u[2]))
        for k in range(3):
            xp[k, i + 3] = u[k]
            mt[k, i] = m[k]
        xp[3, i + 3] = p * inv
        pt[i] = p
        ept[i] = e + p
        return 0

    for load in loads[:3]:
        load.wait()
    edges = sorted({*range(3), *range(lx - 3, lx)})
    for i in edges:
        primitives(i)

    zeros3 = jnp.zeros((3, lz, ly), jnp.float32)

    def x_halo(ref, fields, base):
        to_next = pltpu.make_async_remote_copy(
            ref.at[:, pl.ds(lx, 3)], ref.at[:, pl.ds(0, 3)], hss.at[base], hrs.at[base],
            device_id={"gx": ix + 1}, device_id_type=MESH)
        to_prev = pltpu.make_async_remote_copy(
            ref.at[:, pl.ds(3, 3)], ref.at[:, pl.ds(lx + 3, 3)], hss.at[base + 1], hrs.at[base + 1],
            device_id={"gx": ix - 1}, device_id_type=MESH)

        @pl.when(ix == 0)
        def _():
            for f in range(fields):
                ref[f, 0:3] = zeros3

        @pl.when(ix == nx - 1)
        def _():
            for f in range(fields):
                ref[f, lx + 3 : lx + 6] = zeros3

        return to_next, to_prev, ix, nx

    def y_halo(source, ref, base):
        to_next = pltpu.make_async_remote_copy(
            source.at[pl.ds(16, 16)], ref.at[pl.ds(0, 16)], hss.at[base], hrs.at[base],
            device_id={"gy": iy + 1}, device_id_type=MESH)
        to_prev = pltpu.make_async_remote_copy(
            source.at[pl.ds(0, 16)], ref.at[pl.ds(16, 16)], hss.at[base + 1], hrs.at[base + 1],
            device_id={"gy": iy - 1}, device_id_type=MESH)

        @pl.when(iy == 0)
        def _():
            ref[0:16] = jnp.zeros((16, rows), jnp.float32)

        @pl.when(iy == ny - 1)
        def _():
            ref[16:32] = jnp.zeros((16, rows), jnp.float32)

        return to_next, to_prev, iy, ny

    def start(halo):
        to_next, to_prev, here, count = halo
        pl.when(here < count - 1)(to_next.start)
        pl.when(here > 0)(to_prev.start)

    def arrive(halo):
        to_next, to_prev, here, count = halo
        pl.when(here > 0)(to_next.wait_recv)
        pl.when(here < count - 1)(to_prev.wait_recv)

    def sent(halo):
        to_next, to_prev, here, count = halo
        pl.when(here < count - 1)(to_next.wait_send)
        pl.when(here > 0)(to_prev.wait_send)

    def packed(field, fields):
        total = None
        for f in range(fields):
            s = part("sel", f)
            p = dot(jnp.concatenate([s, s], 1), two(flat(field(f)), 1), NT)
            total = p if total is None else total + p
        return total

    def pairs(count):
        return [tuple(range(f, min(f + 2, count))) for f in range(0, count, 2)]

    h1x = x_halo(xp, 4, 0)
    pl.semaphore_wait(barrier, expected + (ny - 1))
    start(h1x)
    tell()
    lax.fori_loop(3, lx - 3, primitives, 0, unroll=2)
    for load in loads[3:]:
        load.wait()
    ysend[...] = packed(lambda f: xp[f, 3 : lx + 3], 4)
    h1y = y_halo(ysend, yhalo, 2)
    start(h1y)
    for f in range(4):
        gy[f] = block(dot(two(flat(xp[f, 3 : lx + 3]), 1), part("dy"), NN))

    def gradients(i):
        x = [difference(lambda k: xp[f, i + 3 + k]) for f in range(4)]
        z = [around(xp[f, i + 3]) for f in range(4)]
        return x[0], z[2], x[1], x[2] + z[0], z[1], x[3], z[3]

    def ahead(i, _=None):
        for n, g in enumerate(gradients(i)):
            pre[n, i] = g
        return 0

    lax.fori_loop(3, lx - 3, ahead, 0, unroll=2)
    arrive(h1y)
    hear()
    tell()
    outer = two(yhalo[...], 0)
    for fs in pairs(4):
        near = dot(outer, jnp.concatenate([part("ed", f) for f in fs], 1), TN)
        for n, f in enumerate(fs):
            gy[f] += block(near[:, n * ly : n * ly + ly])

    def fluxes(i, g=None):
        u = [xp[k, i + 3] for k in range(3)]
        m = [mt[k, i] for k in range(3)]
        p, ep = pt[i], ept[i]
        xx, zz, xv, xz, zv, xt, zt = g or [pre[n, i] for n in range(7)]
        yu, yy, yw, yt = [gy[f, i] for f in range(4)]
        dilation = (2.0 / 3.0 * viscosity * STEP) * (xx + yy + zz)
        twice, once = 2.0 * viscosity * STEP, viscosity * STEP
        stress = {
            (0, 0): twice * xx - dilation, (1, 1): twice * yy - dilation, (2, 2): twice * zz - dilation,
            (0, 1): once * (xv + yu), (0, 2): once * xz, (1, 2): once * (yw + zv),
        }
        for a, b in ((0, 1), (0, 2), (1, 2)):
            stress[b, a] = stress[a, b]
        heat = (xt, yt, zt)
        for j in range(3):
            entries = [m[j]]
            for k in range(3):
                e = m[k] * u[j] - stress[k, j]
                entries.append(e + p if k == j else e)
            power = u[0] * stress[0, j] + u[1] * stress[1, j] + u[2] * stress[2, j]
            entries.append(ep * u[j] - power - (conductivity * STEP) * heat[j])
            for c in range(5):
                if j == 0:
                    fxp[c, i + 3] = entries[c]
                elif j == 1:
                    fy[c, i] = entries[c]
                else:
                    dz[c, i] = around(entries[c])
        return 0

    def inner(i, _):
        return fluxes(i)

    lax.fori_loop(3, lx - 3, inner, 0)
    arrive(h1x)
    hear()
    tell()
    for i in edges:
        fluxes(i, gradients(i))
    h2x = x_halo(fxp, 5, 4)
    start(h2x)
    ysend2[...] = packed(lambda f: fy[f], 5)
    h2y = y_halo(ysend2, yhalo2, 6)
    start(h2y)

    for f in range(5):
        inner = block(dot(two(flat(fy[f]), 1), part("dy"), NN))
        for i in range(lx):
            s = difference(lambda k: fxp[f, i + 3 + k] if 0 <= i + k < lx else None)
            inc[f, i] = s + dz[f, i] + inner[i]

    width = 32 + 2 * (nx - 1)

    def xtab(k):
        return xt[ix * width + k]

    arrive(h2y)
    outer = two(yhalo2[...], 0)
    for fs in pairs(5):
        near = dot(outer, jnp.concatenate([part("ed", f) for f in fs], 1), TN)
        for n, f in enumerate(fs):
            add = block(near[:, n * ly : n * ly + ly])
            y0 = yl = None
            for i in range(lx):
                s = inc[f, i] + add[i]
                inc[f, i] = s
                a, b = float(scale * xinv[0, i]) * s, float(scale * xinv[-1, i]) * s
                y0, yl = (a, b) if i == 0 else (y0 + a, yl + b)
            first = [fxp[f, 3 + m] for m in range(3)]
            last = [fxp[f, lx + 2 - m] for m in range(3)]
            for w, base in ((0, 0), (1, 8)):
                near_side, far_side = (first, last) if w == 0 else (last, first)
                near_at, far_at = (2, 5) if w == 0 else (5, 2)
                total = xtab(base) * y0 + xtab(base + 1) * yl
                for m in range(3):
                    total += xtab(base + near_at + m) * near_side[m]
                xs[2 + w, f] = total
                for m in range(3):
                    total += xtab(base + far_at + m) * far_side[m]
                xs[w, f] = total
    solved = dot(three(xs[...].reshape(20 * lz, ly), 1), part("inverse"), NN)
    xl[...] = solved.reshape(4, 5, lz, ly)
    hear()
    while (1 << len(stages)) < nx - 1:
        tell()
        hear()
    copies = []
    for d in range(1, nx):
        above, below = (2 if d == 1 else 0), (3 if d == nx - 1 else 1)
        which = jnp.where(ix + d >= nx, below, above).astype(jnp.int32)
        copy = pltpu.make_async_remote_copy(
            xl.at[which], xr.at[d - 1], xss.at[d - 1], xrs.at[d - 1],
            device_id={"gx": lax.rem(ix + d, nx)}, device_id_type=MESH)
        copy.start()
        copies.append(copy)

    ywidth = 8 + 2 * (ny - 1)

    def ytab(k):
        return yt[iy * ywidth + k]

    def ends(data, f):
        w = part("wy", f)
        return dot(jnp.concatenate([w[0:16], w[0:16], w[16:32]], 1), data, NT)

    def y_exchange(values, source, target, send, receive):
        y0, yl = values[0:8], values[8:16]
        source[0] = ytab(0) * y0 + ytab(1) * yl
        source[1] = ytab(2) * y0 + ytab(3) * yl
        started = []
        for d in range(1, ny):
            which = jnp.where(iy + d >= ny, 1, 0).astype(jnp.int32)
            copy = pltpu.make_async_remote_copy(
                source.at[which], target.at[d - 1], send.at[d - 1], receive.at[d - 1],
                device_id={"gy": lax.rem(iy + d, ny)}, device_id_type=MESH)
            copy.start()
            started.append(copy)

        def finish():
            before = ytab(4) * y0 + ytab(5) * yl
            after = ytab(6) * y0 + ytab(7) * yl
            for d in range(1, ny):
                started[d - 1].wait_recv()
                r = target[d - 1]
                before += ytab(7 + d) * r
                after += ytab(7 + ny - 1 + d) * r
            return before, after

        return started, finish

    values = None
    spare = jnp.zeros((ly - 4 * lz, ly), jnp.float32)
    for f in range(5):
        p = ends(three(jnp.concatenate([xs[:, f].reshape(4 * lz, ly), spare], 0), 1), f)
        values = p if values is None else values + p
    vcopies, finish = y_exchange(values, vs, vr, vss, vrs)
    for fs in pairs(5):
        v = {}
        for i in range(lx):
            for f in fs:
                s = float(scale * ipiv[i]) * inc[f, i]
                v[f] = s if i == 0 else s + float(coefficient * ipiv[i]) * v[f]
                inc[f, i] = v[f]
        for i in range(lx - 2, -1, -1):
            for f in fs:
                v[f] = inc[f, i] - float(coefficient * ipiv[i]) * v[f]
                inc[f, i] = v[f]
    local = None
    for f in range(5):
        data = three(flat(inc[f]), 1)
        p = ends(data, f)
        local = p if local is None else local + p
        fy[f] = block(dot(data, part("inverse"), NN))
    before, after = finish()
    lane = lax.broadcasted_iota(jnp.int32, (8, ly), 1)

    def shifted(v, by):
        return pltpu.roll(v, by % ly, 1) if by % ly else v

    for w in range(4):
        low, high = shifted(before, -lz * w), shifted(after, lz - lz * w)
        cs[w] = jnp.where(lane < lz, low, jnp.where(lane < 2 * lz, high, 0.0))
    ccopies = []
    for d in range(1, nx):
        above, below = (2 if d == 1 else 0), (3 if d == nx - 1 else 1)
        which = jnp.where(ix + d >= nx, below, above).astype(jnp.int32)
        copy = pltpu.make_async_remote_copy(
            cs.at[which], cr.at[d - 1], css.at[d - 1], crs.at[d - 1],
            device_id={"gx": lax.rem(ix + d, nx)}, device_id_type=MESH)
        copy.start()
        ccopies.append(copy)

    arrive(h2x)
    halo_rows = [*range(3), *range(lx - 3, lx)]
    own_x = []
    small = None
    for f in range(5):
        added = []
        for i in halo_rows:
            added.append(scale * difference(lambda k: None if 0 <= i + k < lx else fxp[f, i + 3 + k]))
        y0, yl = inc[f, 0], inc[f, lx - 1]
        for i, v in zip(halo_rows, added):
            y0 += float(xinv[0, i]) * v
            yl += float(xinv[-1, i]) * v
        terms = [y0, yl] + [fxp[f, 3 + m] for m in range(3)] + [fxp[f, lx + 2 - m] for m in range(3)]
        sides = []
        for base in (16, 24):
            total = xtab(base) * terms[0]
            for k in range(1, 8):
                total += xtab(base + k) * terms[k]
            sides.append(total)
        own_x.append(jnp.concatenate(sides + added, 0))
        p = ends(three(own_x[f], 1), f)
        small = p if small is None else small + p
    spread = jnp.concatenate([part("spread", c) for c in range(rows // ly)], 1)
    ycopies, finish = y_exchange(local + dot(three(small, 1), spread, NN), ws, wr, wss, wrs)
    solved = dot(three(jnp.concatenate(own_x, 0), 1), part("inverse"), NN)
    for f in range(5):
        pieces = [solved[lz * (8 * f + n) : lz * (8 * f + n + 1)] for n in range(8)]
        for i in range(lx):
            at = pl.ds(i, lz, stride=lx)
            state = mass[at, :] if f == 0 else (energy[at, :] if f == 4 else mt[f - 1, i])
            total = state + fy[f, i]
            weights = [alpha[i], beta[i], *(xinv[i, r] for r in halo_rows)]
            for w, v in zip(weights, pieces):
                total += float(w) * v
            inc[f, i] = total
    outside = three(jnp.concatenate(finish(), 0), 0)
    for fs in pairs(5):
        far = dot(outside, jnp.concatenate([part("ey", f) for f in fs], 1), TN)
        for n, f in enumerate(fs):
            total = block(far[:, n * ly : n * ly + ly])
            for i in range(lx):
                out[f, pl.ds(i, lz, stride=lx), :] = inc[f, i] + total[i]

    for copy in ccopies:
        copy.wait_recv()
    sides = []
    for at in (31, 31 + nx - 1):
        total = xtab(at + 1) * cr[0]
        for d in range(2, nx):
            total += xtab(at + d) * cr[d - 1]
        sides.append(jnp.concatenate([total, shifted(total, -lz)], 0))
    lane = lax.broadcasted_iota(jnp.int32, (16, ly), 1)
    outside = three(jnp.where(lane < lz, sides[0], jnp.where(lane < 2 * lz, shifted(sides[1], lz), 0.0)), 0)
    for copy in copies:
        copy.wait_recv()
    for fs in pairs(5):
        far = dot(outside, jnp.concatenate([part("ey", f) for f in fs], 1), TN)
        for n, f in enumerate(fs):
            low = far[0:lz, n * ly : n * ly + ly]
            high = far[lz : 2 * lz, n * ly : n * ly + ly]
            for d in range(1, nx):
                r = xr[d - 1, f]
                low += xtab(31 + d) * r
                high += xtab(31 + nx - 1 + d) * r
            low_out[f], high_out[f] = low, high

    for halo in (h1x, h1y, h2x, h2y):
        sent(halo)
    for copy in copies + ccopies + vcopies + ycopies:
        copy.wait_send()


def body(nx, ny, mass, mom, energy):
    lz, lx, ly = mass.shape
    rows = lx * lz
    coefficient = float(max(lx, ly))
    xtab, xinv, xa, xb = coupled_tables(lx, nx, coefficient, -2.0 * coefficient * STEP)
    ytab, ya, yb = reduced_tables(ly, ny, coefficient)
    tab, places = lane_tables(lx, lz, ly, coefficient, xinv, xa, xb, ya, yb)
    vm = pl.BlockSpec(memory_space=pltpu.VMEM)
    hbm = pl.BlockSpec(memory_space=pltpu.HBM)
    f32 = jnp.float32
    block = (lx, lz, ly)
    dma = pltpu.SemaphoreType.DMA
    operands = (
        mass.reshape(rows, ly), mom.reshape(3, rows, ly), energy.reshape(rows, ly),
        jnp.asarray(tab), jnp.asarray(xtab.reshape(-1)), jnp.asarray(ytab.reshape(-1)),
    )
    result, low, high = pl.pallas_call(
        functools.partial(
            kernel, nx, ny, lx, lz, ly, coefficient, pivots(lx, coefficient), xinv, xa, xb, places),
        out_shape=(jax.ShapeDtypeStruct((5, rows, ly), f32), *[jax.ShapeDtypeStruct((5, lz, ly), f32)] * 2),
        in_specs=[hbm] * 6,
        out_specs=(vm, vm, vm),
        scratch_shapes=[
            pltpu.VMEM((rows, ly), f32),
            pltpu.VMEM((3, rows, ly), f32),
            pltpu.VMEM((rows, ly), f32),
            pltpu.VMEM(tab.shape, jnp.bfloat16),
            pltpu.SMEM((xtab.size,), f32),
            pltpu.SMEM((ytab.size,), f32),
            pltpu.VMEM((4, lx + 6, lz, ly), f32),
            pltpu.VMEM(block, f32),
            pltpu.VMEM(block, f32),
            pltpu.VMEM((3, *block), f32),
            pltpu.VMEM((4, *block), f32),
            pltpu.VMEM((7, *block), f32),
            pltpu.VMEM((5, lx + 6, lz, ly), f32),
            pltpu.VMEM((5, *block), f32),
            pltpu.VMEM((5, *block), f32),
            pltpu.VMEM((5, *block), f32),
            pltpu.VMEM((32, rows), f32),
            pltpu.VMEM((32, rows), f32),
            pltpu.VMEM((32, rows), f32),
            pltpu.VMEM((32, rows), f32),
            pltpu.VMEM((4, 5, lz, ly), f32),
            pltpu.VMEM((4, 5, lz, ly), f32),
            pltpu.VMEM((nx - 1, 5, lz, ly), f32),
            pltpu.VMEM((2, 8, rows), f32),
            pltpu.VMEM((ny - 1, 8, rows), f32),
            pltpu.VMEM((2, 8, ly), f32),
            pltpu.VMEM((ny - 1, 8, ly), f32),
            pltpu.VMEM((4, 8, ly), f32),
            pltpu.VMEM((nx - 1, 8, ly), f32),
            dma((8,)),
            dma((8,)),
            dma((nx - 1,)),
            dma((nx - 1,)),
            dma((ny - 1,)),
            dma((ny - 1,)),
            dma((ny - 1,)),
            dma((ny - 1,)),
            dma((nx - 1,)),
            dma((nx - 1,)),
            dma((6,)),
            pltpu.SemaphoreType.REGULAR((max(1, (nx - 1).bit_length()),)),
        ],
        compiler_params=pltpu.CompilerParams(
            collective_id=0, has_side_effects=True, vmem_limit_bytes=40 * 2**20
        ),
    )(*[pltpu.with_memory_space_constraint(a, pltpu.HBM) for a in operands])
    low, high = low[:, :, None], high[:, :, None]
    along = [jnp.broadcast_to(jnp.asarray(w.astype(np.float32))[:, None], (lx, ly)) for w in (xa, xb)]
    return result.reshape(5, lz, lx, ly) + along[0] * low + along[1] * high


def solution(mesh):
    return jax.shard_map(
        functools.partial(body, mesh.shape["gx"], mesh.shape["gy"]),
        mesh=mesh,
        in_specs=(P(None, "gx", "gy"), P(None, None, "gx", "gy"), P(None, "gx", "gy")),
        out_specs=P(None, None, "gx", "gy"),
        check_vma=False,
    )
```

```python
import functools
import jax
import jax.numpy as jnp
import ml_dtypes
import numpy as np
from jax import lax
from jax.experimental import pallas as pl
from jax.experimental.pallas import tpu as pltpu
from jax.sharding import PartitionSpec as P

viscosity = 0.1
conductivity = 0.1 * 1.4 / (0.4 * 0.72)
MESH = pl.DeviceIdType.MESH
WEIGHTS = {1: 45.0, -1: -45.0, 2: -9.0, -2: 9.0, 3: 1.0, -3: -1.0}
STEP = 1.0 / 60.0


def local_inverse(length, coefficient):
    matrix = np.eye(length)
    matrix += coefficient * (np.eye(length, k=1) - np.eye(length, k=-1))
    return np.linalg.inv(matrix)


def reduced_system(length, count, coefficient):
    inverse = local_inverse(length, coefficient)
    alpha, beta = coefficient * inverse[:, 0], -coefficient * inverse[:, -1]
    system = np.eye(2 * count)
    for b in range(count):
        for row, at in ((2 * b, 0), (2 * b + 1, length - 1)):
            if b > 0:
                system[row, 2 * b - 1] -= alpha[at]
            if b < count - 1:
                system[row, 2 * b + 2] -= beta[at]
    g = np.linalg.inv(system)
    up = [g[2 * b + 1, 2 * b : 2 * b + 2] for b in range(count)]
    down = [g[2 * b, 2 * b : 2 * b + 2] for b in range(count)]
    return inverse, alpha, beta, g, up, down


def outside_lines(g, b, count):
    prev = g[2 * b - 1] if b > 0 else np.zeros(2 * count)
    nxt = g[2 * b + 2] if b < count - 1 else np.zeros(2 * count)
    return prev, nxt


def received(line, b, count, up, down):
    weights = []
    for d in range(1, count):
        other = (b - d) % count
        basis = up[other] if other < b else down[other]
        weights.append(line[2 * other : 2 * other + 2] @ basis / (basis @ basis))
    return weights


def reduced_tables(length, count, coefficient):
    inverse, alpha, beta, g, up, down = reduced_system(length, count, coefficient)
    rows = []
    for b in range(count):
        prev, nxt = outside_lines(g, b, count)
        own = [*prev[2 * b : 2 * b + 2], *nxt[2 * b : 2 * b + 2]]
        rows.append([*up[b], *down[b], *own, *received(prev, b, count, up, down), *received(nxt, b, count, up, down)])
    return np.asarray(rows).astype(np.float32), alpha, beta


def coupled_tables(length, count, coefficient, scale):
    inverse, alpha, beta, g, up, down = reduced_system(length, count, coefficient)
    ends = [0, length - 1]
    to_next, to_prev = [], []
    for m in range(3):
        n, p = np.zeros(2), np.zeros(2)
        for r in range(3 - m):
            n += scale * inverse[ends, r] * WEIGHTS[-(r + 1 + m)]
            p += scale * inverse[ends, length - 1 - r] * WEIGHTS[r + 1 + m]
        to_next.append(n)
        to_prev.append(p)
    rows = []
    for b in range(count):
        prev, nxt = outside_lines(g, b, count)

        def via(line, j, spread):
            if not 0 <= j < count:
                return [0.0] * 3
            return [line[2 * j : 2 * j + 2] @ s for s in spread]

        def ratio(line, j, basis):
            return line[2 * j : 2 * j + 2] @ basis[j] / (basis[j] @ basis[j])

        def sent(basis, t, line_at):
            if not 0 <= t < count:
                low, high = 0.0, 0.0
                ref = None
            else:
                ref = g[line_at(t)]
            out = []
            for j, spread in ((b - 1, to_prev), (b + 1, to_next)):
                if not 0 <= j < count:
                    out += [0.0] * 3
                    continue
                line = ref
                if line is None:
                    line = g[line_at(b + 1 if basis is up else b - 1)] if 0 <= (b + 1 if basis is up else b - 1) < count else None
                beyond = (j > b) if basis is up else (j < b)
                if line is None or (ref is None and beyond):
                    out += [0.0] * 3
                    continue
                scale_j = ratio(line, j, basis) / ratio(line, b, basis)
                out += [scale_j * (basis[j] @ s) for s in spread]
            return out

        u = sent(up, b + 2, lambda t: 2 * t - 1)
        d = sent(down, b - 2, lambda t: 2 * t + 2)
        own = []
        for line in (prev, nxt):
            own += [*line[2 * b : 2 * b + 2], *via(line, b - 1, to_prev), *via(line, b + 1, to_next)]
        rows.append([*up[b], *u, *down[b], *d, *own, *received(prev, b, count, up, down), *received(nxt, b, count, up, down)])
    return np.asarray(rows).astype(np.float32), inverse, alpha, beta


def pivots(length, coefficient):
    inverse_pivot = np.ones(length)
    for i in range(1, length):
        inverse_pivot[i] = 1.0 / (1.0 + coefficient * coefficient * inverse_pivot[i - 1])
    return inverse_pivot


def halves(matrix):
    high = matrix.astype(ml_dtypes.bfloat16)
    low = (matrix - high.astype(np.float64)).astype(ml_dtypes.bfloat16)
    return high.astype(np.float64), low.astype(np.float64)


def lane_tables(lx, lz, ly, coefficient, xinv, xa, xb, ya, yb):
    inverse = local_inverse(ly, coefficient)
    dy = np.zeros((ly, ly))
    for j in range(ly):
        for k, w in WEIGHTS.items():
            if 0 <= j + k < ly:
                dy[j + k, j] = w
    sel = np.zeros((5, 32, ly))
    ed = np.zeros((5, 32, ly))
    wy = np.zeros((5, 16, ly))
    ey = np.zeros((5, 16, ly))
    for f in range(5):
        for k in range(3):
            sel[f, 3 * f + k, k] = 1.0
            sel[f, 16 + 3 * f + k, ly - 3 + k] = 1.0
            for row, position in ((3 * f + k, k - 3), (16 + 3 * f + k, ly + k)):
                for step, w in WEIGHTS.items():
                    if 0 <= position - step < ly:
                        ed[f, row, position - step] = w
        wy[f, f], wy[f, 8 + f] = inverse[0], inverse[-1]
        ey[f, f], ey[f, 8 + f] = ya, yb
    profiles = [xa, xb, *(xinv[:, r] for r in (*range(3), *range(lx - 3, lx)))]
    spread = np.zeros((8, lz, lx, lz))
    for n, profile in enumerate(profiles):
        for z in range(lz):
            spread[n, z, :, z] = profile
    spread = spread.reshape(8 * lz, lx * lz)
    parts = {"dy": np.concatenate([dy, dy])}
    high, low = halves(inverse.T)
    parts["inverse"] = np.concatenate([high, high, low])
    for f in range(5):
        parts["sel", f] = sel[f]
        parts["ed", f] = np.concatenate([ed[f], ed[f]])
        high, low = halves(wy[f])
        parts["wy", f] = np.concatenate([high, low])
        high, low = halves(ey[f])
        parts["ey", f] = np.concatenate([high, high, low])
    high, low = halves(spread)
    spread = np.concatenate([high, high, low])
    for c in range(lx * lz // ly):
        parts["spread", c] = spread[:, c * ly : c * ly + ly]
    places, at = {}, 0
    for name, part in parts.items():
        places[name] = (at, at + part.shape[0])
        at += part.shape[0]
    return np.concatenate(list(parts.values()), 0).astype(ml_dtypes.bfloat16), places


NN, NT, TN = ((1,), (0,)), ((1,), (1,)), ((0,), (0,))


def dot(a, b, dims):
    return lax.dot_general(a, b, (dims, ((), ())), preferred_element_type=jnp.float32)


def split(v):
    high = v.astype(jnp.bfloat16)
    low = (v - high.astype(jnp.float32)).astype(jnp.bfloat16)
    return high, low


def two(v, axis):
    return jnp.concatenate(split(v), axis)


def three(v, axis):
    high, low = split(v)
    return jnp.concatenate([high, low, high], axis)


def difference(at):
    total = None
    for k, w in ((1, 45.0), (2, -9.0), (3, 1.0)):
        a, b = at(k), at(-k)
        if a is None and b is None:
            continue
        pair = -b if a is None else (a if b is None else a - b)
        pair = pair if w == 1.0 else w * pair
        total = pair if total is None else total + pair
    return total


def around(v):
    n = v.shape[0]
    return difference(lambda k: pltpu.roll(v, (-k) % n, 0))


def kernel(
    nx, ny, lx, lz, ly, coefficient, ipiv, xinv, alpha, beta, places,
    mass_in, mom_in, energy_in, tab_in, xt_in, yt_in, out, low_out, high_out,
    mass, mom, energy, tab, xt, yt,
    xp, pt, ept, mt, gy, pre, fxp, fy, dz, inc, ysend, yhalo, ysend2, yhalo2,
    xs, xl, xr, ws, wr, vs, vr, cs, cr,
    hss, hrs, xss, xrs, wss, wrs, vss, vrs, css, crs, lsem, near_sem,
):
    ix, iy = lax.axis_index("gx"), lax.axis_index("gy")
    rows = lx * lz
    scale = -2.0 * coefficient * STEP

    barrier = pltpu.get_barrier_semaphore()


    def both_sides(semaphore, distance):
        above, below = ix + distance < nx, ix - distance >= 0

        @pl.when(above)
        def _():
            pl.semaphore_signal(semaphore, inc=1, device_id={"gx": ix + distance}, device_id_type=MESH)

        @pl.when(below)
        def _():
            pl.semaphore_signal(semaphore, inc=1, device_id={"gx": ix - distance}, device_id_type=MESH)

        return above.astype(jnp.int32) + below.astype(jnp.int32)

    expected = both_sides(barrier, 1)
    stages = []

    def tell():
        distance = 1 << len(stages)
        if distance < nx - 1:
            stages.append(both_sides(near_sem.at[len(stages)], distance))

    def hear():
        if stages and stages[-1] is not None:
            pl.semaphore_wait(near_sem.at[len(stages) - 1], stages[-1])

    for d in range(1, ny):
        pl.semaphore_signal(barrier, inc=1, device_id={"gy": lax.rem(iy + d, ny)}, device_id_type=MESH)

    loads = [
        pltpu.make_async_copy(a, b, lsem.at[k])
        for k, (a, b) in enumerate((
            (mass_in, mass), (mom_in, mom), (energy_in, energy), (tab_in, tab), (xt_in, xt), (yt_in, yt)))
    ]
    for load in loads:
        load.start()

    def part(*name):
        low, high = places[name if len(name) > 1 else name[0]]
        return tab[low:high]

    def flat(v):
        return v.reshape(rows, ly)

    def block(v):
        return v.reshape(lx, lz, ly)

    def primitives(i, _=None):
        at = pl.ds(i, lz, stride=lx)
        rho, e = mass[at, :], energy[at, :]
        m = [mom[k, at, :] for k in range(3)]
        inv = 1.0 / rho
        u = [a * inv for a in m]
        p = 0.4 * (e - 0.5 * (m[0] * u[0] + m[1] * u[1] + m[2] * u[2]))
        for k in range(3):
            xp[k, i + 3] = u[k]
            mt[k, i] = m[k]
        xp[3, i + 3] = p * inv
        pt[i] = p
        ept[i] = e + p
        return 0

    for load in loads[:3]:
        load.wait()
    edges = sorted({*range(3), *range(lx - 3, lx)})
    for i in edges:
        primitives(i)

    zeros3 = jnp.zeros((3, lz, ly), jnp.float32)

    def x_halo(ref, fields, base):
        to_next = pltpu.make_async_remote_copy(
            ref.at[:, pl.ds(lx, 3)], ref.at[:, pl.ds(0, 3)], hss.at[base], hrs.at[base],
            device_id={"gx": ix + 1}, device_id_type=MESH)
        to_prev = pltpu.make_async_remote_copy(
            ref.at[:, pl.ds(3, 3)], ref.at[:, pl.ds(lx + 3, 3)], hss.at[base + 1], hrs.at[base + 1],
            device_id={"gx": ix - 1}, device_id_type=MESH)

        @pl.when(ix == 0)
        def _():
            for f in range(fields):
                ref[f, 0:3] = zeros3

        @pl.when(ix == nx - 1)
        def _():
            for f in range(fields):
                ref[f, lx + 3 : lx + 6] = zeros3

        return to_next, to_prev, ix, nx

    def y_halo(source, ref, base):
        to_next = pltpu.make_async_remote_copy(
            source.at[pl.ds(16, 16)], ref.at[pl.ds(0, 16)], hss.at[base], hrs.at[base],
            device_id={"gy": iy + 1}, device_id_type=MESH)
        to_prev = pltpu.make_async_remote_copy(
            source.at[pl.ds(0, 16)], ref.at[pl.ds(16, 16)], hss.at[base + 1], hrs.at[base + 1],
            device_id={"gy": iy - 1}, device_id_type=MESH)

        @pl.when(iy == 0)
        def _():
            ref[0:16] = jnp.zeros((16, rows), jnp.float32)

        @pl.when(iy == ny - 1)
        def _():
            ref[16:32] = jnp.zeros((16, rows), jnp.float32)

        return to_next, to_prev, iy, ny

    def start(halo):
        to_next, to_prev, here, count = halo
        pl.when(here < count - 1)(to_next.start)
        pl.when(here > 0)(to_prev.start)

    def arrive(halo):
        to_next, to_prev, here, count = halo
        pl.when(here > 0)(to_next.wait_recv)
        pl.when(here < count - 1)(to_prev.wait_recv)

    def sent(halo):
        to_next, to_prev, here, count = halo
        pl.when(here < count - 1)(to_next.wait_send)
        pl.when(here > 0)(to_prev.wait_send)

    def packed(field, fields):
        total = None
        for f in range(fields):
            s = part("sel", f)
            p = dot(jnp.concatenate([s, s], 1), two(flat(field(f)), 1), NT)
            total = p if total is None else total + p
        return total

    def pairs(count):
        return [tuple(range(f, min(f + 2, count))) for f in range(0, count, 2)]

    h1x = x_halo(xp, 4, 0)
    pl.semaphore_wait(barrier, expected + (ny - 1))
    start(h1x)
    tell()
    lax.fori_loop(3, lx - 3, primitives, 0, unroll=2)
    for load in loads[3:]:
        load.wait()
    ysend[...] = packed(lambda f: xp[f, 3 : lx + 3], 4)
    h1y = y_halo(ysend, yhalo, 2)
    start(h1y)
    for f in range(4):
        gy[f] = block(dot(two(flat(xp[f, 3 : lx + 3]), 1), part("dy"), NN))

    def gradients(i):
        x = [difference(lambda k: xp[f, i + 3 + k]) for f in range(4)]
        z = [around(xp[f, i + 3]) for f in range(4)]
        return x[0], z[2], x[1], x[2] + z[0], z[1], x[3], z[3]

    def ahead(i, _=None):
        for n, g in enumerate(gradients(i)):
            pre[n, i] = g
        return 0

    lax.fori_loop(3, lx - 3, ahead, 0, unroll=2)
    arrive(h1y)
    hear()
    tell()
    outer = two(yhalo[...], 0)
    for fs in pairs(4):
        near = dot(outer, jnp.concatenate([part("ed", f) for f in fs], 1), TN)
        for n, f in enumerate(fs):
            gy[f] += block(near[:, n * ly : n * ly + ly])

    def fluxes(i, g=None):
        u = [xp[k, i + 3] for k in range(3)]
        m = [mt[k, i] for k in range(3)]
        p, ep = pt[i], ept[i]
        xx, zz, xv, xz, zv, xt, zt = g or [pre[n, i] for n in range(7)]
        yu, yy, yw, yt = [gy[f, i] for f in range(4)]
        dilation = (2.0 / 3.0 * viscosity * STEP) * (xx + yy + zz)
        twice, once = 2.0 * viscosity * STEP, viscosity * STEP
        stress = {
            (0, 0): twice * xx - dilation, (1, 1): twice * yy - dilation, (2, 2): twice * zz - dilation,
            (0, 1): once * (xv + yu), (0, 2): once * xz, (1, 2): once * (yw + zv),
        }
        for a, b in ((0, 1), (0, 2), (1, 2)):
            stress[b, a] = stress[a, b]
        heat = (xt, yt, zt)
        for j in range(3):
            entries = [m[j]]
            for k in range(3):
                e = m[k] * u[j] - stress[k, j]
                entries.append(e + p if k == j else e)
            power = u[0] * stress[0, j] + u[1] * stress[1, j] + u[2] * stress[2, j]
            entries.append(ep * u[j] - power - (conductivity * STEP) * heat[j])
            for c in range(5):
                if j == 0:
                    fxp[c, i + 3] = entries[c]
                elif j == 1:
                    fy[c, i] = entries[c]
                else:
                    dz[c, i] = around(entries[c])
        return 0

    def inner(i, _):
        return fluxes(i)

    lax.fori_loop(3, lx - 3, inner, 0)
    arrive(h1x)
    hear()
    tell()
    for i in edges:
        fluxes(i, gradients(i))
    h2x = x_halo(fxp, 5, 4)
    start(h2x)
    ysend2[...] = packed(lambda f: fy[f], 5)
    h2y = y_halo(ysend2, yhalo2, 6)
    start(h2y)

    for f in range(5):
        inner = block(dot(two(flat(fy[f]), 1), part("dy"), NN))
        for i in range(lx):
            s = difference(lambda k: fxp[f, i + 3 + k] if 0 <= i + k < lx else None)
            inc[f, i] = s + dz[f, i] + inner[i]

    width = 32 + 2 * (nx - 1)

    def xtab(k):
        return xt[ix * width + k]

    arrive(h2y)
    outer = two(yhalo2[...], 0)
    for fs in pairs(5):
        near = dot(outer, jnp.concatenate([part("ed", f) for f in fs], 1), TN)
        for n, f in enumerate(fs):
            add = block(near[:, n * ly : n * ly + ly])
            y0 = yl = None
            for i in range(lx):
                s = inc[f, i] + add[i]
                inc[f, i] = s
                a, b = float(scale * xinv[0, i]) * s, float(scale * xinv[-1, i]) * s
                y0, yl = (a, b) if i == 0 else (y0 + a, yl + b)
            first = [fxp[f, 3 + m] for m in range(3)]
            last = [fxp[f, lx + 2 - m] for m in range(3)]
            for w, base in ((0, 0), (1, 8)):
                near_side, far_side = (first, last) if w == 0 else (last, first)
                near_at, far_at = (2, 5) if w == 0 else (5, 2)
                total = xtab(base) * y0 + xtab(base + 1) * yl
                for m in range(3):
                    total += xtab(base + near_at + m) * near_side[m]
                xs[2 + w, f] = total
                for m in range(3):
                    total += xtab(base + far_at + m) * far_side[m]
                xs[w, f] = total
    solved = dot(three(xs[...].reshape(20 * lz, ly), 1), part("inverse"), NN)
    xl[...] = solved.reshape(4, 5, lz, ly)
    hear()
    while (1 << len(stages)) < nx - 1:
        tell()
        hear()
    ywidth = 8 + 2 * (ny - 1)

    def ytab(k):
        return yt[iy * ywidth + k]

    def ends(data, f):
        w = part("wy", f)
        return dot(jnp.concatenate([w[0:16], w[0:16], w[16:32]], 1), data, NT)

    def y_exchange(values, source, target, send, receive):
        y0, yl = values[0:8], values[8:16]
        source[0] = ytab(0) * y0 + ytab(1) * yl
        source[1] = ytab(2) * y0 + ytab(3) * yl
        started = []
        for d in range(1, ny):
            which = jnp.where(iy + d >= ny, 1, 0).astype(jnp.int32)
            copy = pltpu.make_async_remote_copy(
                source.at[which], target.at[d - 1], send.at[d - 1], receive.at[d - 1],
                device_id={"gy": lax.rem(iy + d, ny)}, device_id_type=MESH)
            copy.start()
            started.append(copy)

        def finish():
            before = ytab(4) * y0 + ytab(5) * yl
            after = ytab(6) * y0 + ytab(7) * yl
            for d in range(1, ny):
                started[d - 1].wait_recv()
                r = target[d - 1]
                before += ytab(7 + d) * r
                after += ytab(7 + ny - 1 + d) * r
            return before, after

        return started, finish

    values = None
    spare = jnp.zeros((ly - 4 * lz, ly), jnp.float32)
    for f in range(5):
        p = ends(three(jnp.concatenate([xs[:, f].reshape(4 * lz, ly), spare], 0), 1), f)
        values = p if values is None else values + p
    lane = lax.broadcasted_iota(jnp.int32, (8, ly), 1)

    def shifted(v, by):
        return pltpu.roll(v, by % ly, 1) if by % ly else v

    def side_by_side(first, second):
        return jnp.where(lane < lz, first, jnp.where(lane < 2 * lz, second, 0.0))

    for w in range(4):
        cs[w] = side_by_side(shifted(values[0:8], -lz * w), shifted(values[8:16], lz - lz * w))
    ccopies = []
    for d in range(1, nx):
        above, below = (2 if d == 1 else 0), (3 if d == nx - 1 else 1)
        which = jnp.where(ix + d >= nx, below, above).astype(jnp.int32)
        copy = pltpu.make_async_remote_copy(
            cs.at[which], cr.at[d - 1], css.at[d - 1], crs.at[d - 1],
            device_id={"gx": lax.rem(ix + d, nx)}, device_id_type=MESH)
        copy.start()
        ccopies.append(copy)
    copies = []
    for d in range(1, nx):
        above, below = (2 if d == 1 else 0), (3 if d == nx - 1 else 1)
        which = jnp.where(ix + d >= nx, below, above).astype(jnp.int32)
        copy = pltpu.make_async_remote_copy(
            xl.at[which], xr.at[d - 1], xss.at[d - 1], xrs.at[d - 1],
            device_id={"gx": lax.rem(ix + d, nx)}, device_id_type=MESH)
        copy.start()
        copies.append(copy)

    for fs in pairs(5):
        v = {}
        for i in range(lx):
            for f in fs:
                s = float(scale * ipiv[i]) * inc[f, i]
                v[f] = s if i == 0 else s + float(coefficient * ipiv[i]) * v[f]
                inc[f, i] = v[f]
        for i in range(lx - 2, -1, -1):
            for f in fs:
                v[f] = inc[f, i] - float(coefficient * ipiv[i]) * v[f]
                inc[f, i] = v[f]
    local = None
    for f in range(5):
        data = three(flat(inc[f]), 1)
        p = ends(data, f)
        local = p if local is None else local + p
        fy[f] = block(dot(data, part("inverse"), NN))
    arrive(h2x)
    halo_rows = [*range(3), *range(lx - 3, lx)]
    own_x = []
    small = None
    for f in range(5):
        added = []
        for i in halo_rows:
            added.append(scale * difference(lambda k: None if 0 <= i + k < lx else fxp[f, i + 3 + k]))
        y0, yl = inc[f, 0], inc[f, lx - 1]
        for i, v in zip(halo_rows, added):
            y0 += float(xinv[0, i]) * v
            yl += float(xinv[-1, i]) * v
        terms = [y0, yl] + [fxp[f, 3 + m] for m in range(3)] + [fxp[f, lx + 2 - m] for m in range(3)]
        sides = []
        for base in (16, 24):
            total = xtab(base) * terms[0]
            for k in range(1, 8):
                total += xtab(base + k) * terms[k]
            sides.append(total)
        own_x.append(jnp.concatenate(sides + added, 0))
        p = ends(three(own_x[f], 1), f)
        small = p if small is None else small + p
    spread = jnp.concatenate([part("spread", c) for c in range(rows // ly)], 1)
    ycopies, finish = y_exchange(local + dot(three(small, 1), spread, NN), ws, wr, wss, wrs)
    solved = dot(three(jnp.concatenate(own_x, 0), 1), part("inverse"), NN)
    for f in range(5):
        pieces = [solved[lz * (8 * f + n) : lz * (8 * f + n + 1)] for n in range(8)]
        for i in range(lx):
            at = pl.ds(i, lz, stride=lx)
            state = mass[at, :] if f == 0 else (energy[at, :] if f == 4 else mt[f - 1, i])
            total = state + fy[f, i]
            weights = [alpha[i], beta[i], *(xinv[i, r] for r in halo_rows)]
            for w, v in zip(weights, pieces):
                total += float(w) * v
            inc[f, i] = total
    for copy in ccopies:
        copy.wait_recv()
    sums = []
    for at in (31, 31 + nx - 1):
        total = xtab(at + 1) * cr[0]
        for d in range(2, nx):
            total += xtab(at + d) * cr[d - 1]
        sums.append(total)
    values = [side_by_side(sums[0], shifted(sums[1], lz)), side_by_side(shifted(sums[0], -lz), sums[1])]
    vcopies, finish_sides = y_exchange(jnp.concatenate(values, 0), vs, vr, vss, vrs)
    outside = three(jnp.concatenate(finish(), 0), 0)
    for fs in pairs(5):
        far = dot(outside, jnp.concatenate([part("ey", f) for f in fs], 1), TN)
        for n, f in enumerate(fs):
            total = block(far[:, n * ly : n * ly + ly])
            for i in range(lx):
                out[f, pl.ds(i, lz, stride=lx), :] = inc[f, i] + total[i]

    outside = three(jnp.concatenate(finish_sides(), 0), 0)
    for copy in copies:
        copy.wait_recv()
    for fs in pairs(5):
        far = dot(outside, jnp.concatenate([part("ey", f) for f in fs], 1), TN)
        for n, f in enumerate(fs):
            low = far[0:lz, n * ly : n * ly + ly]
            high = far[lz : 2 * lz, n * ly : n * ly + ly]
            for d in range(1, nx):
                r = xr[d - 1, f]
                low += xtab(31 + d) * r
                high += xtab(31 + nx - 1 + d) * r
            low_out[f], high_out[f] = low, high

    for halo in (h1x, h1y, h2x, h2y):
        sent(halo)
    for copy in copies + ccopies + vcopies + ycopies:
        copy.wait_send()


def body(nx, ny, mass, mom, energy):
    lz, lx, ly = mass.shape
    rows = lx * lz
    coefficient = float(max(lx, ly))
    xtab, xinv, xa, xb = coupled_tables(lx, nx, coefficient, -2.0 * coefficient * STEP)
    ytab, ya, yb = reduced_tables(ly, ny, coefficient)
    tab, places = lane_tables(lx, lz, ly, coefficient, xinv, xa, xb, ya, yb)
    vm = pl.BlockSpec(memory_space=pltpu.VMEM)
    hbm = pl.BlockSpec(memory_space=pltpu.HBM)
    f32 = jnp.float32
    block = (lx, lz, ly)
    dma = pltpu.SemaphoreType.DMA
    operands = (
        mass.reshape(rows, ly), mom.reshape(3, rows, ly), energy.reshape(rows, ly),
        jnp.asarray(tab), jnp.asarray(xtab.reshape(-1)), jnp.asarray(ytab.reshape(-1)),
    )
    result, low, high = pl.pallas_call(
        functools.partial(
            kernel, nx, ny, lx, lz, ly, coefficient, pivots(lx, coefficient), xinv, xa, xb, places),
        out_shape=(jax.ShapeDtypeStruct((5, rows, ly), f32), *[jax.ShapeDtypeStruct((5, lz, ly), f32)] * 2),
        in_specs=[hbm] * 6,
        out_specs=(vm, vm, vm),
        scratch_shapes=[
            pltpu.VMEM((rows, ly), f32),
            pltpu.VMEM((3, rows, ly), f32),
            pltpu.VMEM((rows, ly), f32),
            pltpu.VMEM(tab.shape, jnp.bfloat16),
            pltpu.SMEM((xtab.size,), f32),
            pltpu.SMEM((ytab.size,), f32),
            pltpu.VMEM((4, lx + 6, lz, ly), f32),
            pltpu.VMEM(block, f32),
            pltpu.VMEM(block, f32),
            pltpu.VMEM((3, *block), f32),
            pltpu.VMEM((4, *block), f32),
            pltpu.VMEM((7, *block), f32),
            pltpu.VMEM((5, lx + 6, lz, ly), f32),
            pltpu.VMEM((5, *block), f32),
            pltpu.VMEM((5, *block), f32),
            pltpu.VMEM((5, *block), f32),
            pltpu.VMEM((32, rows), f32),
            pltpu.VMEM((32, rows), f32),
            pltpu.VMEM((32, rows), f32),
            pltpu.VMEM((32, rows), f32),
            pltpu.VMEM((4, 5, lz, ly), f32),
            pltpu.VMEM((4, 5, lz, ly), f32),
            pltpu.VMEM((nx - 1, 5, lz, ly), f32),
            pltpu.VMEM((2, 8, rows), f32),
            pltpu.VMEM((ny - 1, 8, rows), f32),
            pltpu.VMEM((2, 8, ly), f32),
            pltpu.VMEM((ny - 1, 8, ly), f32),
            pltpu.VMEM((4, 8, ly), f32),
            pltpu.VMEM((nx - 1, 8, ly), f32),
            dma((8,)),
            dma((8,)),
            dma((nx - 1,)),
            dma((nx - 1,)),
            dma((ny - 1,)),
            dma((ny - 1,)),
            dma((ny - 1,)),
            dma((ny - 1,)),
            dma((nx - 1,)),
            dma((nx - 1,)),
            dma((6,)),
            pltpu.SemaphoreType.REGULAR((max(1, (nx - 1).bit_length()),)),
        ],
        compiler_params=pltpu.CompilerParams(
            collective_id=0, has_side_effects=True, vmem_limit_bytes=40 * 2**20
        ),
    )(*[pltpu.with_memory_space_constraint(a, pltpu.HBM) for a in operands])
    low, high = low[:, :, None], high[:, :, None]
    along = [jnp.broadcast_to(jnp.asarray(w.astype(np.float32))[:, None], (lx, ly)) for w in (xa, xb)]
    return result.reshape(5, lz, lx, ly) + along[0] * low + along[1] * high


def solution(mesh):
    return jax.shard_map(
        functools.partial(body, mesh.shape["gx"], mesh.shape["gy"]),
        mesh=mesh,
        in_specs=(P(None, "gx", "gy"), P(None, None, "gx", "gy"), P(None, "gx", "gy")),
        out_specs=P(None, None, "gx", "gy"),
        check_vma=False,
    )
```

```python
import functools
import jax
import jax.numpy as jnp
import ml_dtypes
import numpy as np
from jax import lax
from jax.experimental import pallas as pl
from jax.experimental.pallas import tpu as pltpu
from jax.sharding import PartitionSpec as P

viscosity = 0.1
conductivity = 0.1 * 1.4 / (0.4 * 0.72)
MESH = pl.DeviceIdType.MESH
WEIGHTS = {1: 45.0, -1: -45.0, 2: -9.0, -2: 9.0, 3: 1.0, -3: -1.0}
STEP = 1.0 / 60.0


def local_inverse(length, coefficient):
    matrix = np.eye(length)
    matrix += coefficient * (np.eye(length, k=1) - np.eye(length, k=-1))
    return np.linalg.inv(matrix)


def reduced_system(length, count, coefficient):
    inverse = local_inverse(length, coefficient)
    alpha, beta = coefficient * inverse[:, 0], -coefficient * inverse[:, -1]
    system = np.eye(2 * count)
    for b in range(count):
        for row, at in ((2 * b, 0), (2 * b + 1, length - 1)):
            if b > 0:
                system[row, 2 * b - 1] -= alpha[at]
            if b < count - 1:
                system[row, 2 * b + 2] -= beta[at]
    g = np.linalg.inv(system)
    up = [g[2 * b + 1, 2 * b : 2 * b + 2] for b in range(count)]
    down = [g[2 * b, 2 * b : 2 * b + 2] for b in range(count)]
    return inverse, alpha, beta, g, up, down


def outside_lines(g, b, count):
    prev = g[2 * b - 1] if b > 0 else np.zeros(2 * count)
    nxt = g[2 * b + 2] if b < count - 1 else np.zeros(2 * count)
    return prev, nxt


def received(line, b, count, up, down):
    weights = []
    for d in range(1, count):
        other = (b - d) % count
        basis = up[other] if other < b else down[other]
        weights.append(line[2 * other : 2 * other + 2] @ basis / (basis @ basis))
    return weights


def reduced_tables(length, count, coefficient):
    inverse, alpha, beta, g, up, down = reduced_system(length, count, coefficient)
    rows = []
    for b in range(count):
        prev, nxt = outside_lines(g, b, count)
        own = [*prev[2 * b : 2 * b + 2], *nxt[2 * b : 2 * b + 2]]
        rows.append([*up[b], *down[b], *own, *received(prev, b, count, up, down), *received(nxt, b, count, up, down)])
    return np.asarray(rows).astype(np.float32), alpha, beta


def coupled_tables(length, count, coefficient, scale):
    inverse, alpha, beta, g, up, down = reduced_system(length, count, coefficient)
    ends = [0, length - 1]
    to_next, to_prev = [], []
    for m in range(3):
        n, p = np.zeros(2), np.zeros(2)
        for r in range(3 - m):
            n += scale * inverse[ends, r] * WEIGHTS[-(r + 1 + m)]
            p += scale * inverse[ends, length - 1 - r] * WEIGHTS[r + 1 + m]
        to_next.append(n)
        to_prev.append(p)
    rows = []
    for b in range(count):
        prev, nxt = outside_lines(g, b, count)

        def via(line, j, spread):
            if not 0 <= j < count:
                return [0.0] * 3
            return [line[2 * j : 2 * j + 2] @ s for s in spread]

        def ratio(line, j, basis):
            return line[2 * j : 2 * j + 2] @ basis[j] / (basis[j] @ basis[j])

        def sent(basis, t, line_at):
            if not 0 <= t < count:
                low, high = 0.0, 0.0
                ref = None
            else:
                ref = g[line_at(t)]
            out = []
            for j, spread in ((b - 1, to_prev), (b + 1, to_next)):
                if not 0 <= j < count:
                    out += [0.0] * 3
                    continue
                line = ref
                if line is None:
                    line = g[line_at(b + 1 if basis is up else b - 1)] if 0 <= (b + 1 if basis is up else b - 1) < count else None
                beyond = (j > b) if basis is up else (j < b)
                if line is None or (ref is None and beyond):
                    out += [0.0] * 3
                    continue
                scale_j = ratio(line, j, basis) / ratio(line, b, basis)
                out += [scale_j * (basis[j] @ s) for s in spread]
            return out

        u = sent(up, b + 2, lambda t: 2 * t - 1)
        d = sent(down, b - 2, lambda t: 2 * t + 2)
        own = []
        for line in (prev, nxt):
            own += [*line[2 * b : 2 * b + 2], *via(line, b - 1, to_prev), *via(line, b + 1, to_next)]
        rows.append([*up[b], *u, *down[b], *d, *own, *received(prev, b, count, up, down), *received(nxt, b, count, up, down)])
    return np.asarray(rows).astype(np.float32), inverse, alpha, beta


def pivots(length, coefficient):
    inverse_pivot = np.ones(length)
    for i in range(1, length):
        inverse_pivot[i] = 1.0 / (1.0 + coefficient * coefficient * inverse_pivot[i - 1])
    return inverse_pivot


def halves(matrix):
    high = matrix.astype(ml_dtypes.bfloat16)
    low = (matrix - high.astype(np.float64)).astype(ml_dtypes.bfloat16)
    return high.astype(np.float64), low.astype(np.float64)


def lane_tables(lx, lz, ly, coefficient, xinv, xa, xb, ya, yb):
    inverse = local_inverse(ly, coefficient)
    dy = np.zeros((ly, ly))
    for j in range(ly):
        for k, w in WEIGHTS.items():
            if 0 <= j + k < ly:
                dy[j + k, j] = w
    sel = np.zeros((5, 32, ly))
    ed = np.zeros((5, 32, ly))
    wy = np.zeros((5, 16, ly))
    ey = np.zeros((5, 16, ly))
    for f in range(5):
        for k in range(3):
            sel[f, 3 * f + k, k] = 1.0
            sel[f, 16 + 3 * f + k, ly - 3 + k] = 1.0
            for row, position in ((3 * f + k, k - 3), (16 + 3 * f + k, ly + k)):
                for step, w in WEIGHTS.items():
                    if 0 <= position - step < ly:
                        ed[f, row, position - step] = w
        wy[f, f], wy[f, 8 + f] = inverse[0], inverse[-1]
        ey[f, f], ey[f, 8 + f] = ya, yb
    profiles = [xa, xb, *(xinv[:, r] for r in (*range(3), *range(lx - 3, lx)))]
    spread = np.zeros((8, lz, lx, lz))
    for n, profile in enumerate(profiles):
        for z in range(lz):
            spread[n, z, :, z] = profile
    spread = spread.reshape(8 * lz, lx * lz)
    parts = {"dy": np.concatenate([dy, dy])}
    high, low = halves(inverse.T)
    parts["inverse"] = np.concatenate([high, high, low])
    for f in range(5):
        parts["sel", f] = sel[f]
        parts["ed", f] = np.concatenate([ed[f], ed[f]])
        high, low = halves(wy[f])
        parts["wy", f] = np.concatenate([high, low])
        high, low = halves(ey[f])
        parts["ey", f] = np.concatenate([high, high, low])
    high, low = halves(spread)
    spread = np.concatenate([high, high, low])
    for c in range(lx * lz // ly):
        parts["spread", c] = spread[:, c * ly : c * ly + ly]
    places, at = {}, 0
    for name, part in parts.items():
        places[name] = (at, at + part.shape[0])
        at += part.shape[0]
    return np.concatenate(list(parts.values()), 0).astype(ml_dtypes.bfloat16), places


NN, NT, TN = ((1,), (0,)), ((1,), (1,)), ((0,), (0,))


def dot(a, b, dims):
    return lax.dot_general(a, b, (dims, ((), ())), preferred_element_type=jnp.float32)


def split(v):
    high = v.astype(jnp.bfloat16)
    low = (v - high.astype(jnp.float32)).astype(jnp.bfloat16)
    return high, low


def two(v, axis):
    return jnp.concatenate(split(v), axis)


def three(v, axis):
    high, low = split(v)
    return jnp.concatenate([high, low, high], axis)


def difference(at):
    total = None
    for k, w in ((1, 45.0), (2, -9.0), (3, 1.0)):
        a, b = at(k), at(-k)
        if a is None and b is None:
            continue
        pair = -b if a is None else (a if b is None else a - b)
        pair = pair if w == 1.0 else w * pair
        total = pair if total is None else total + pair
    return total


def around(v):
    n = v.shape[0]
    return difference(lambda k: pltpu.roll(v, (-k) % n, 0))


def kernel(
    nx, ny, lx, lz, ly, coefficient, ipiv, xinv, alpha, beta, places,
    mass_in, mom_in, energy_in, tab_in, xt_in, yt_in, out, low_out, high_out,
    mass, energy, tab, xt, yt,
    xp, pt, ept, mt, gy, pre, fxp, fy, dz, inc, ysend, yhalo, ysend2, yhalo2,
    xs, xl, xr, ws, wr, vs, vr, cs, cr,
    hss, hrs, xss, xrs, wss, wrs, vss, vrs, css, crs, lsem, near_sem,
):
    ix, iy = lax.axis_index("gx"), lax.axis_index("gy")
    rows = lx * lz
    scale = -2.0 * coefficient * STEP

    def group(rows_in, k):
        for i in rows_in:
            pltpu.make_async_copy(mass_in.at[:, i], mass.at[i], lsem.at[k]).start()
            pltpu.make_async_copy(mom_in.at[:, :, i], mt.at[:, i], lsem.at[k + 1]).start()
            pltpu.make_async_copy(energy_in.at[:, i], energy.at[i], lsem.at[k + 2]).start()
        whole = pl.ds(0, len(rows_in))

        def wait():
            for n, ref in enumerate((mass.at[whole], mt.at[:, whole], energy.at[whole])):
                pltpu.make_async_copy(ref, ref, lsem.at[k + n]).wait()

        return wait

    edges = sorted({*range(3), *range(lx - 3, lx)})
    edges_loaded = group(edges, 3)
    inner_loaded = group(range(3, lx - 3), 6)
    loads = [
        pltpu.make_async_copy(a, b, lsem.at[k])
        for k, (a, b) in enumerate(((tab_in, tab), (xt_in, xt), (yt_in, yt)))
    ]
    for load in loads:
        load.start()

    barrier = pltpu.get_barrier_semaphore()


    def both_sides(semaphore, distance):
        above, below = ix + distance < nx, ix - distance >= 0

        @pl.when(above)
        def _():
            pl.semaphore_signal(semaphore, inc=1, device_id={"gx": ix + distance}, device_id_type=MESH)

        @pl.when(below)
        def _():
            pl.semaphore_signal(semaphore, inc=1, device_id={"gx": ix - distance}, device_id_type=MESH)

        return above.astype(jnp.int32) + below.astype(jnp.int32)

    expected = both_sides(barrier, 1)
    stages = []

    def tell():
        distance = 1 << len(stages)
        if distance < nx - 1:
            stages.append(both_sides(near_sem.at[len(stages)], distance))

    def hear():
        if stages and stages[-1] is not None:
            pl.semaphore_wait(near_sem.at[len(stages) - 1], stages[-1])

    for d in range(1, ny):
        pl.semaphore_signal(barrier, inc=1, device_id={"gy": lax.rem(iy + d, ny)}, device_id_type=MESH)

    def part(*name):
        low, high = places[name if len(name) > 1 else name[0]]
        return tab[low:high]

    def flat(v):
        return v.reshape(rows, ly)

    def block(v):
        return v.reshape(lx, lz, ly)

    def primitives(i, _=None):
        rho, e = mass[i], energy[i]
        m = [mt[k, i] for k in range(3)]
        inv = 1.0 / rho
        u = [a * inv for a in m]
        p = 0.4 * (e - 0.5 * (m[0] * u[0] + m[1] * u[1] + m[2] * u[2]))
        for k in range(3):
            xp[k, i + 3] = u[k]
        xp[3, i + 3] = p * inv
        pt[i] = p
        ept[i] = e + p
        return 0

    edges_loaded()
    for i in edges:
        primitives(i)

    zeros3 = jnp.zeros((3, lz, ly), jnp.float32)

    def x_halo(ref, fields, base):
        to_next = pltpu.make_async_remote_copy(
            ref.at[:, pl.ds(lx, 3)], ref.at[:, pl.ds(0, 3)], hss.at[base], hrs.at[base],
            device_id={"gx": ix + 1}, device_id_type=MESH)
        to_prev = pltpu.make_async_remote_copy(
            ref.at[:, pl.ds(3, 3)], ref.at[:, pl.ds(lx + 3, 3)], hss.at[base + 1], hrs.at[base + 1],
            device_id={"gx": ix - 1}, device_id_type=MESH)

        @pl.when(ix == 0)
        def _():
            for f in range(fields):
                ref[f, 0:3] = zeros3

        @pl.when(ix == nx - 1)
        def _():
            for f in range(fields):
                ref[f, lx + 3 : lx + 6] = zeros3

        return to_next, to_prev, ix, nx

    def y_halo(source, ref, base):
        to_next = pltpu.make_async_remote_copy(
            source.at[pl.ds(16, 16)], ref.at[pl.ds(0, 16)], hss.at[base], hrs.at[base],
            device_id={"gy": iy + 1}, device_id_type=MESH)
        to_prev = pltpu.make_async_remote_copy(
            source.at[pl.ds(0, 16)], ref.at[pl.ds(16, 16)], hss.at[base + 1], hrs.at[base + 1],
            device_id={"gy": iy - 1}, device_id_type=MESH)

        @pl.when(iy == 0)
        def _():
            ref[0:16] = jnp.zeros((16, rows), jnp.float32)

        @pl.when(iy == ny - 1)
        def _():
            ref[16:32] = jnp.zeros((16, rows), jnp.float32)

        return to_next, to_prev, iy, ny

    def start(halo):
        to_next, to_prev, here, count = halo
        pl.when(here < count - 1)(to_next.start)
        pl.when(here > 0)(to_prev.start)

    def arrive(halo):
        to_next, to_prev, here, count = halo
        pl.when(here > 0)(to_next.wait_recv)
        pl.when(here < count - 1)(to_prev.wait_recv)

    def sent(halo):
        to_next, to_prev, here, count = halo
        pl.when(here < count - 1)(to_next.wait_send)
        pl.when(here > 0)(to_prev.wait_send)

    def packed(field, fields):
        total = None
        for f in range(fields):
            s = part("sel", f)
            p = dot(jnp.concatenate([s, s], 1), two(flat(field(f)), 1), NT)
            total = p if total is None else total + p
        return total

    def pairs(count):
        return [tuple(range(f, min(f + 2, count))) for f in range(0, count, 2)]

    h1x = x_halo(xp, 4, 0)
    pl.semaphore_wait(barrier, expected + (ny - 1))
    start(h1x)
    tell()
    inner_loaded()
    lax.fori_loop(3, lx - 3, primitives, 0, unroll=2)
    for load in loads:
        load.wait()
    ysend[...] = packed(lambda f: xp[f, 3 : lx + 3], 4)
    h1y = y_halo(ysend, yhalo, 2)
    start(h1y)
    for f in range(4):
        gy[f] = block(dot(two(flat(xp[f, 3 : lx + 3]), 1), part("dy"), NN))

    def gradients(i):
        x = [difference(lambda k: xp[f, i + 3 + k]) for f in range(4)]
        z = [around(xp[f, i + 3]) for f in range(4)]
        return x[0], z[2], x[1], x[2] + z[0], z[1], x[3], z[3]

    def ahead(i, _=None):
        for n, g in enumerate(gradients(i)):
            pre[n, i] = g
        return 0

    lax.fori_loop(3, lx - 3, ahead, 0, unroll=2)
    arrive(h1y)
    hear()
    tell()
    outer = two(yhalo[...], 0)
    for fs in pairs(4):
        near = dot(outer, jnp.concatenate([part("ed", f) for f in fs], 1), TN)
        for n, f in enumerate(fs):
            gy[f] += block(near[:, n * ly : n * ly + ly])

    def fluxes(i, g=None):
        u = [xp[k, i + 3] for k in range(3)]
        m = [mt[k, i] for k in range(3)]
        p, ep = pt[i], ept[i]
        xx, zz, xv, xz, zv, xt, zt = g or [pre[n, i] for n in range(7)]
        yu, yy, yw, yt = [gy[f, i] for f in range(4)]
        dilation = (2.0 / 3.0 * viscosity * STEP) * (xx + yy + zz)
        twice, once = 2.0 * viscosity * STEP, viscosity * STEP
        stress = {
            (0, 0): twice * xx - dilation, (1, 1): twice * yy - dilation, (2, 2): twice * zz - dilation,
            (0, 1): once * (xv + yu), (0, 2): once * xz, (1, 2): once * (yw + zv),
        }
        for a, b in ((0, 1), (0, 2), (1, 2)):
            stress[b, a] = stress[a, b]
        heat = (xt, yt, zt)
        for j in range(3):
            entries = [m[j]]
            for k in range(3):
                e = m[k] * u[j] - stress[k, j]
                entries.append(e + p if k == j else e)
            power = u[0] * stress[0, j] + u[1] * stress[1, j] + u[2] * stress[2, j]
            entries.append(ep * u[j] - power - (conductivity * STEP) * heat[j])
            for c in range(5):
                if j == 0:
                    fxp[c, i + 3] = entries[c]
                elif j == 1:
                    fy[c, i] = entries[c]
                else:
                    dz[c, i] = around(entries[c])
        return 0

    def inner(i, _):
        return fluxes(i)

    lax.fori_loop(3, lx - 3, inner, 0)
    arrive(h1x)
    hear()
    tell()
    h2x = x_halo(fxp, 5, 4)
    for i in range(3):
        fluxes(i, gradients(i))
    pl.when(ix > 0)(h2x[1].start)
    for i in range(lx - 3, lx):
        fluxes(i, gradients(i))
    pl.when(ix < nx - 1)(h2x[0].start)
    ysend2[...] = packed(lambda f: fy[f], 5)
    h2y = y_halo(ysend2, yhalo2, 6)
    start(h2y)

    for f in range(5):
        inner = block(dot(two(flat(fy[f]), 1), part("dy"), NN))
        for i in range(lx):
            s = difference(lambda k: fxp[f, i + 3 + k] if 0 <= i + k < lx else None)
            inc[f, i] = s + dz[f, i] + inner[i]

    width = 32 + 2 * (nx - 1)

    def xtab(k):
        return xt[ix * width + k]

    arrive(h2y)
    outer = two(yhalo2[...], 0)
    for fs in pairs(5):
        near = dot(outer, jnp.concatenate([part("ed", f) for f in fs], 1), TN)
        for n, f in enumerate(fs):
            add = block(near[:, n * ly : n * ly + ly])
            y0 = yl = None
            for i in range(lx):
                s = inc[f, i] + add[i]
                inc[f, i] = s
                a, b = float(scale * xinv[0, i]) * s, float(scale * xinv[-1, i]) * s
                y0, yl = (a, b) if i == 0 else (y0 + a, yl + b)
            first = [fxp[f, 3 + m] for m in range(3)]
            last = [fxp[f, lx + 2 - m] for m in range(3)]
            for w, base in ((0, 0), (1, 8)):
                near_side, far_side = (first, last) if w == 0 else (last, first)
                near_at, far_at = (2, 5) if w == 0 else (5, 2)
                total = xtab(base) * y0 + xtab(base + 1) * yl
                for m in range(3):
                    total += xtab(base + near_at + m) * near_side[m]
                xs[2 + w, f] = total
                for m in range(3):
                    total += xtab(base + far_at + m) * far_side[m]
                xs[w, f] = total
    solved = dot(three(xs[...].reshape(20 * lz, ly), 1), part("inverse"), NN)
    xl[...] = solved.reshape(4, 5, lz, ly)
    hear()
    while (1 << len(stages)) < nx - 1:
        tell()
        hear()
    ywidth = 8 + 2 * (ny - 1)

    def ytab(k):
        return yt[iy * ywidth + k]

    def ends(data, f):
        w = part("wy", f)
        return dot(jnp.concatenate([w[0:16], w[0:16], w[16:32]], 1), data, NT)

    def y_exchange(values, source, target, send, receive):
        y0, yl = values[0:8], values[8:16]
        source[0] = ytab(0) * y0 + ytab(1) * yl
        source[1] = ytab(2) * y0 + ytab(3) * yl
        started = []
        for d in range(1, ny):
            which = jnp.where(iy + d >= ny, 1, 0).astype(jnp.int32)
            copy = pltpu.make_async_remote_copy(
                source.at[which], target.at[d - 1], send.at[d - 1], receive.at[d - 1],
                device_id={"gy": lax.rem(iy + d, ny)}, device_id_type=MESH)
            copy.start()
            started.append(copy)

        def finish():
            before = ytab(4) * y0 + ytab(5) * yl
            after = ytab(6) * y0 + ytab(7) * yl
            for d in range(1, ny):
                started[d - 1].wait_recv()
                r = target[d - 1]
                before += ytab(7 + d) * r
                after += ytab(7 + ny - 1 + d) * r
            return before, after

        return started, finish

    values = None
    spare = jnp.zeros((ly - 4 * lz, ly), jnp.float32)
    for f in range(5):
        p = ends(three(jnp.concatenate([xs[:, f].reshape(4 * lz, ly), spare], 0), 1), f)
        values = p if values is None else values + p
    lane = lax.broadcasted_iota(jnp.int32, (8, ly), 1)

    def shifted(v, by):
        return pltpu.roll(v, by % ly, 1) if by % ly else v

    def side_by_side(first, second):
        return jnp.where(lane < lz, first, jnp.where(lane < 2 * lz, second, 0.0))

    for w in range(4):
        cs[w] = side_by_side(shifted(values[0:8], -lz * w), shifted(values[8:16], lz - lz * w))
    ccopies = []
    for d in range(1, nx):
        above, below = (2 if d == 1 else 0), (3 if d == nx - 1 else 1)
        which = jnp.where(ix + d >= nx, below, above).astype(jnp.int32)
        copy = pltpu.make_async_remote_copy(
            cs.at[which], cr.at[d - 1], css.at[d - 1], crs.at[d - 1],
            device_id={"gx": lax.rem(ix + d, nx)}, device_id_type=MESH)
        copy.start()
        ccopies.append(copy)
    copies = []
    for d in range(1, nx):
        above, below = (2 if d == 1 else 0), (3 if d == nx - 1 else 1)
        which = jnp.where(ix + d >= nx, below, above).astype(jnp.int32)
        copy = pltpu.make_async_remote_copy(
            xl.at[which], xr.at[d - 1], xss.at[d - 1], xrs.at[d - 1],
            device_id={"gx": lax.rem(ix + d, nx)}, device_id_type=MESH)
        copy.start()
        copies.append(copy)

    for fs in pairs(5):
        v = {}
        for i in range(lx):
            for f in fs:
                s = float(scale * ipiv[i]) * inc[f, i]
                v[f] = s if i == 0 else s + float(coefficient * ipiv[i]) * v[f]
                inc[f, i] = v[f]
        for i in range(lx - 2, -1, -1):
            for f in fs:
                v[f] = inc[f, i] - float(coefficient * ipiv[i]) * v[f]
                inc[f, i] = v[f]
    local = None
    for f in range(5):
        data = three(flat(inc[f]), 1)
        p = ends(data, f)
        local = p if local is None else local + p
        fy[f] = block(dot(data, part("inverse"), NN))
    arrive(h2x)
    halo_rows = [*range(3), *range(lx - 3, lx)]
    own_x = []
    small = None
    for f in range(5):
        added = []
        for i in halo_rows:
            added.append(scale * difference(lambda k: None if 0 <= i + k < lx else fxp[f, i + 3 + k]))
        y0, yl = inc[f, 0], inc[f, lx - 1]
        for i, v in zip(halo_rows, added):
            y0 += float(xinv[0, i]) * v
            yl += float(xinv[-1, i]) * v
        terms = [y0, yl] + [fxp[f, 3 + m] for m in range(3)] + [fxp[f, lx + 2 - m] for m in range(3)]
        sides = []
        for base in (16, 24):
            total = xtab(base) * terms[0]
            for k in range(1, 8):
                total += xtab(base + k) * terms[k]
            sides.append(total)
        own_x.append(jnp.concatenate(sides + added, 0))
        p = ends(three(own_x[f], 1), f)
        small = p if small is None else small + p
    spread = jnp.concatenate([part("spread", c) for c in range(rows // ly)], 1)
    ycopies, finish = y_exchange(local + dot(three(small, 1), spread, NN), ws, wr, wss, wrs)
    solved = dot(three(jnp.concatenate(own_x, 0), 1), part("inverse"), NN)
    for f in range(5):
        pieces = [solved[lz * (8 * f + n) : lz * (8 * f + n + 1)] for n in range(8)]
        for i in range(lx):
            state = mass[i] if f == 0 else (energy[i] if f == 4 else mt[f - 1, i])
            total = state + fy[f, i]
            weights = [alpha[i], beta[i], *(xinv[i, r] for r in halo_rows)]
            for w, v in zip(weights, pieces):
                total += float(w) * v
            inc[f, i] = total
    for copy in ccopies:
        copy.wait_recv()
    sums = []
    for at in (31, 31 + nx - 1):
        total = xtab(at + 1) * cr[0]
        for d in range(2, nx):
            total += xtab(at + d) * cr[d - 1]
        sums.append(total)
    values = [side_by_side(sums[0], shifted(sums[1], lz)), side_by_side(shifted(sums[0], -lz), sums[1])]
    vcopies, finish_sides = y_exchange(jnp.concatenate(values, 0), vs, vr, vss, vrs)
    outside = three(jnp.concatenate(finish(), 0), 0)
    for fs in pairs(5):
        far = dot(outside, jnp.concatenate([part("ey", f) for f in fs], 1), TN)
        for n, f in enumerate(fs):
            total = block(far[:, n * ly : n * ly + ly])
            for i in range(lx):
                out[f, pl.ds(i, lz, stride=lx), :] = inc[f, i] + total[i]

    outside = three(jnp.concatenate(finish_sides(), 0), 0)
    for copy in copies:
        copy.wait_recv()
    for fs in pairs(5):
        far = dot(outside, jnp.concatenate([part("ey", f) for f in fs], 1), TN)
        for n, f in enumerate(fs):
            low = far[0:lz, n * ly : n * ly + ly]
            high = far[lz : 2 * lz, n * ly : n * ly + ly]
            for d in range(1, nx):
                r = xr[d - 1, f]
                low += xtab(31 + d) * r
                high += xtab(31 + nx - 1 + d) * r
            low_out[f], high_out[f] = low, high

    for halo in (h1x, h1y, h2x, h2y):
        sent(halo)
    for copy in copies + ccopies + vcopies + ycopies:
        copy.wait_send()


def body(nx, ny, mass, mom, energy):
    lz, lx, ly = mass.shape
    rows = lx * lz
    coefficient = float(max(lx, ly))
    xtab, xinv, xa, xb = coupled_tables(lx, nx, coefficient, -2.0 * coefficient * STEP)
    ytab, ya, yb = reduced_tables(ly, ny, coefficient)
    tab, places = lane_tables(lx, lz, ly, coefficient, xinv, xa, xb, ya, yb)
    vm = pl.BlockSpec(memory_space=pltpu.VMEM)
    hbm = pl.BlockSpec(memory_space=pltpu.HBM)
    f32 = jnp.float32
    block = (lx, lz, ly)
    dma = pltpu.SemaphoreType.DMA
    operands = (
        mass, mom, energy,
        jnp.asarray(tab), jnp.asarray(xtab.reshape(-1)), jnp.asarray(ytab.reshape(-1)),
    )
    result, low, high = pl.pallas_call(
        functools.partial(
            kernel, nx, ny, lx, lz, ly, coefficient, pivots(lx, coefficient), xinv, xa, xb, places),
        out_shape=(jax.ShapeDtypeStruct((5, rows, ly), f32), *[jax.ShapeDtypeStruct((5, lz, ly), f32)] * 2),
        in_specs=[hbm] * 6,
        out_specs=(vm, vm, vm),
        scratch_shapes=[
            pltpu.VMEM(block, f32),
            pltpu.VMEM(block, f32),
            pltpu.VMEM(tab.shape, jnp.bfloat16),
            pltpu.SMEM((xtab.size,), f32),
            pltpu.SMEM((ytab.size,), f32),
            pltpu.VMEM((4, lx + 6, lz, ly), f32),
            pltpu.VMEM(block, f32),
            pltpu.VMEM(block, f32),
            pltpu.VMEM((3, *block), f32),
            pltpu.VMEM((4, *block), f32),
            pltpu.VMEM((7, *block), f32),
            pltpu.VMEM((5, lx + 6, lz, ly), f32),
            pltpu.VMEM((5, *block), f32),
            pltpu.VMEM((5, *block), f32),
            pltpu.VMEM((5, *block), f32),
            pltpu.VMEM((32, rows), f32),
            pltpu.VMEM((32, rows), f32),
            pltpu.VMEM((32, rows), f32),
            pltpu.VMEM((32, rows), f32),
            pltpu.VMEM((4, 5, lz, ly), f32),
            pltpu.VMEM((4, 5, lz, ly), f32),
            pltpu.VMEM((nx - 1, 5, lz, ly), f32),
            pltpu.VMEM((2, 8, rows), f32),
            pltpu.VMEM((ny - 1, 8, rows), f32),
            pltpu.VMEM((2, 8, ly), f32),
            pltpu.VMEM((ny - 1, 8, ly), f32),
            pltpu.VMEM((4, 8, ly), f32),
            pltpu.VMEM((nx - 1, 8, ly), f32),
            dma((8,)),
            dma((8,)),
            dma((nx - 1,)),
            dma((nx - 1,)),
            dma((ny - 1,)),
            dma((ny - 1,)),
            dma((ny - 1,)),
            dma((ny - 1,)),
            dma((nx - 1,)),
            dma((nx - 1,)),
            dma((9,)),
            pltpu.SemaphoreType.REGULAR((max(1, (nx - 1).bit_length()),)),
        ],
        compiler_params=pltpu.CompilerParams(
            collective_id=0, has_side_effects=True, vmem_limit_bytes=40 * 2**20
        ),
    )(*[pltpu.with_memory_space_constraint(a, pltpu.HBM) for a in operands])
    low, high = low[:, :, None], high[:, :, None]
    along = [jnp.broadcast_to(jnp.asarray(w.astype(np.float32))[:, None], (lx, ly)) for w in (xa, xb)]
    return result.reshape(5, lz, lx, ly) + along[0] * low + along[1] * high


def solution(mesh):
    return jax.shard_map(
        functools.partial(body, mesh.shape["gx"], mesh.shape["gy"]),
        mesh=mesh,
        in_specs=(P(None, "gx", "gy"), P(None, None, "gx", "gy"), P(None, "gx", "gy")),
        out_specs=P(None, None, "gx", "gy"),
        check_vma=False,
    )
```

```python
import functools
import jax
import jax.numpy as jnp
import ml_dtypes
import numpy as np
from jax import lax
from jax.experimental import pallas as pl
from jax.experimental.pallas import tpu as pltpu
from jax.sharding import PartitionSpec as P

viscosity = 0.1
conductivity = 0.1 * 1.4 / (0.4 * 0.72)
MESH = pl.DeviceIdType.MESH
WEIGHTS = {1: 45.0, -1: -45.0, 2: -9.0, -2: 9.0, 3: 1.0, -3: -1.0}
STEP = 1.0 / 60.0


def local_inverse(length, coefficient):
    matrix = np.eye(length)
    matrix += coefficient * (np.eye(length, k=1) - np.eye(length, k=-1))
    return np.linalg.inv(matrix)


def reduced_system(length, count, coefficient):
    inverse = local_inverse(length, coefficient)
    alpha, beta = coefficient * inverse[:, 0], -coefficient * inverse[:, -1]
    system = np.eye(2 * count)
    for b in range(count):
        for row, at in ((2 * b, 0), (2 * b + 1, length - 1)):
            if b > 0:
                system[row, 2 * b - 1] -= alpha[at]
            if b < count - 1:
                system[row, 2 * b + 2] -= beta[at]
    g = np.linalg.inv(system)
    up = [g[2 * b + 1, 2 * b : 2 * b + 2] for b in range(count)]
    down = [g[2 * b, 2 * b : 2 * b + 2] for b in range(count)]
    return inverse, alpha, beta, g, up, down


def outside_lines(g, b, count):
    prev = g[2 * b - 1] if b > 0 else np.zeros(2 * count)
    nxt = g[2 * b + 2] if b < count - 1 else np.zeros(2 * count)
    return prev, nxt


def received(line, b, count, up, down):
    weights = []
    for d in range(1, count):
        other = (b - d) % count
        basis = up[other] if other < b else down[other]
        weights.append(line[2 * other : 2 * other + 2] @ basis / (basis @ basis))
    return weights


def reduced_tables(length, count, coefficient):
    inverse, alpha, beta, g, up, down = reduced_system(length, count, coefficient)
    rows = []
    for b in range(count):
        prev, nxt = outside_lines(g, b, count)
        own = [*prev[2 * b : 2 * b + 2], *nxt[2 * b : 2 * b + 2]]
        rows.append([*up[b], *down[b], *own, *received(prev, b, count, up, down), *received(nxt, b, count, up, down)])
    return np.asarray(rows).astype(np.float32), alpha, beta


def coupled_tables(length, count, coefficient, scale):
    inverse, alpha, beta, g, up, down = reduced_system(length, count, coefficient)
    ends = [0, length - 1]
    to_next, to_prev = [], []
    for m in range(3):
        n, p = np.zeros(2), np.zeros(2)
        for r in range(3 - m):
            n += scale * inverse[ends, r] * WEIGHTS[-(r + 1 + m)]
            p += scale * inverse[ends, length - 1 - r] * WEIGHTS[r + 1 + m]
        to_next.append(n)
        to_prev.append(p)
    rows = []
    for b in range(count):
        prev, nxt = outside_lines(g, b, count)

        def via(line, j, spread):
            if not 0 <= j < count:
                return [0.0] * 3
            return [line[2 * j : 2 * j + 2] @ s for s in spread]

        def ratio(line, j, basis):
            return line[2 * j : 2 * j + 2] @ basis[j] / (basis[j] @ basis[j])

        def sent(basis, t, line_at):
            if not 0 <= t < count:
                low, high = 0.0, 0.0
                ref = None
            else:
                ref = g[line_at(t)]
            out = []
            for j, spread in ((b - 1, to_prev), (b + 1, to_next)):
                if not 0 <= j < count:
                    out += [0.0] * 3
                    continue
                line = ref
                if line is None:
                    line = g[line_at(b + 1 if basis is up else b - 1)] if 0 <= (b + 1 if basis is up else b - 1) < count else None
                beyond = (j > b) if basis is up else (j < b)
                if line is None or (ref is None and beyond):
                    out += [0.0] * 3
                    continue
                scale_j = ratio(line, j, basis) / ratio(line, b, basis)
                out += [scale_j * (basis[j] @ s) for s in spread]
            return out

        u = sent(up, b + 2, lambda t: 2 * t - 1)
        d = sent(down, b - 2, lambda t: 2 * t + 2)
        own = []
        for line in (prev, nxt):
            own += [*line[2 * b : 2 * b + 2], *via(line, b - 1, to_prev), *via(line, b + 1, to_next)]
        rows.append([*up[b], *u, *down[b], *d, *own, *received(prev, b, count, up, down), *received(nxt, b, count, up, down)])
    return np.asarray(rows).astype(np.float32), inverse, alpha, beta


def pivots(length, coefficient):
    inverse_pivot = np.ones(length)
    for i in range(1, length):
        inverse_pivot[i] = 1.0 / (1.0 + coefficient * coefficient * inverse_pivot[i - 1])
    return inverse_pivot


def halves(matrix):
    high = matrix.astype(ml_dtypes.bfloat16)
    low = (matrix - high.astype(np.float64)).astype(ml_dtypes.bfloat16)
    return high.astype(np.float64), low.astype(np.float64)


def lane_tables(lx, lz, ly, coefficient, xinv, xa, xb, ya, yb):
    inverse = local_inverse(ly, coefficient)
    dy = np.zeros((ly, ly))
    for j in range(ly):
        for k, w in WEIGHTS.items():
            if 0 <= j + k < ly:
                dy[j + k, j] = w
    sel = np.zeros((5, 32, ly))
    ed = np.zeros((5, 32, ly))
    wy = np.zeros((5, 16, ly))
    ey = np.zeros((5, 16, ly))
    for f in range(5):
        for k in range(3):
            sel[f, 3 * f + k, k] = 1.0
            sel[f, 16 + 3 * f + k, ly - 3 + k] = 1.0
            for row, position in ((3 * f + k, k - 3), (16 + 3 * f + k, ly + k)):
                for step, w in WEIGHTS.items():
                    if 0 <= position - step < ly:
                        ed[f, row, position - step] = w
        wy[f, f], wy[f, 8 + f] = inverse[0], inverse[-1]
        ey[f, f], ey[f, 8 + f] = ya, yb
    profiles = [xa, xb, *(xinv[:, r] for r in (*range(3), *range(lx - 3, lx)))]
    spread = np.zeros((8, lz, lx, lz))
    for n, profile in enumerate(profiles):
        for z in range(lz):
            spread[n, z, :, z] = profile
    spread = spread.reshape(8 * lz, lx * lz)
    parts = {"dy": np.concatenate([dy, dy])}
    high, low = halves(inverse.T)
    parts["inverse"] = np.concatenate([high, high, low])
    for f in range(5):
        parts["sel", f] = sel[f]
        parts["ed", f] = np.concatenate([ed[f], ed[f]])
        high, low = halves(wy[f])
        parts["wy", f] = np.concatenate([high, low])
        high, low = halves(ey[f])
        parts["ey", f] = np.concatenate([high, high, low])
    high, low = halves(spread)
    spread = np.concatenate([high, high, low])
    for c in range(lx * lz // ly):
        parts["spread", c] = spread[:, c * ly : c * ly + ly]
    places, at = {}, 0
    for name, part in parts.items():
        places[name] = (at, at + part.shape[0])
        at += part.shape[0]
    return np.concatenate(list(parts.values()), 0).astype(ml_dtypes.bfloat16), places


NN, NT, TN = ((1,), (0,)), ((1,), (1,)), ((0,), (0,))


def dot(a, b, dims):
    return lax.dot_general(a, b, (dims, ((), ())), preferred_element_type=jnp.float32)


def split(v):
    high = v.astype(jnp.bfloat16)
    low = (v - high.astype(jnp.float32)).astype(jnp.bfloat16)
    return high, low


def two(v, axis):
    return jnp.concatenate(split(v), axis)


def three(v, axis):
    high, low = split(v)
    return jnp.concatenate([high, low, high], axis)


def difference(at):
    total = None
    for k, w in ((1, 45.0), (2, -9.0), (3, 1.0)):
        a, b = at(k), at(-k)
        if a is None and b is None:
            continue
        pair = -b if a is None else (a if b is None else a - b)
        pair = pair if w == 1.0 else w * pair
        total = pair if total is None else total + pair
    return total


def around(v):
    n = v.shape[0]
    return difference(lambda k: pltpu.roll(v, (-k) % n, 0))


def kernel(
    nx, ny, lx, lz, ly, coefficient, ipiv, xinv, alpha, beta, places,
    mass_in, mom_in, energy_in, tab_in, xt_in, yt_in, out, low_out, high_out,
    mass, energy, tab, xt, yt,
    xp, pt, ept, mt, gy, pre, fxp, fy, dz, inc, ysend, yhalo, ysend2, yhalo2,
    xs, xl, xr, ws, wr, vs, vr, cs, cr,
    hss, hrs, xss, xrs, wss, wrs, vss, vrs, css, crs, lsem, near_sem,
):
    ix, iy = lax.axis_index("gx"), lax.axis_index("gy")
    rows = lx * lz
    scale = -2.0 * coefficient * STEP

    def group(rows_in, k):
        for i in rows_in:
            pltpu.make_async_copy(mass_in.at[:, i], mass.at[i], lsem.at[k]).start()
            pltpu.make_async_copy(mom_in.at[:, :, i], mt.at[:, i], lsem.at[k + 1]).start()
            pltpu.make_async_copy(energy_in.at[:, i], energy.at[i], lsem.at[k + 2]).start()
        whole = pl.ds(0, len(rows_in))

        def wait():
            for n, ref in enumerate((mass.at[whole], mt.at[:, whole], energy.at[whole])):
                pltpu.make_async_copy(ref, ref, lsem.at[k + n]).wait()

        return wait

    edges = sorted({*range(3), *range(lx - 3, lx)})
    edges_loaded = group(edges, 3)
    inner_loaded = group(range(3, lx - 3), 6)
    loads = [
        pltpu.make_async_copy(a, b, lsem.at[k])
        for k, (a, b) in enumerate(((tab_in, tab), (xt_in, xt), (yt_in, yt)))
    ]
    for load in loads:
        load.start()

    barrier = pltpu.get_barrier_semaphore()


    def both_sides(semaphore, distance):
        above, below = ix + distance < nx, ix - distance >= 0

        @pl.when(above)
        def _():
            pl.semaphore_signal(semaphore, inc=1, device_id={"gx": ix + distance}, device_id_type=MESH)

        @pl.when(below)
        def _():
            pl.semaphore_signal(semaphore, inc=1, device_id={"gx": ix - distance}, device_id_type=MESH)

        return above.astype(jnp.int32) + below.astype(jnp.int32)

    expected = both_sides(barrier, 1)
    stages = []

    def tell():
        distance = 1 << len(stages)
        if distance < nx - 1:
            stages.append(both_sides(near_sem.at[len(stages)], distance))

    def hear():
        if stages and stages[-1] is not None:
            pl.semaphore_wait(near_sem.at[len(stages) - 1], stages[-1])

    for d in range(1, ny):
        pl.semaphore_signal(barrier, inc=1, device_id={"gy": lax.rem(iy + d, ny)}, device_id_type=MESH)

    def part(*name):
        low, high = places[name if len(name) > 1 else name[0]]
        return tab[low:high]

    def flat(v):
        return v.reshape(rows, ly)

    def block(v):
        return v.reshape(lx, lz, ly)

    def primitives(i, _=None):
        rho, e = mass[i], energy[i]
        m = [mt[k, i] for k in range(3)]
        inv = 1.0 / rho
        u = [a * inv for a in m]
        p = 0.4 * (e - 0.5 * (m[0] * u[0] + m[1] * u[1] + m[2] * u[2]))
        for k in range(3):
            xp[k, i + 3] = u[k]
        xp[3, i + 3] = p * inv
        pt[i] = p
        ept[i] = e + p
        return 0

    edges_loaded()
    for i in edges:
        primitives(i)

    zeros3 = jnp.zeros((3, lz, ly), jnp.float32)

    def x_halo(ref, fields, base):
        to_next = pltpu.make_async_remote_copy(
            ref.at[:, pl.ds(lx, 3)], ref.at[:, pl.ds(0, 3)], hss.at[base], hrs.at[base],
            device_id={"gx": ix + 1}, device_id_type=MESH)
        to_prev = pltpu.make_async_remote_copy(
            ref.at[:, pl.ds(3, 3)], ref.at[:, pl.ds(lx + 3, 3)], hss.at[base + 1], hrs.at[base + 1],
            device_id={"gx": ix - 1}, device_id_type=MESH)

        @pl.when(ix == 0)
        def _():
            for f in range(fields):
                ref[f, 0:3] = zeros3

        @pl.when(ix == nx - 1)
        def _():
            for f in range(fields):
                ref[f, lx + 3 : lx + 6] = zeros3

        return to_next, to_prev, ix, nx

    def y_halo(source, ref, base):
        to_next = pltpu.make_async_remote_copy(
            source.at[pl.ds(16, 16)], ref.at[pl.ds(0, 16)], hss.at[base], hrs.at[base],
            device_id={"gy": iy + 1}, device_id_type=MESH)
        to_prev = pltpu.make_async_remote_copy(
            source.at[pl.ds(0, 16)], ref.at[pl.ds(16, 16)], hss.at[base + 1], hrs.at[base + 1],
            device_id={"gy": iy - 1}, device_id_type=MESH)

        @pl.when(iy == 0)
        def _():
            ref[0:16] = jnp.zeros((16, rows), jnp.float32)

        @pl.when(iy == ny - 1)
        def _():
            ref[16:32] = jnp.zeros((16, rows), jnp.float32)

        return to_next, to_prev, iy, ny

    def start(halo):
        to_next, to_prev, here, count = halo
        pl.when(here < count - 1)(to_next.start)
        pl.when(here > 0)(to_prev.start)

    def arrive(halo):
        to_next, to_prev, here, count = halo
        pl.when(here > 0)(to_next.wait_recv)
        pl.when(here < count - 1)(to_prev.wait_recv)

    def sent(halo):
        to_next, to_prev, here, count = halo
        pl.when(here < count - 1)(to_next.wait_send)
        pl.when(here > 0)(to_prev.wait_send)

    def packed(field, fields):
        total = None
        for f in range(fields):
            s = part("sel", f)
            p = dot(jnp.concatenate([s, s], 1), two(flat(field(f)), 1), NT)
            total = p if total is None else total + p
        return total

    def pairs(count):
        return [tuple(range(f, min(f + 2, count))) for f in range(0, count, 2)]

    h1x = x_halo(xp, 4, 0)
    pl.semaphore_wait(barrier, expected + (ny - 1))
    start(h1x)
    tell()
    inner_loaded()
    lax.fori_loop(3, lx - 3, primitives, 0, unroll=2)
    for load in loads:
        load.wait()
    ysend[...] = packed(lambda f: xp[f, 3 : lx + 3], 4)
    h1y = y_halo(ysend, yhalo, 2)
    start(h1y)
    for f in range(4):
        gy[f] = block(dot(two(flat(xp[f, 3 : lx + 3]), 1), part("dy"), NN))

    def gradients(i):
        x = [difference(lambda k: xp[f, i + 3 + k]) for f in range(4)]
        z = [around(xp[f, i + 3]) for f in range(4)]
        return x[0], z[2], x[1], x[2] + z[0], z[1], x[3], z[3]

    def ahead(i, _=None):
        for n, g in enumerate(gradients(i)):
            pre[n, i] = g
        return 0

    lax.fori_loop(3, lx - 3, ahead, 0, unroll=2)
    for i in edges:
        z = [around(xp[f, i + 3]) for f in range(4)]
        for n, g in ((1, z[2]), (3, z[0]), (4, z[1]), (6, z[3])):
            pre[n, i] = g

    def at_edge(i):
        x = [difference(lambda k: xp[f, i + 3 + k]) for f in range(4)]
        return x[0], pre[1, i], x[1], x[2] + pre[3, i], pre[4, i], x[3], pre[6, i]

    arrive(h1y)
    hear()
    tell()
    outer = two(yhalo[...], 0)
    for fs in pairs(4):
        near = dot(outer, jnp.concatenate([part("ed", f) for f in fs], 1), TN)
        for n, f in enumerate(fs):
            gy[f] += block(near[:, n * ly : n * ly + ly])

    def fluxes(i, g=None):
        u = [xp[k, i + 3] for k in range(3)]
        m = [mt[k, i] for k in range(3)]
        p, ep = pt[i], ept[i]
        xx, zz, xv, xz, zv, xt, zt = g or [pre[n, i] for n in range(7)]
        yu, yy, yw, yt = [gy[f, i] for f in range(4)]
        dilation = (2.0 / 3.0 * viscosity * STEP) * (xx + yy + zz)
        twice, once = 2.0 * viscosity * STEP, viscosity * STEP
        stress = {
            (0, 0): twice * xx - dilation, (1, 1): twice * yy - dilation, (2, 2): twice * zz - dilation,
            (0, 1): once * (xv + yu), (0, 2): once * xz, (1, 2): once * (yw + zv),
        }
        for a, b in ((0, 1), (0, 2), (1, 2)):
            stress[b, a] = stress[a, b]
        heat = (xt, yt, zt)
        for j in range(3):
            entries = [m[j]]
            for k in range(3):
                e = m[k] * u[j] - stress[k, j]
                entries.append(e + p if k == j else e)
            power = u[0] * stress[0, j] + u[1] * stress[1, j] + u[2] * stress[2, j]
            entries.append(ep * u[j] - power - (conductivity * STEP) * heat[j])
            for c in range(5):
                if j == 0:
                    fxp[c, i + 3] = entries[c]
                elif j == 1:
                    fy[c, i] = entries[c]
                else:
                    dz[c, i] = around(entries[c])
        return 0

    def inner(i, _):
        return fluxes(i)

    lax.fori_loop(3, lx - 3, inner, 0, unroll=2)
    arrive(h1x)
    hear()
    tell()
    h2x = x_halo(fxp, 5, 4)
    for i in range(3):
        fluxes(i, at_edge(i))
    pl.when(ix > 0)(h2x[1].start)
    for i in range(lx - 3, lx):
        fluxes(i, at_edge(i))
    pl.when(ix < nx - 1)(h2x[0].start)
    ysend2[...] = packed(lambda f: fy[f], 5)
    h2y = y_halo(ysend2, yhalo2, 6)
    start(h2y)

    for f in range(5):
        inner = block(dot(two(flat(fy[f]), 1), part("dy"), NN))
        for i in range(lx):
            s = difference(lambda k: fxp[f, i + 3 + k] if 0 <= i + k < lx else None)
            inc[f, i] = s + dz[f, i] + inner[i]

    width = 32 + 2 * (nx - 1)

    def xtab(k):
        return xt[ix * width + k]

    arrive(h2y)
    outer = two(yhalo2[...], 0)
    for fs in pairs(5):
        near = dot(outer, jnp.concatenate([part("ed", f) for f in fs], 1), TN)
        for n, f in enumerate(fs):
            add = block(near[:, n * ly : n * ly + ly])
            y0 = yl = None
            for i in range(lx):
                s = inc[f, i] + add[i]
                inc[f, i] = s
                a, b = float(scale * xinv[0, i]) * s, float(scale * xinv[-1, i]) * s
                y0, yl = (a, b) if i == 0 else (y0 + a, yl + b)
            first = [fxp[f, 3 + m] for m in range(3)]
            last = [fxp[f, lx + 2 - m] for m in range(3)]
            for w, base in ((0, 0), (1, 8)):
                near_side, far_side = (first, last) if w == 0 else (last, first)
                near_at, far_at = (2, 5) if w == 0 else (5, 2)
                total = xtab(base) * y0 + xtab(base + 1) * yl
                for m in range(3):
                    total += xtab(base + near_at + m) * near_side[m]
                xs[2 + w, f] = total
                for m in range(3):
                    total += xtab(base + far_at + m) * far_side[m]
                xs[w, f] = total
    solved = dot(three(xs[...].reshape(20 * lz, ly), 1), part("inverse"), NN)
    xl[...] = solved.reshape(4, 5, lz, ly)
    hear()
    while (1 << len(stages)) < nx - 1:
        tell()
        hear()
    ywidth = 8 + 2 * (ny - 1)

    def ytab(k):
        return yt[iy * ywidth + k]

    def ends(data, f):
        w = part("wy", f)
        return dot(jnp.concatenate([w[0:16], w[0:16], w[16:32]], 1), data, NT)

    def y_exchange(values, source, target, send, receive):
        y0, yl = values[0:8], values[8:16]
        source[0] = ytab(0) * y0 + ytab(1) * yl
        source[1] = ytab(2) * y0 + ytab(3) * yl
        started = []
        for d in range(1, ny):
            which = jnp.where(iy + d >= ny, 1, 0).astype(jnp.int32)
            copy = pltpu.make_async_remote_copy(
                source.at[which], target.at[d - 1], send.at[d - 1], receive.at[d - 1],
                device_id={"gy": lax.rem(iy + d, ny)}, device_id_type=MESH)
            copy.start()
            started.append(copy)

        def finish():
            before = ytab(4) * y0 + ytab(5) * yl
            after = ytab(6) * y0 + ytab(7) * yl
            for d in range(1, ny):
                started[d - 1].wait_recv()
                r = target[d - 1]
                before += ytab(7 + d) * r
                after += ytab(7 + ny - 1 + d) * r
            return before, after

        return started, finish

    values = None
    spare = jnp.zeros((ly - 4 * lz, ly), jnp.float32)
    for f in range(5):
        p = ends(three(jnp.concatenate([xs[:, f].reshape(4 * lz, ly), spare], 0), 1), f)
        values = p if values is None else values + p
    lane = lax.broadcasted_iota(jnp.int32, (8, ly), 1)

    def shifted(v, by):
        return pltpu.roll(v, by % ly, 1) if by % ly else v

    def side_by_side(first, second):
        return jnp.where(lane < lz, first, jnp.where(lane < 2 * lz, second, 0.0))

    for w in range(4):
        cs[w] = side_by_side(shifted(values[0:8], -lz * w), shifted(values[8:16], lz - lz * w))
    ccopies = []
    for d in range(1, nx):
        above, below = (2 if d == 1 else 0), (3 if d == nx - 1 else 1)
        which = jnp.where(ix + d >= nx, below, above).astype(jnp.int32)
        copy = pltpu.make_async_remote_copy(
            cs.at[which], cr.at[d - 1], css.at[d - 1], crs.at[d - 1],
            device_id={"gx": lax.rem(ix + d, nx)}, device_id_type=MESH)
        copy.start()
        ccopies.append(copy)
    copies = []
    for d in range(1, nx):
        above, below = (2 if d == 1 else 0), (3 if d == nx - 1 else 1)
        which = jnp.where(ix + d >= nx, below, above).astype(jnp.int32)
        copy = pltpu.make_async_remote_copy(
            xl.at[which], xr.at[d - 1], xss.at[d - 1], xrs.at[d - 1],
            device_id={"gx": lax.rem(ix + d, nx)}, device_id_type=MESH)
        copy.start()
        copies.append(copy)

    for fs in pairs(5):
        v = {}
        for i in range(lx):
            for f in fs:
                s = float(scale * ipiv[i]) * inc[f, i]
                v[f] = s if i == 0 else s + float(coefficient * ipiv[i]) * v[f]
                inc[f, i] = v[f]
        for i in range(lx - 2, -1, -1):
            for f in fs:
                v[f] = inc[f, i] - float(coefficient * ipiv[i]) * v[f]
                inc[f, i] = v[f]
    local = None
    for f in range(5):
        data = three(flat(inc[f]), 1)
        p = ends(data, f)
        local = p if local is None else local + p
        fy[f] = block(dot(data, part("inverse"), NN))
    arrive(h2x)
    halo_rows = [*range(3), *range(lx - 3, lx)]
    own_x = []
    small = None
    for f in range(5):
        added = []
        for i in halo_rows:
            added.append(scale * difference(lambda k: None if 0 <= i + k < lx else fxp[f, i + 3 + k]))
        y0, yl = inc[f, 0], inc[f, lx - 1]
        for i, v in zip(halo_rows, added):
            y0 += float(xinv[0, i]) * v
            yl += float(xinv[-1, i]) * v
        terms = [y0, yl] + [fxp[f, 3 + m] for m in range(3)] + [fxp[f, lx + 2 - m] for m in range(3)]
        sides = []
        for base in (16, 24):
            total = xtab(base) * terms[0]
            for k in range(1, 8):
                total += xtab(base + k) * terms[k]
            sides.append(total)
        own_x.append(jnp.concatenate(sides + added, 0))
        p = ends(three(own_x[f], 1), f)
        small = p if small is None else small + p
    spread = jnp.concatenate([part("spread", c) for c in range(rows // ly)], 1)
    ycopies, finish = y_exchange(local + dot(three(small, 1), spread, NN), ws, wr, wss, wrs)
    solved = dot(three(jnp.concatenate(own_x, 0), 1), part("inverse"), NN)
    for f in range(5):
        pieces = [solved[lz * (8 * f + n) : lz * (8 * f + n + 1)] for n in range(8)]
        for i in range(lx):
            state = mass[i] if f == 0 else (energy[i] if f == 4 else mt[f - 1, i])
            total = state + fy[f, i]
            weights = [alpha[i], beta[i], *(xinv[i, r] for r in halo_rows)]
            for w, v in zip(weights, pieces):
                total += float(w) * v
            inc[f, i] = total
    for copy in ccopies:
        copy.wait_recv()
    sums = []
    for at in (31, 31 + nx - 1):
        total = xtab(at + 1) * cr[0]
        for d in range(2, nx):
            total += xtab(at + d) * cr[d - 1]
        sums.append(total)
    values = [side_by_side(sums[0], shifted(sums[1], lz)), side_by_side(shifted(sums[0], -lz), sums[1])]
    vcopies, finish_sides = y_exchange(jnp.concatenate(values, 0), vs, vr, vss, vrs)
    outside = three(jnp.concatenate(finish(), 0), 0)
    for fs in pairs(5):
        far = dot(outside, jnp.concatenate([part("ey", f) for f in fs], 1), TN)
        for n, f in enumerate(fs):
            total = block(far[:, n * ly : n * ly + ly])
            for i in range(lx):
                out[f, pl.ds(i, lz, stride=lx), :] = inc[f, i] + total[i]

    outside = three(jnp.concatenate(finish_sides(), 0), 0)
    for copy in copies:
        copy.wait_recv()
    for fs in pairs(5):
        far = dot(outside, jnp.concatenate([part("ey", f) for f in fs], 1), TN)
        for n, f in enumerate(fs):
            low = far[0:lz, n * ly : n * ly + ly]
            high = far[lz : 2 * lz, n * ly : n * ly + ly]
            for d in range(1, nx):
                r = xr[d - 1, f]
                low += xtab(31 + d) * r
                high += xtab(31 + nx - 1 + d) * r
            low_out[f], high_out[f] = low, high

    for halo in (h1x, h1y, h2x, h2y):
        sent(halo)
    for copy in copies + ccopies + vcopies + ycopies:
        copy.wait_send()


def body(nx, ny, mass, mom, energy):
    lz, lx, ly = mass.shape
    rows = lx * lz
    coefficient = float(max(lx, ly))
    xtab, xinv, xa, xb = coupled_tables(lx, nx, coefficient, -2.0 * coefficient * STEP)
    ytab, ya, yb = reduced_tables(ly, ny, coefficient)
    tab, places = lane_tables(lx, lz, ly, coefficient, xinv, xa, xb, ya, yb)
    vm = pl.BlockSpec(memory_space=pltpu.VMEM)
    hbm = pl.BlockSpec(memory_space=pltpu.HBM)
    f32 = jnp.float32
    block = (lx, lz, ly)
    dma = pltpu.SemaphoreType.DMA
    operands = (
        mass, mom, energy,
        jnp.asarray(tab), jnp.asarray(xtab.reshape(-1)), jnp.asarray(ytab.reshape(-1)),
    )
    result, low, high = pl.pallas_call(
        functools.partial(
            kernel, nx, ny, lx, lz, ly, coefficient, pivots(lx, coefficient), xinv, xa, xb, places),
        out_shape=(jax.ShapeDtypeStruct((5, rows, ly), f32), *[jax.ShapeDtypeStruct((5, lz, ly), f32)] * 2),
        in_specs=[hbm] * 6,
        out_specs=(vm, vm, vm),
        scratch_shapes=[
            pltpu.VMEM(block, f32),
            pltpu.VMEM(block, f32),
            pltpu.VMEM(tab.shape, jnp.bfloat16),
            pltpu.SMEM((xtab.size,), f32),
            pltpu.SMEM((ytab.size,), f32),
            pltpu.VMEM((4, lx + 6, lz, ly), f32),
            pltpu.VMEM(block, f32),
            pltpu.VMEM(block, f32),
            pltpu.VMEM((3, *block), f32),
            pltpu.VMEM((4, *block), f32),
            pltpu.VMEM((7, *block), f32),
            pltpu.VMEM((5, lx + 6, lz, ly), f32),
            pltpu.VMEM((5, *block), f32),
            pltpu.VMEM((5, *block), f32),
            pltpu.VMEM((5, *block), f32),
            pltpu.VMEM((32, rows), f32),
            pltpu.VMEM((32, rows), f32),
            pltpu.VMEM((32, rows), f32),
            pltpu.VMEM((32, rows), f32),
            pltpu.VMEM((4, 5, lz, ly), f32),
            pltpu.VMEM((4, 5, lz, ly), f32),
            pltpu.VMEM((nx - 1, 5, lz, ly), f32),
            pltpu.VMEM((2, 8, rows), f32),
            pltpu.VMEM((ny - 1, 8, rows), f32),
            pltpu.VMEM((2, 8, ly), f32),
            pltpu.VMEM((ny - 1, 8, ly), f32),
            pltpu.VMEM((4, 8, ly), f32),
            pltpu.VMEM((nx - 1, 8, ly), f32),
            dma((8,)),
            dma((8,)),
            dma((nx - 1,)),
            dma((nx - 1,)),
            dma((ny - 1,)),
            dma((ny - 1,)),
            dma((ny - 1,)),
            dma((ny - 1,)),
            dma((nx - 1,)),
            dma((nx - 1,)),
            dma((9,)),
            pltpu.SemaphoreType.REGULAR((max(1, (nx - 1).bit_length()),)),
        ],
        compiler_params=pltpu.CompilerParams(
            collective_id=0, has_side_effects=True, vmem_limit_bytes=40 * 2**20
        ),
    )(*[pltpu.with_memory_space_constraint(a, pltpu.HBM) for a in operands])
    low, high = low[:, :, None], high[:, :, None]
    along = [jnp.broadcast_to(jnp.asarray(w.astype(np.float32))[:, None], (lx, ly)) for w in (xa, xb)]
    return result.reshape(5, lz, lx, ly) + along[0] * low + along[1] * high


def solution(mesh):
    return jax.shard_map(
        functools.partial(body, mesh.shape["gx"], mesh.shape["gy"]),
        mesh=mesh,
        in_specs=(P(None, "gx", "gy"), P(None, None, "gx", "gy"), P(None, "gx", "gy")),
        out_specs=P(None, None, "gx", "gy"),
        check_vma=False,
    )
```

```python
import functools
import jax
import jax.numpy as jnp
import ml_dtypes
import numpy as np
from jax import lax
from jax.experimental import pallas as pl
from jax.experimental.pallas import tpu as pltpu
from jax.sharding import PartitionSpec as P

viscosity = 0.1
conductivity = 0.1 * 1.4 / (0.4 * 0.72)
MESH = pl.DeviceIdType.MESH
WEIGHTS = {1: 45.0, -1: -45.0, 2: -9.0, -2: 9.0, 3: 1.0, -3: -1.0}
STEP = 1.0 / 60.0


def local_inverse(length, coefficient):
    matrix = np.eye(length)
    matrix += coefficient * (np.eye(length, k=1) - np.eye(length, k=-1))
    return np.linalg.inv(matrix)


def reduced_system(length, count, coefficient):
    inverse = local_inverse(length, coefficient)
    alpha, beta = coefficient * inverse[:, 0], -coefficient * inverse[:, -1]
    system = np.eye(2 * count)
    for b in range(count):
        for row, at in ((2 * b, 0), (2 * b + 1, length - 1)):
            if b > 0:
                system[row, 2 * b - 1] -= alpha[at]
            if b < count - 1:
                system[row, 2 * b + 2] -= beta[at]
    g = np.linalg.inv(system)
    up = [g[2 * b + 1, 2 * b : 2 * b + 2] for b in range(count)]
    down = [g[2 * b, 2 * b : 2 * b + 2] for b in range(count)]
    return inverse, alpha, beta, g, up, down


def outside_lines(g, b, count):
    prev = g[2 * b - 1] if b > 0 else np.zeros(2 * count)
    nxt = g[2 * b + 2] if b < count - 1 else np.zeros(2 * count)
    return prev, nxt


def received(line, b, count, up, down):
    weights = []
    for d in range(1, count):
        other = (b - d) % count
        basis = up[other] if other < b else down[other]
        weights.append(line[2 * other : 2 * other + 2] @ basis / (basis @ basis))
    return weights


def reduced_tables(length, count, coefficient):
    inverse, alpha, beta, g, up, down = reduced_system(length, count, coefficient)
    rows = []
    for b in range(count):
        prev, nxt = outside_lines(g, b, count)
        own = [*prev[2 * b : 2 * b + 2], *nxt[2 * b : 2 * b + 2]]
        rows.append([*up[b], *down[b], *own, *received(prev, b, count, up, down), *received(nxt, b, count, up, down)])
    return np.asarray(rows).astype(np.float32), alpha, beta


def coupled_tables(length, count, coefficient, scale):
    inverse, alpha, beta, g, up, down = reduced_system(length, count, coefficient)
    ends = [0, length - 1]
    to_next, to_prev = [], []
    for m in range(3):
        n, p = np.zeros(2), np.zeros(2)
        for r in range(3 - m):
            n += scale * inverse[ends, r] * WEIGHTS[-(r + 1 + m)]
            p += scale * inverse[ends, length - 1 - r] * WEIGHTS[r + 1 + m]
        to_next.append(n)
        to_prev.append(p)
    rows = []
    for b in range(count):
        prev, nxt = outside_lines(g, b, count)

        def via(line, j, spread):
            if not 0 <= j < count:
                return [0.0] * 3
            return [line[2 * j : 2 * j + 2] @ s for s in spread]

        def ratio(line, j, basis):
            return line[2 * j : 2 * j + 2] @ basis[j] / (basis[j] @ basis[j])

        def sent(basis, t, line_at):
            if not 0 <= t < count:
                low, high = 0.0, 0.0
                ref = None
            else:
                ref = g[line_at(t)]
            out = []
            for j, spread in ((b - 1, to_prev), (b + 1, to_next)):
                if not 0 <= j < count:
                    out += [0.0] * 3
                    continue
                line = ref
                if line is None:
                    line = g[line_at(b + 1 if basis is up else b - 1)] if 0 <= (b + 1 if basis is up else b - 1) < count else None
                beyond = (j > b) if basis is up else (j < b)
                if line is None or (ref is None and beyond):
                    out += [0.0] * 3
                    continue
                scale_j = ratio(line, j, basis) / ratio(line, b, basis)
                out += [scale_j * (basis[j] @ s) for s in spread]
            return out

        u = sent(up, b + 2, lambda t: 2 * t - 1)
        d = sent(down, b - 2, lambda t: 2 * t + 2)
        own = []
        for line in (prev, nxt):
            own += [*line[2 * b : 2 * b + 2], *via(line, b - 1, to_prev), *via(line, b + 1, to_next)]
        rows.append([*up[b], *u, *down[b], *d, *own, *received(prev, b, count, up, down), *received(nxt, b, count, up, down)])
    return np.asarray(rows).astype(np.float32), inverse, alpha, beta


def pivots(length, coefficient):
    inverse_pivot = np.ones(length)
    for i in range(1, length):
        inverse_pivot[i] = 1.0 / (1.0 + coefficient * coefficient * inverse_pivot[i - 1])
    return inverse_pivot


def halves(matrix):
    high = matrix.astype(ml_dtypes.bfloat16)
    low = (matrix - high.astype(np.float64)).astype(ml_dtypes.bfloat16)
    return high.astype(np.float64), low.astype(np.float64)


def lane_tables(lx, lz, ly, coefficient, xinv, xa, xb, ya, yb):
    inverse = local_inverse(ly, coefficient)
    dy = np.zeros((ly, ly))
    for j in range(ly):
        for k, w in WEIGHTS.items():
            if 0 <= j + k < ly:
                dy[j + k, j] = w
    sel = np.zeros((5, 32, ly))
    ed = np.zeros((5, 32, ly))
    wy = np.zeros((5, 16, ly))
    ey = np.zeros((5, 16, ly))
    for f in range(5):
        for k in range(3):
            sel[f, 3 * f + k, k] = 1.0
            sel[f, 16 + 3 * f + k, ly - 3 + k] = 1.0
            for row, position in ((3 * f + k, k - 3), (16 + 3 * f + k, ly + k)):
                for step, w in WEIGHTS.items():
                    if 0 <= position - step < ly:
                        ed[f, row, position - step] = w
        wy[f, f], wy[f, 8 + f] = inverse[0], inverse[-1]
        ey[f, f], ey[f, 8 + f] = ya, yb
    profiles = [xa, xb, *(xinv[:, r] for r in (*range(3), *range(lx - 3, lx)))]
    spread = np.zeros((8, lz, lx, lz))
    for n, profile in enumerate(profiles):
        for z in range(lz):
            spread[n, z, :, z] = profile
    spread = spread.reshape(8 * lz, lx * lz)
    parts = {"dy": np.concatenate([dy, dy])}
    high, low = halves(inverse.T)
    parts["inverse"] = np.concatenate([high, high, low])
    for f in range(5):
        parts["sel", f] = sel[f]
        parts["ed", f] = np.concatenate([ed[f], ed[f]])
        high, low = halves(wy[f])
        parts["wy", f] = np.concatenate([high, low])
        high, low = halves(ey[f])
        parts["ey", f] = np.concatenate([high, high, low])
    high, low = halves(spread)
    spread = np.concatenate([high, high, low])
    for c in range(lx * lz // ly):
        parts["spread", c] = spread[:, c * ly : c * ly + ly]
    places, at = {}, 0
    for name, part in parts.items():
        places[name] = (at, at + part.shape[0])
        at += part.shape[0]
    return np.concatenate(list(parts.values()), 0).astype(ml_dtypes.bfloat16), places


NN, NT, TN = ((1,), (0,)), ((1,), (1,)), ((0,), (0,))


def dot(a, b, dims):
    return lax.dot_general(a, b, (dims, ((), ())), preferred_element_type=jnp.float32)


def split(v):
    high = v.astype(jnp.bfloat16)
    low = (v - high.astype(jnp.float32)).astype(jnp.bfloat16)
    return high, low


def two(v, axis):
    return jnp.concatenate(split(v), axis)


def three(v, axis):
    high, low = split(v)
    return jnp.concatenate([high, low, high], axis)


def difference(at):
    total = None
    for k, w in ((1, 45.0), (2, -9.0), (3, 1.0)):
        a, b = at(k), at(-k)
        if a is None and b is None:
            continue
        pair = -b if a is None else (a if b is None else a - b)
        pair = pair if w == 1.0 else w * pair
        total = pair if total is None else total + pair
    return total


def around(v):
    n = v.shape[0]
    return difference(lambda k: pltpu.roll(v, (-k) % n, 0))


def kernel(
    nx, ny, lx, lz, ly, coefficient, ipiv, xinv, alpha, beta, places,
    mass_in, mom_in, energy_in, tab_in, xt_in, yt_in, out, low_out, high_out,
    mass, energy, tab, xt, yt,
    xp, pt, ept, mt, gy, pre, fxp, fy, dz, inc, ysend, yhalo, ysend2, yhalo2,
    xs, xl, xr, ws, wr, vs, vr, cs, cr,
    hss, hrs, xss, xrs, wss, wrs, vss, vrs, css, crs, lsem, near_sem,
):
    ix, iy = lax.axis_index("gx"), lax.axis_index("gy")
    rows = lx * lz
    scale = -2.0 * coefficient * STEP

    def group(rows_in, k):
        for i in rows_in:
            pltpu.make_async_copy(mass_in.at[:, i], mass.at[i], lsem.at[k]).start()
            pltpu.make_async_copy(mom_in.at[:, :, i], mt.at[:, i], lsem.at[k + 1]).start()
            pltpu.make_async_copy(energy_in.at[:, i], energy.at[i], lsem.at[k + 2]).start()
        whole = pl.ds(0, len(rows_in))

        def wait():
            for n, ref in enumerate((mass.at[whole], mt.at[:, whole], energy.at[whole])):
                pltpu.make_async_copy(ref, ref, lsem.at[k + n]).wait()

        return wait

    edges = sorted({*range(3), *range(lx - 3, lx)})
    edges_loaded = group(edges, 3)
    inner_loaded = group(range(3, lx - 3), 6)
    loads = [
        pltpu.make_async_copy(a, b, lsem.at[k])
        for k, (a, b) in enumerate(((tab_in, tab), (xt_in, xt), (yt_in, yt)))
    ]
    for load in loads:
        load.start()

    barrier = pltpu.get_barrier_semaphore()


    def both_sides(semaphore, distance):
        above, below = ix + distance < nx, ix - distance >= 0

        @pl.when(above)
        def _():
            pl.semaphore_signal(semaphore, inc=1, device_id={"gx": ix + distance}, device_id_type=MESH)

        @pl.when(below)
        def _():
            pl.semaphore_signal(semaphore, inc=1, device_id={"gx": ix - distance}, device_id_type=MESH)

        return above.astype(jnp.int32) + below.astype(jnp.int32)

    expected = both_sides(barrier, 1)
    stages = []

    def tell():
        distance = 1 << len(stages)
        if distance < nx - 1:
            stages.append(both_sides(near_sem.at[len(stages)], distance))

    def hear():
        if stages and stages[-1] is not None:
            pl.semaphore_wait(near_sem.at[len(stages) - 1], stages[-1])

    for d in range(1, ny):
        pl.semaphore_signal(barrier, inc=1, device_id={"gy": lax.rem(iy + d, ny)}, device_id_type=MESH)

    def part(*name):
        low, high = places[name if len(name) > 1 else name[0]]
        return tab[low:high]

    def flat(v):
        return v.reshape(rows, ly)

    def block(v):
        return v.reshape(lx, lz, ly)

    def primitives(i, _=None):
        rho, e = mass[i], energy[i]
        m = [mt[k, i] for k in range(3)]
        inv = 1.0 / rho
        u = [a * inv for a in m]
        p = 0.4 * (e - 0.5 * (m[0] * u[0] + m[1] * u[1] + m[2] * u[2]))
        for k in range(3):
            xp[k, i + 3] = u[k]
        xp[3, i + 3] = p * inv
        pt[i] = p
        ept[i] = e + p
        return 0

    edges_loaded()
    for i in edges:
        primitives(i)

    zeros3 = jnp.zeros((3, lz, ly), jnp.float32)

    def x_halo(ref, fields, base):
        to_next = pltpu.make_async_remote_copy(
            ref.at[:, pl.ds(lx, 3)], ref.at[:, pl.ds(0, 3)], hss.at[base], hrs.at[base],
            device_id={"gx": ix + 1}, device_id_type=MESH)
        to_prev = pltpu.make_async_remote_copy(
            ref.at[:, pl.ds(3, 3)], ref.at[:, pl.ds(lx + 3, 3)], hss.at[base + 1], hrs.at[base + 1],
            device_id={"gx": ix - 1}, device_id_type=MESH)

        @pl.when(ix == 0)
        def _():
            for f in range(fields):
                ref[f, 0:3] = zeros3

        @pl.when(ix == nx - 1)
        def _():
            for f in range(fields):
                ref[f, lx + 3 : lx + 6] = zeros3

        return to_next, to_prev, ix, nx

    def y_halo(source, ref, base):
        to_next = pltpu.make_async_remote_copy(
            source.at[pl.ds(16, 16)], ref.at[pl.ds(0, 16)], hss.at[base], hrs.at[base],
            device_id={"gy": iy + 1}, device_id_type=MESH)
        to_prev = pltpu.make_async_remote_copy(
            source.at[pl.ds(0, 16)], ref.at[pl.ds(16, 16)], hss.at[base + 1], hrs.at[base + 1],
            device_id={"gy": iy - 1}, device_id_type=MESH)

        @pl.when(iy == 0)
        def _():
            ref[0:16] = jnp.zeros((16, rows), jnp.float32)

        @pl.when(iy == ny - 1)
        def _():
            ref[16:32] = jnp.zeros((16, rows), jnp.float32)

        return to_next, to_prev, iy, ny

    def start(halo):
        to_next, to_prev, here, count = halo
        pl.when(here < count - 1)(to_next.start)
        pl.when(here > 0)(to_prev.start)

    def arrive(halo):
        to_next, to_prev, here, count = halo
        pl.when(here > 0)(to_next.wait_recv)
        pl.when(here < count - 1)(to_prev.wait_recv)

    def sent(halo):
        to_next, to_prev, here, count = halo
        pl.when(here < count - 1)(to_next.wait_send)
        pl.when(here > 0)(to_prev.wait_send)

    def packed(field, fields):
        total = None
        for f in range(fields):
            s = part("sel", f)
            p = dot(jnp.concatenate([s, s], 1), two(flat(field(f)), 1), NT)
            total = p if total is None else total + p
        return total

    def pairs(count):
        return [tuple(range(f, min(f + 2, count))) for f in range(0, count, 2)]

    h1x = x_halo(xp, 4, 0)
    pl.semaphore_wait(barrier, expected + (ny - 1))
    start(h1x)
    tell()
    inner_loaded()
    lax.fori_loop(3, lx - 3, primitives, 0, unroll=2)
    for load in loads:
        load.wait()
    ysend[...] = packed(lambda f: xp[f, 3 : lx + 3], 4)
    h1y = y_halo(ysend, yhalo, 2)
    start(h1y)
    for f in range(4):
        gy[f] = block(dot(two(flat(xp[f, 3 : lx + 3]), 1), part("dy"), NN))

    def gradients(i):
        x = [difference(lambda k: xp[f, i + 3 + k]) for f in range(4)]
        z = [around(xp[f, i + 3]) for f in range(4)]
        return x[0], z[2], x[1], x[2] + z[0], z[1], x[3], z[3]

    def ahead(i, _=None):
        for n, g in enumerate(gradients(i)):
            pre[n, i] = g
        return 0

    lax.fori_loop(3, lx - 3, ahead, 0, unroll=2)
    for i in edges:
        z = [around(xp[f, i + 3]) for f in range(4)]
        for n, g in ((1, z[2]), (3, z[0]), (4, z[1]), (6, z[3])):
            pre[n, i] = g

    def at_edge(i):
        x = [difference(lambda k: xp[f, i + 3 + k]) for f in range(4)]
        return x[0], pre[1, i], x[1], x[2] + pre[3, i], pre[4, i], x[3], pre[6, i]

    arrive(h1y)
    hear()
    tell()
    outer = two(yhalo[...], 0)
    for fs in pairs(4):
        near = dot(outer, jnp.concatenate([part("ed", f) for f in fs], 1), TN)
        for n, f in enumerate(fs):
            gy[f] += block(near[:, n * ly : n * ly + ly])

    def fluxes(i, g=None):
        u = [xp[k, i + 3] for k in range(3)]
        m = [mt[k, i] for k in range(3)]
        p, ep = pt[i], ept[i]
        xx, zz, xv, xz, zv, xt, zt = g or [pre[n, i] for n in range(7)]
        yu, yy, yw, yt = [gy[f, i] for f in range(4)]
        dilation = (2.0 / 3.0 * viscosity * STEP) * (xx + yy + zz)
        twice, once = 2.0 * viscosity * STEP, viscosity * STEP
        stress = {
            (0, 0): twice * xx - dilation, (1, 1): twice * yy - dilation, (2, 2): twice * zz - dilation,
            (0, 1): once * (xv + yu), (0, 2): once * xz, (1, 2): once * (yw + zv),
        }
        for a, b in ((0, 1), (0, 2), (1, 2)):
            stress[b, a] = stress[a, b]
        heat = (xt, yt, zt)
        for j in range(3):
            entries = [m[j]]
            for k in range(3):
                e = m[k] * u[j] - stress[k, j]
                entries.append(e + p if k == j else e)
            power = u[0] * stress[0, j] + u[1] * stress[1, j] + u[2] * stress[2, j]
            entries.append(ep * u[j] - power - (conductivity * STEP) * heat[j])
            for c in range(5):
                if j == 0:
                    fxp[c, i + 3] = entries[c]
                elif j == 1:
                    fy[c, i] = entries[c]
                else:
                    dz[c, i] = around(entries[c])
        return 0

    def inner(i, _):
        return fluxes(i)

    lax.fori_loop(3, lx - 3, inner, 0, unroll=2)
    arrive(h1x)
    hear()
    tell()
    h2x = x_halo(fxp, 5, 4)
    for i in range(3):
        fluxes(i, at_edge(i))
    pl.when(ix > 0)(h2x[1].start)
    for i in range(lx - 3, lx):
        fluxes(i, at_edge(i))
    pl.when(ix < nx - 1)(h2x[0].start)
    ysend2[...] = packed(lambda f: fy[f], 5)
    h2y = y_halo(ysend2, yhalo2, 6)
    start(h2y)

    for f in range(5):
        inner = block(dot(two(flat(fy[f]), 1), part("dy"), NN))
        for i in range(lx):
            s = difference(lambda k: fxp[f, i + 3 + k] if 0 <= i + k < lx else None)
            inc[f, i] = s + dz[f, i] + inner[i]

    width = 32 + 2 * (nx - 1)

    def xtab(k):
        return xt[ix * width + k]

    arrive(h2y)
    outer = two(yhalo2[...], 0)
    for fs in pairs(5):
        near = dot(outer, jnp.concatenate([part("ed", f) for f in fs], 1), TN)
        for n, f in enumerate(fs):
            add = block(near[:, n * ly : n * ly + ly])
            y0 = yl = None
            for i in range(lx):
                s = inc[f, i] + add[i]
                inc[f, i] = s
                a, b = float(scale * xinv[0, i]) * s, float(scale * xinv[-1, i]) * s
                y0, yl = (a, b) if i == 0 else (y0 + a, yl + b)
            first = [fxp[f, 3 + m] for m in range(3)]
            last = [fxp[f, lx + 2 - m] for m in range(3)]
            for w, base in ((0, 0), (1, 8)):
                near_side, far_side = (first, last) if w == 0 else (last, first)
                near_at, far_at = (2, 5) if w == 0 else (5, 2)
                total = xtab(base) * y0 + xtab(base + 1) * yl
                for m in range(3):
                    total += xtab(base + near_at + m) * near_side[m]
                xs[2 + w, f] = total
                for m in range(3):
                    total += xtab(base + far_at + m) * far_side[m]
                xs[w, f] = total
    solved = dot(three(xs[...].reshape(20 * lz, ly), 1), part("inverse"), NN)
    xl[...] = solved.reshape(4, 5, lz, ly)
    hear()
    while (1 << len(stages)) < nx - 1:
        tell()
        hear()
    ywidth = 8 + 2 * (ny - 1)

    def ytab(k):
        return yt[iy * ywidth + k]

    def ends(data, f):
        w = part("wy", f)
        return dot(jnp.concatenate([w[0:16], w[0:16], w[16:32]], 1), data, NT)

    def y_exchange(values, source, target, send, receive):
        y0, yl = values[0:8], values[8:16]
        source[0] = ytab(0) * y0 + ytab(1) * yl
        source[1] = ytab(2) * y0 + ytab(3) * yl
        started = []
        for d in range(1, ny):
            which = jnp.where(iy + d >= ny, 1, 0).astype(jnp.int32)
            copy = pltpu.make_async_remote_copy(
                source.at[which], target.at[d - 1], send.at[d - 1], receive.at[d - 1],
                device_id={"gy": lax.rem(iy + d, ny)}, device_id_type=MESH)
            copy.start()
            started.append(copy)

        def finish():
            before = ytab(4) * y0 + ytab(5) * yl
            after = ytab(6) * y0 + ytab(7) * yl
            for d in range(1, ny):
                started[d - 1].wait_recv()
                r = target[d - 1]
                before += ytab(7 + d) * r
                after += ytab(7 + ny - 1 + d) * r
            return before, after

        return started, finish

    values = None
    spare = jnp.zeros((ly - 4 * lz, ly), jnp.float32)
    for f in range(5):
        p = ends(three(jnp.concatenate([xs[:, f].reshape(4 * lz, ly), spare], 0), 1), f)
        values = p if values is None else values + p
    lane = lax.broadcasted_iota(jnp.int32, (8, ly), 1)

    def shifted(v, by):
        return pltpu.roll(v, by % ly, 1) if by % ly else v

    def side_by_side(first, second):
        return jnp.where(lane < lz, first, jnp.where(lane < 2 * lz, second, 0.0))

    for w in range(4):
        cs[w] = side_by_side(shifted(values[0:8], -lz * w), shifted(values[8:16], lz - lz * w))
    ccopies = []
    for d in sorted(range(1, nx), key=lambda d: -min(d, nx - d)):
        above, below = (2 if d == 1 else 0), (3 if d == nx - 1 else 1)
        which = jnp.where(ix + d >= nx, below, above).astype(jnp.int32)
        copy = pltpu.make_async_remote_copy(
            cs.at[which], cr.at[d - 1], css.at[d - 1], crs.at[d - 1],
            device_id={"gx": lax.rem(ix + d, nx)}, device_id_type=MESH)
        copy.start()
        ccopies.append(copy)
    copies = []
    for d in sorted(range(1, nx), key=lambda d: -min(d, nx - d)):
        above, below = (2 if d == 1 else 0), (3 if d == nx - 1 else 1)
        which = jnp.where(ix + d >= nx, below, above).astype(jnp.int32)
        copy = pltpu.make_async_remote_copy(
            xl.at[which], xr.at[d - 1], xss.at[d - 1], xrs.at[d - 1],
            device_id={"gx": lax.rem(ix + d, nx)}, device_id_type=MESH)
        copy.start()
        copies.append(copy)

    for fs in pairs(5):
        v = {}
        for i in range(lx):
            for f in fs:
                s = float(scale * ipiv[i]) * inc[f, i]
                v[f] = s if i == 0 else s + float(coefficient * ipiv[i]) * v[f]
                inc[f, i] = v[f]
        for i in range(lx - 2, -1, -1):
            for f in fs:
                v[f] = inc[f, i] - float(coefficient * ipiv[i]) * v[f]
                inc[f, i] = v[f]
    local = None
    for f in range(5):
        data = three(flat(inc[f]), 1)
        p = ends(data, f)
        local = p if local is None else local + p
        fy[f] = block(dot(data, part("inverse"), NN))
    arrive(h2x)
    halo_rows = [*range(3), *range(lx - 3, lx)]
    own_x = []
    small = None
    for f in range(5):
        added = []
        for i in halo_rows:
            added.append(scale * difference(lambda k: None if 0 <= i + k < lx else fxp[f, i + 3 + k]))
        y0, yl = inc[f, 0], inc[f, lx - 1]
        for i, v in zip(halo_rows, added):
            y0 += float(xinv[0, i]) * v
            yl += float(xinv[-1, i]) * v
        terms = [y0, yl] + [fxp[f, 3 + m] for m in range(3)] + [fxp[f, lx + 2 - m] for m in range(3)]
        sides = []
        for base in (16, 24):
            total = xtab(base) * terms[0]
            for k in range(1, 8):
                total += xtab(base + k) * terms[k]
            sides.append(total)
        own_x.append(jnp.concatenate(sides + added, 0))
        p = ends(three(own_x[f], 1), f)
        small = p if small is None else small + p
    spread = jnp.concatenate([part("spread", c) for c in range(rows // ly)], 1)
    ycopies, finish = y_exchange(local + dot(three(small, 1), spread, NN), ws, wr, wss, wrs)
    solved = dot(three(jnp.concatenate(own_x, 0), 1), part("inverse"), NN)
    for f in range(5):
        pieces = [solved[lz * (8 * f + n) : lz * (8 * f + n + 1)] for n in range(8)]
        for i in range(lx):
            state = mass[i] if f == 0 else (energy[i] if f == 4 else mt[f - 1, i])
            total = state + fy[f, i]
            weights = [alpha[i], beta[i], *(xinv[i, r] for r in halo_rows)]
            for w, v in zip(weights, pieces):
                total += float(w) * v
            inc[f, i] = total
    for copy in ccopies:
        copy.wait_recv()
    sums = []
    for at in (31, 31 + nx - 1):
        total = xtab(at + 1) * cr[0]
        for d in range(2, nx):
            total += xtab(at + d) * cr[d - 1]
        sums.append(total)
    values = [side_by_side(sums[0], shifted(sums[1], lz)), side_by_side(shifted(sums[0], -lz), sums[1])]
    vcopies, finish_sides = y_exchange(jnp.concatenate(values, 0), vs, vr, vss, vrs)
    outside = three(jnp.concatenate(finish(), 0), 0)
    for fs in pairs(5):
        far = dot(outside, jnp.concatenate([part("ey", f) for f in fs], 1), TN)
        for n, f in enumerate(fs):
            total = block(far[:, n * ly : n * ly + ly])
            for i in range(lx):
                out[f, pl.ds(i, lz, stride=lx), :] = inc[f, i] + total[i]

    outside = three(jnp.concatenate(finish_sides(), 0), 0)
    for copy in copies:
        copy.wait_recv()
    for fs in pairs(5):
        far = dot(outside, jnp.concatenate([part("ey", f) for f in fs], 1), TN)
        for n, f in enumerate(fs):
            low = far[0:lz, n * ly : n * ly + ly]
            high = far[lz : 2 * lz, n * ly : n * ly + ly]
            for d in range(1, nx):
                r = xr[d - 1, f]
                low += xtab(31 + d) * r
                high += xtab(31 + nx - 1 + d) * r
            low_out[f], high_out[f] = low, high

    for halo in (h1x, h1y, h2x, h2y):
        sent(halo)
    for copy in copies + ccopies + vcopies + ycopies:
        copy.wait_send()


def body(nx, ny, mass, mom, energy):
    lz, lx, ly = mass.shape
    rows = lx * lz
    coefficient = float(max(lx, ly))
    xtab, xinv, xa, xb = coupled_tables(lx, nx, coefficient, -2.0 * coefficient * STEP)
    ytab, ya, yb = reduced_tables(ly, ny, coefficient)
    tab, places = lane_tables(lx, lz, ly, coefficient, xinv, xa, xb, ya, yb)
    vm = pl.BlockSpec(memory_space=pltpu.VMEM)
    hbm = pl.BlockSpec(memory_space=pltpu.HBM)
    f32 = jnp.float32
    block = (lx, lz, ly)
    dma = pltpu.SemaphoreType.DMA
    operands = (
        mass, mom, energy,
        jnp.asarray(tab), jnp.asarray(xtab.reshape(-1)), jnp.asarray(ytab.reshape(-1)),
    )
    result, low, high = pl.pallas_call(
        functools.partial(
            kernel, nx, ny, lx, lz, ly, coefficient, pivots(lx, coefficient), xinv, xa, xb, places),
        out_shape=(jax.ShapeDtypeStruct((5, rows, ly), f32), *[jax.ShapeDtypeStruct((5, lz, ly), f32)] * 2),
        in_specs=[hbm] * 6,
        out_specs=(vm, vm, vm),
        scratch_shapes=[
            pltpu.VMEM(block, f32),
            pltpu.VMEM(block, f32),
            pltpu.VMEM(tab.shape, jnp.bfloat16),
            pltpu.SMEM((xtab.size,), f32),
            pltpu.SMEM((ytab.size,), f32),
            pltpu.VMEM((4, lx + 6, lz, ly), f32),
            pltpu.VMEM(block, f32),
            pltpu.VMEM(block, f32),
            pltpu.VMEM((3, *block), f32),
            pltpu.VMEM((4, *block), f32),
            pltpu.VMEM((7, *block), f32),
            pltpu.VMEM((5, lx + 6, lz, ly), f32),
            pltpu.VMEM((5, *block), f32),
            pltpu.VMEM((5, *block), f32),
            pltpu.VMEM((5, *block), f32),
            pltpu.VMEM((32, rows), f32),
            pltpu.VMEM((32, rows), f32),
            pltpu.VMEM((32, rows), f32),
            pltpu.VMEM((32, rows), f32),
            pltpu.VMEM((4, 5, lz, ly), f32),
            pltpu.VMEM((4, 5, lz, ly), f32),
            pltpu.VMEM((nx - 1, 5, lz, ly), f32),
            pltpu.VMEM((2, 8, rows), f32),
            pltpu.VMEM((ny - 1, 8, rows), f32),
            pltpu.VMEM((2, 8, ly), f32),
            pltpu.VMEM((ny - 1, 8, ly), f32),
            pltpu.VMEM((4, 8, ly), f32),
            pltpu.VMEM((nx - 1, 8, ly), f32),
            dma((8,)),
            dma((8,)),
            dma((nx - 1,)),
            dma((nx - 1,)),
            dma((ny - 1,)),
            dma((ny - 1,)),
            dma((ny - 1,)),
            dma((ny - 1,)),
            dma((nx - 1,)),
            dma((nx - 1,)),
            dma((9,)),
            pltpu.SemaphoreType.REGULAR((max(1, (nx - 1).bit_length()),)),
        ],
        compiler_params=pltpu.CompilerParams(
            collective_id=0, has_side_effects=True, vmem_limit_bytes=40 * 2**20
        ),
    )(*[pltpu.with_memory_space_constraint(a, pltpu.HBM) for a in operands])
    low, high = low[:, :, None], high[:, :, None]
    along = [jnp.broadcast_to(jnp.asarray(w.astype(np.float32))[:, None], (lx, ly)) for w in (xa, xb)]
    return result.reshape(5, lz, lx, ly) + along[0] * low + along[1] * high


def solution(mesh):
    return jax.shard_map(
        functools.partial(body, mesh.shape["gx"], mesh.shape["gy"]),
        mesh=mesh,
        in_specs=(P(None, "gx", "gy"), P(None, None, "gx", "gy"), P(None, "gx", "gy")),
        out_specs=P(None, None, "gx", "gy"),
        check_vma=False,
    )
```
